32 devices in a mesh: dp: 4 (over z), row: 4 (over y, x), col: 2 (over core).
Axes of the slice: x: 2, y: 2, z: 4, core: 2. Of those that a mesh axis runs over, the one named last changes fastest.
Arguments:
- tokens_in: bfloat16 [16384, 768], P(('dp', 'col', 'row')), may hold values from -6 to 6
- gain_attn: float32 [768], replicated, may hold values from 0.5 to 1.5
- w_qkv: bfloat16 [768, 12, 192], P(None, 'row'), may hold values from -0.21875 to 0.21875
- w_out: bfloat16 [768, 768], P('row'), may hold values from -0.875 to 0.875
- rel_table: float32 [32, 12], P(None, 'row'), may hold values from -4 to 4
- gain_moe: float32 [768], replicated, may hold values from 0.5 to 1.5
- w_router: bfloat16 [768, 8], replicated, may hold values from -0.21875 to 0.21875
- w_in: bfloat16 [8, 768, 3072], P(('dp', 'col'), None, 'row'), may hold values from -0.21875 to 0.21875
- w_down: bfloat16 [8, 3072, 768], P(('dp', 'col'), 'row'), may hold values from -0.109375 to 0.109375
- grad_out: bfloat16 [16384, 768], P(('dp', 'col', 'row')), may hold values from -6 to 6
- routes: int32 [16384, 2], P(('dp', 'col')), may hold values from 0 to 7, all different within a row; in each aligned block of 2048 rows (0 to 2047, 2048 to 4095, ...) at most 1024 rows name the same one
- segments: int32 [16384], P(('dp', 'col')), may hold values from 0 to 31, never falling along the last dimension, each value on 1 to 1024 neighbouring positions
- rel_buckets: int32 [1024], replicated, may hold values from 0 to 31, as said below
Outputs:
- block_out: bfloat16 [16384, 768], P(('dp', 'col', 'row'))
- grad_input: bfloat16 [16384, 768], P(('dp', 'col', 'row'))
- grad_gain_attn: float32 [768], P('row')
- grad_w_qkv: float32 [768, 12, 192], P(None, 'row')
- grad_w_out: float32 [768, 768], P('row')
- grad_rel_table: float32 [32, 12], P(None, 'row')
- grad_gain_moe: float32 [768], replicated
- grad_w_router: float32 [768, 8], replicated
- grad_w_in: float32 [8, 768, 3072], P(('dp', 'col'), None, 'row')
- grad_w_down: float32 [8, 3072, 768], P(('dp', 'col'), 'row')
The draws below stay inside these ranges and needn't reach their ends.
Inputs may be any that keep to these rules, and one draw needn't show every extreme that they name: `routes`: each token names two different experts; among the 2048 tokens of one index of dp and col no expert is named more than 1024 times, and in some of them one expert exactly 1024 times. `segments`: never falls along the tokens; a document has at most 1024 tokens. `rel_buckets`: never falls as the distance grows; 0 at distance 0 and 31 at distance 1024 - 1.
All inputs are finite; a program needn't handle non-finite values.
Results may differ from the reference program's by a relative error of at most 0.018.
Values may be sent and summed in bfloat16 or wider, within the bound.
No kernel may reach another device: no remote copies, remote signals or barrier semaphores. Data moves between devices by JAX's collectives and lax.ppermute only.
A program may use at most 320 MiB of HBM per device.

```python
import math
import jax
import jax.numpy as jnp
import numpy as np
from jax import lax

D = 768
HEADS = 12
HD = 64
FF = 3072
NB = 32
SEQ = 1024
TOK_DEV = 512
EXPERTS = 8
TOK = 2048
TOKENS = 16384
CAP = 1024
N_DP = 4
N_ROW = 4
N_COL = 2


def draw_rel_buckets(key, part):
    distance = jnp.arange(SEQ, dtype=jnp.int32)
    exact_count = NB // 2
    spread_max = jnp.maximum(distance // exact_count, 1) + 1
    coin_flip = jax.random.randint(jax.random.fold_in(key, 7), (SEQ,), 0, spread_max)
    step_up = jnp.where(distance < exact_count, 1, (coin_flip == 0).astype(jnp.int32))
    step_up = jnp.where(distance == 0, 0, step_up)
    level = jnp.minimum(jnp.cumsum(step_up), NB - 1)
    return jnp.where(distance == SEQ - 1, NB - 1, level).astype(jnp.int32)


def block_scale(own_key, extent, pieces, smallest, high):
    level, own = 1.0, jax.random.fold_in(own_key, 6)
    for axis_at, shards_of in pieces:
        heights = jnp.exp(jax.random.uniform(jax.random.fold_in(own, axis_at), (shards_of,), jnp.float32, smallest / len(pieces), high / len(pieces)))
        level = level * jnp.repeat(heights, extent[axis_at] // shards_of).reshape([-1 if axis == axis_at else 1 for axis in range(len(extent))])
    return level


def split_up(number_of, total, bound, lean):
    portions = [(1 << 20) // math.isqrt(rank ** lean) + 1 for rank in range(2, number_of + 1)]
    spare, counts = total - bound - (number_of - 1), [1] * (number_of - 1)
    while spare > 0:
        movable = [i for i in range(number_of - 1) if counts[i] < bound]
        pool, budget = sum([portions[i] for i in movable]), spare
        for i in movable:
            addition = min(bound - counts[i], max(1, budget * portions[i] // pool), spare)
            counts[i] = counts[i] + addition
            spare = spare - addition
    return np.array([bound] + counts)


def ragged_sizes(stream_key, amount, total, bound, skew):
    if amount == 2:
        one = jax.random.randint(stream_key, (), max(1, total - bound), min(bound, total - 1) + 1)
        return jnp.stack([one, total - one])
    sizes = jnp.asarray(split_up(amount, total, bound, skew), jnp.int32)
    twos = (amount - 1) // 2
    donor, taker = sizes[1:1 + 2 * twos:2], sizes[2:2 + 2 * twos:2]
    room = jnp.minimum(donor - 1, bound - taker)
    shifted = jax.random.randint(jax.random.fold_in(stream_key, 1), (twos,), 0, 1 << 20) % (room + 1)
    sizes = sizes.at[1:1 + 2 * twos:2].set(donor - shifted).at[2:2 + 2 * twos:2].set(taker + shifted)
    return sizes[jax.random.permutation(jax.random.fold_in(stream_key, 2), amount)]


def assign_block(key, own, number, rows, count, top, reach, slope):
    order = jax.random.permutation(key, count)
    crowded, ordinary = shares(count, rows * top, reach, slope, True), shares(count, rows * top, reach, slope, False)
    places = jnp.arange(count)

    def named(tallies, offset_by):
        used = int((tallies > 0).sum())
        fixed = max(1, used // 4)
        moved = fixed + (places - fixed + offset_by * (used - fixed)) % max(1, count - fixed)
        return jnp.zeros((count,), jnp.int32).at[order[jnp.where(places < fixed, places, moved)]].set(jnp.asarray(tallies, jnp.int32))

    tallies = jnp.where(number % 4 == 0, named(crowded, number // 4), named(ordinary, number - number // 4 - 1))
    mixed = jax.random.permutation(jax.random.fold_in(own, 3), count)
    donor, taker = mixed[0:count // 2 * 2:2], mixed[1:count // 2 * 2:2]
    slack = jnp.minimum(tallies[donor] - 1, reach - tallies[taker]) // 2
    slack = jnp.where((donor == order[0]) | (taker == order[0]) | (tallies[taker] == 0), 0, jnp.maximum(slack, 0))
    moved = jax.random.randint(jax.random.fold_in(own, 4), (count // 2,), 0, 1 << 20) % (slack + 1)
    tallies = tallies.at[donor].add(-moved).at[taker].add(moved)
    items = jnp.searchsorted(jnp.cumsum(tallies), jnp.arange(rows * top), side="right").astype(jnp.int32)
    table = items.reshape(top, rows).T
    table = table[jax.random.permutation(jax.random.fold_in(own, 1), rows)]
    offset_by = jax.random.randint(jax.random.fold_in(own, 2), (rows, 1), 0, top)
    return jnp.take_along_axis(table, (jnp.arange(top)[None, :] + offset_by) % top, axis=1)


def shares(number_of, total, bound, lean, full):
    loads = [(1 << 20) // math.isqrt(standing ** lean) + 1 for standing in range(1, number_of + 1)]
    largest = bound if full else min(bound, max(-(-total // number_of), total * loads[0] // sum(loads)))
    least = 1 if total - largest >= number_of - 1 else 0
    holding, surplus = [largest] + [least] * (number_of - 1), total - largest - least * (number_of - 1)
    while surplus > 0:
        candidates = [i for i in range(1, number_of) if holding[i] < largest] or [i for i in range(1, number_of) if holding[i] < bound]
        mass, remaining = sum([loads[i] for i in candidates]), surplus
        for i in candidates:
            extra = min(bound - holding[i], max(1, remaining * loads[i] // mass), surplus)
            holding[i] = holding[i] + extra
            surplus = surplus - extra
    return np.array(holding)


def gaussian(own_key, dims, deviation, reach, pieces=(), kind=jnp.bfloat16):
    values = deviation * jax.random.normal(own_key, dims, jnp.float32)
    if pieces:
        values = values * block_scale(own_key, dims, pieces, -0.22, 0.18)
    return jnp.clip(values, -reach, reach).astype(kind)


def setup_inputs(seed: int = 0) -> dict:
    arg_keys = jax.random.split(jax.random.key(seed), 14)
    tokens_in = gaussian(arg_keys[0], (TOKENS, D), 1.0, 6.0, ((0, 32),))
    gain_attn = jnp.clip(1.0 + 0.1 * jax.random.normal(arg_keys[1], (D,), jnp.float32), 0.5, 1.5)
    w_qkv = gaussian(arg_keys[2], (D, HEADS, 3 * HD), D ** -0.5, 0.21875, ((1, 4),))
    w_out = gaussian(arg_keys[3], (HEADS * HD, D), (D // 16) ** -0.5, 0.875, ((0, 4),))
    rel_table = gaussian(arg_keys[4], (NB, HEADS), 1.0, 4.0, ((1, 4),), jnp.float32)
    gain_moe = jnp.clip(1.0 + 0.1 * jax.random.normal(arg_keys[5], (D,), jnp.float32), 0.5, 1.5)
    w_router = gaussian(arg_keys[6], (D, EXPERTS), D ** -0.5, 0.21875)
    w_in = gaussian(arg_keys[7], (EXPERTS, D, FF), D ** -0.5, 0.21875, ((0, 8), (2, 4)))
    w_down = gaussian(arg_keys[8], (EXPERTS, FF, D), FF ** -0.5, 0.109375, ((0, 8), (1, 4)))
    grad_out = gaussian(arg_keys[9], (TOKENS, D), 1.0, 6.0, ((0, 32),))
    routes_keys = jax.random.split(jax.random.fold_in(arg_keys[10], 1), TOKENS // TOK)
    routes_turns = jax.random.permutation(jax.random.fold_in(arg_keys[10], 3), TOKENS // TOK)
    routes = jax.vmap(lambda own, number: assign_block(jax.random.fold_in(arg_keys[10], 2), own, number, TOK, EXPERTS, 2, CAP, 2))(routes_keys, routes_turns).reshape((TOKENS, 2))
    segments = jnp.searchsorted(jnp.cumsum(ragged_sizes(arg_keys[11], TOKENS // (SEQ // 2), TOKENS, SEQ, 1)), jnp.arange(TOKENS), side="right").astype(jnp.int32)
    rel_buckets = draw_rel_buckets(jax.random.fold_in(arg_keys[13], 71), 0)
    return {"tokens_in": tokens_in, "gain_attn": gain_attn, "w_qkv": w_qkv, "w_out": w_out, "rel_table": rel_table, "gain_moe": gain_moe, "w_router": w_router, "w_in": w_in, "w_down": w_down, "grad_out": grad_out, "routes": routes, "segments": segments, "rel_buckets": rel_buckets}


EPSILON = 1e-06
HIGHEST = lax.Precision.HIGHEST

@jax.custom_vjp
def low(v):
    return lax.optimization_barrier(v.astype(jnp.bfloat16)).astype(jnp.float32)

@jax.custom_vjp
def low_back(v):
    return v

def low_keep(v):
    return (low(v), None)

def low_pass(kept, grad):
    return (grad,)

def back_keep(v):
    return (v, None)

def back_low(kept, grad):
    return (low(grad),)
low.defvjp(low_keep, low_pass)
low_back.defvjp(back_keep, back_low)

def rms_norm(values, gain_vec):
    factor = lax.rsqrt(lax.optimization_barrier(jnp.mean(values * values, axis=-1, keepdims=True)) + EPSILON)
    return values * factor * gain_vec

def attend(inputs, weight_qkv, weight_out, table, rel_buckets):
    normed, segment_rows = inputs
    packed = jnp.einsum('gsd,dhe->gshe', normed, weight_qkv, precision=HIGHEST)
    packed = low_back(low(packed))
    queries = packed[..., :HD]
    keys_all = packed[..., HD:2 * HD]
    values_all = packed[..., 2 * HD:]
    position = jnp.arange(SEQ, dtype=jnp.int32)
    distance = position[:, None] - position[None, :]
    bucket_ids = rel_buckets[jnp.clip(distance, 0, SEQ - 1)]
    bias_rows = jnp.transpose(table[bucket_ids], (2, 0, 1))
    scores = jnp.einsum('gqhe,gkhe->ghqk', queries, keys_all, precision=HIGHEST) * HD ** (-0.5) + bias_rows[None]
    scores = low_back(scores)
    allowed = (distance >= 0)[None, None] & (segment_rows[:, None, :, None] == segment_rows[:, None, None, :])
    scores = jnp.where(allowed, scores, -1e+30)
    prob_rows = low(jax.nn.softmax(scores, axis=-1))
    mixed_heads = jnp.einsum('ghqk,gkhe->gqhe', prob_rows, values_all, precision=HIGHEST)
    mixed_heads = low_back(low(mixed_heads)).reshape(normed.shape[0], SEQ, HEADS * HD)
    return low_back(jnp.einsum('gso,od->gsd', mixed_heads, weight_out, precision=HIGHEST))

def expert_rows(inputs):
    rows_in, weight_in, weight_down = inputs
    group_width = FF // N_ROW
    total = jnp.zeros(rows_in.shape, jnp.float32)
    for group in range(N_ROW):
        columns = slice(group * group_width, (group + 1) * group_width)
        sent_rows = low_back(rows_in)
        pre_act = low_back(jnp.dot(sent_rows, weight_in[:, columns], precision=HIGHEST))
        hidden_act = low(jax.nn.gelu(pre_act, approximate=True))
        total = total + low_back(low(jnp.dot(hidden_act, weight_down[columns], precision=HIGHEST)))
    return total

def reference(tokens_in, gain_attn, w_qkv, w_out, rel_table, gain_moe, w_router, w_in, w_down, grad_out, routes, segments, rel_buckets):
    group_tok = TOK_DEV * N_ROW
    sources = N_DP * N_COL
    per_source = routes.reshape(sources, group_tok * 2)
    onehot = (per_source[..., None] == jnp.arange(EXPERTS, dtype=jnp.int32)).astype(jnp.int32)
    slot_place = lax.optimization_barrier(jnp.sum(onehot * (jnp.cumsum(onehot, axis=1) - 1), axis=-1))
    anchor = jnp.arange(sources, dtype=jnp.int32)[:, None]
    dest_rows = (per_source * (sources * CAP) + anchor * CAP + slot_place).reshape(-1).astype(jnp.int32)
    source_rows = jnp.full((EXPERTS * sources * CAP,), 2 * TOKENS, jnp.int32).at[dest_rows].set(jnp.arange(2 * TOKENS, dtype=jnp.int32))
    n_sequences = TOKENS // SEQ
    batch_seqs = math.gcd(n_sequences, max(1, 4096 // SEQ))

    def forward(tokens_f, gain_one, weight_qkv, weight_out, table, gain_two, weight_router, weight_in, weight_down):
        normed_one = low(rms_norm(tokens_f, gain_one))

        def one_group(inputs):
            return attend(inputs, weight_qkv, weight_out, table, rel_buckets)
        attention = lax.map(jax.checkpoint(one_group), (normed_one.reshape(-1, batch_seqs, SEQ, D), segments.reshape(-1, batch_seqs, SEQ)))
        hidden_one = tokens_f + attention.reshape(TOKENS, D)
        normed_two = low(rms_norm(hidden_one, gain_two))
        logits = low_back(jnp.dot(normed_two, weight_router, precision=HIGHEST))
        chosen = jnp.take_along_axis(logits, routes, axis=1)
        gate_probs = jax.nn.softmax(chosen, axis=1)
        padded = jnp.concatenate([normed_two, jnp.zeros((1, D), jnp.float32)], axis=0)
        dispatched = padded[source_rows // 2].reshape(EXPERTS, sources * CAP, D)
        results = lax.map(jax.checkpoint(expert_rows), (dispatched, weight_in, weight_down))
        returned = results.reshape(-1, D)[dest_rows].reshape(TOKENS, 2, D)
        mixture = lax.optimization_barrier(jnp.sum(gate_probs[..., None] * returned, axis=1))
        return hidden_one + mixture
    block_out, pullback = jax.vjp(forward, tokens_in.astype(jnp.float32), gain_attn, w_qkv.astype(jnp.float32), w_out.astype(jnp.float32), rel_table, gain_moe, w_router.astype(jnp.float32), w_in.astype(jnp.float32), w_down.astype(jnp.float32))
    grads = pullback(grad_out.astype(jnp.float32))
    return (block_out.astype(jnp.bfloat16), grads[0].astype(jnp.bfloat16), grads[1], grads[2], grads[3], grads[4], grads[5], grads[6], grads[7], grads[8])
```

```python
from functools import partial

import jax
import jax.numpy as jnp
from jax import lax
from jax.experimental import pallas as pl
from jax.experimental.pallas import tpu as pltpu
from jax.sharding import PartitionSpec as P

SEQ = 1024
EPSILON = 1e-06
MASKED = -1e30
BLK = 256
PAD = 16
WIN = BLK + PAD
F32 = jnp.float32
BF16 = jnp.bfloat16
GELU_C = 0.7978845608028654
GELU_A = 0.044715


def dot_nn(a, b):
    return lax.dot_general(a, b, (((1,), (0,)), ((), ())), preferred_element_type=F32)


def dot_nt(a, b):
    return lax.dot_general(a, b, (((1,), (1,)), ((), ())), preferred_element_type=F32)


def dot_tn(a, b):
    return lax.dot_general(a, b, (((0,), (0,)), ((), ())), preferred_element_type=F32)


def attn_fwd_kernel(packed_ref, ext_ref, segr_ref, segc_ref, mixed_ref, probs_ref, tile_ref, *, head_size):
    n_blocks = SEQ // BLK
    for hh in range(2):
        base = hh * 3 * head_size
        scale = jnp.asarray(head_size ** (-0.5), BF16)
        q_all = packed_ref[:, base : base + head_size] * scale
        k_all = packed_ref[:, base + head_size : base + 2 * head_size]
        v_all = packed_ref[:, base + 2 * head_size : base + 3 * head_size]
        for t in range(n_blocks):
            rows = jnp.broadcast_to(ext_ref[hh, t : t + 1, :], (BLK, 2 * BLK))
            tile_ref[t] = pltpu.roll(rows, 0, 1, stride=1, stride_axis=0)[:, :BLK]
        for qb in range(n_blocks):
            width = (qb + 1) * BLK
            rows = slice(qb * BLK, (qb + 1) * BLK)
            scores = dot_nt(q_all[rows], k_all[:width])
            bias = jnp.concatenate([tile_ref[qb - kb] for kb in range(qb + 1)], axis=1)
            same = segc_ref[rows, :] == segr_ref[:, :width]
            scores = jnp.where(same, scores + bias, MASKED)
            peak = jnp.max(scores, axis=1, keepdims=True)
            exp_rows = jnp.exp(scores - peak)
            total = jnp.sum(exp_rows, axis=1, keepdims=True)
            probs = (exp_rows * (1.0 / total)).astype(BF16)
            probs_ref[hh, rows, :width] = probs
            mixed_ref[rows, hh * head_size : (hh + 1) * head_size] = dot_nn(
                probs, v_all[:width]
            ).astype(BF16)


def attn_bwd_kernel(
    packed_ref, probs_ref, grad_ref, out_ref, diag_ref, dk_ref, dv_ref, tile_ref, *, head_size
):
    n_blocks = SEQ // BLK
    for hh in range(2):
        base = hh * 3 * head_size
        scale = jnp.asarray(head_size ** (-0.5), BF16)
        q_all = packed_ref[:, base : base + head_size] * scale
        k_all = packed_ref[:, base + head_size : base + 2 * head_size]
        v_all = packed_ref[:, base + 2 * head_size : base + 3 * head_size]
        g_all = grad_ref[:, hh * head_size : (hh + 1) * head_size]
        for qb in reversed(range(n_blocks)):
            width = (qb + 1) * BLK
            rows = slice(qb * BLK, (qb + 1) * BLK)
            probs_b = probs_ref[hh, rows, :width]
            probs = probs_b.astype(F32)
            grad_probs = dot_nt(g_all[rows], v_all[:width])
            delta = jnp.sum(probs * grad_probs, axis=1, keepdims=True)
            grad_scores = probs * (grad_probs - delta)
            scores_b = grad_scores.astype(BF16)
            dq = dot_nn(scores_b, k_all[:width]) * (head_size ** (-0.5))
            out_ref[rows, base : base + head_size] = dq.astype(BF16)
            dk = dot_tn(scores_b, q_all[rows])
            dv = dot_tn(probs_b, g_all[rows])
            if qb == n_blocks - 1:
                dk_ref[...] = dk
                dv_ref[...] = dv
            else:
                dk_ref[:width, :] += dk
                dv_ref[:width, :] += dv
            for kb in range(qb + 1):
                part = grad_scores[:, kb * BLK : (kb + 1) * BLK]
                if qb == n_blocks - 1:
                    tile_ref[qb - kb] = part
                else:
                    tile_ref[qb - kb] += part
        out_ref[:, base + head_size : base + 2 * head_size] = dk_ref[...].astype(BF16)
        out_ref[:, base + 2 * head_size : base + 3 * head_size] = dv_ref[...].astype(BF16)
        for t in range(n_blocks):
            left = tile_ref[t]
            fold = jnp.concatenate([left, jnp.zeros_like(left)], axis=1)
            n = BLK
            while n > 1:
                n //= 2
                fold = fold[:n] + pltpu.roll(fold[n:], 2 * BLK - n, 1)
            diag_ref[hh, t : t + 1, :] = fold


def attention_forward(packed, ext, seg, heads, head_size):
    n_blocks = SEQ // BLK
    return pl.pallas_call(
        partial(attn_fwd_kernel, head_size=head_size),
        name="attn_fwd",
        grid=(heads // 2,),
        in_specs=[
            pl.BlockSpec((SEQ, 6 * head_size), lambda p: (0, p)),
            pl.BlockSpec((2, n_blocks, 2 * BLK), lambda p: (p, 0, 0)),
            pl.BlockSpec((1, SEQ), lambda p: (0, 0)),
            pl.BlockSpec((SEQ, 1), lambda p: (0, 0)),
        ],
        out_specs=[
            pl.BlockSpec((SEQ, 2 * head_size), lambda p: (0, p)),
            pl.BlockSpec((2, SEQ, SEQ), lambda p: (p, 0, 0)),
        ],
        out_shape=[
            jax.ShapeDtypeStruct((SEQ, heads * head_size), BF16),
            jax.ShapeDtypeStruct((heads, SEQ, SEQ), BF16),
        ],
        scratch_shapes=[pltpu.VMEM((n_blocks, BLK, BLK), F32)],
    )(packed, ext, seg.reshape(1, SEQ), seg.reshape(SEQ, 1))


def attention_backward(packed, probs, grad_mixed, heads, head_size):
    n_blocks = SEQ // BLK
    return pl.pallas_call(
        partial(attn_bwd_kernel, head_size=head_size),
        name="attn_bwd",
        grid=(heads // 2,),
        in_specs=[
            pl.BlockSpec((SEQ, 6 * head_size), lambda p: (0, p)),
            pl.BlockSpec((2, SEQ, SEQ), lambda p: (p, 0, 0)),
            pl.BlockSpec((SEQ, 2 * head_size), lambda p: (0, p)),
        ],
        out_specs=[
            pl.BlockSpec((SEQ, 6 * head_size), lambda p: (0, p)),
            pl.BlockSpec((2, n_blocks, 2 * BLK), lambda p: (p, 0, 0)),
        ],
        out_shape=[
            jax.ShapeDtypeStruct((SEQ, heads * 3 * head_size), BF16),
            jax.ShapeDtypeStruct((heads, n_blocks, 2 * BLK), F32),
        ],
        scratch_shapes=[
            pltpu.VMEM((SEQ, head_size), F32),
            pltpu.VMEM((SEQ, head_size), F32),
            pltpu.VMEM((n_blocks, BLK, BLK), F32),
        ],
    )(packed, probs, grad_mixed)


def experts_kernel(
    scal_ref,
    x_ref,
    g_ref,
    rank_ref,
    other_ref,
    router_ref,
    win_hbm,
    wdn_hbm,
    y_out,
    gr_out,
    gwi_hbm,
    gwd_hbm,
    grt_ref,
    xc,
    gc,
    oc,
    win,
    wdn,
    acc_i,
    acc_d,
    y_s,
    gr_s,
    sem,
    *,
    n_blk,
    n_ff,
):
    step = pl.program_id(0)
    width = xc.shape[1]
    count = scal_ref[n_blk]
    me = scal_ref[n_blk + 1]
    sub_iota = lax.broadcasted_iota(jnp.int32, (WIN, BLK), 0)
    row_iota = lax.broadcasted_iota(jnp.int32, (WIN, 1), 0)

    def window(start):
        return pl.multiple_of((start // PAD) * PAD, PAD)

    @pl.when(step == 0)
    def _():
        pltpu.make_async_copy(win_hbm, win, sem.at[0]).start()
        pltpu.make_async_copy(wdn_hbm, wdn, sem.at[1]).start()

    @pl.when(step < n_blk)
    def _():
        start = scal_ref[step]
        at = window(start)
        keep = row_iota < (start - at)
        hot = rank_ref[0] == (sub_iota + at)
        pick = jnp.where(hot, 1.0, 0.0).astype(BF16)
        xw = xc[pl.ds(at, WIN), :]
        xc[pl.ds(at, WIN), :] = jnp.where(keep, xw, dot_nn(pick, x_ref[...]).astype(BF16))
        gw = gc[pl.ds(at, WIN), :]
        gc[pl.ds(at, WIN), :] = jnp.where(keep, gw, dot_nn(pick, g_ref[...]).astype(BF16))
        ids = jnp.sum(jnp.where(hot, other_ref[0], 0.0), axis=1, keepdims=True)
        oc[pl.ds(at, WIN), :] = jnp.where(keep, oc[pl.ds(at, WIN), :], ids)

    @pl.when(step == n_blk)
    def _():
        at = window(count)
        keep = row_iota < (count - at)
        zero = jnp.zeros((), BF16)
        xc[pl.ds(at, WIN), :] = jnp.where(keep, xc[pl.ds(at, WIN), :], zero)
        gc[pl.ds(at, WIN), :] = jnp.where(keep, gc[pl.ds(at, WIN), :], zero)
        oc[pl.ds(at, WIN), :] = jnp.where(keep, oc[pl.ds(at, WIN), :], 0.0)
        for k in range(n_ff):
            acc_i[k] = jnp.zeros((width, width), F32)
            acc_d[k] = jnp.zeros((width, width), F32)
        grt_ref[...] = jnp.zeros(grt_ref.shape, F32)
        pltpu.make_async_copy(win_hbm, win, sem.at[0]).wait()
        pltpu.make_async_copy(wdn_hbm, wdn, sem.at[1]).wait()
        lane = lax.broadcasted_iota(jnp.int32, (BLK, 128), 1)

        def tile_body(i, carry):
            at_i = pl.multiple_of(i * BLK, BLK)
            x = xc[pl.ds(at_i, BLK), :]
            g = gc[pl.ds(at_i, BLK), :]
            mine_hot = lane == me
            other_hot = lane == oc[pl.ds(at_i, BLK), :].astype(jnp.int32)
            logits = dot_nn(x, router_ref[...])
            diff = jnp.sum(
                jnp.where(mine_hot, logits, 0.0) - jnp.where(other_hot, logits, 0.0),
                axis=1,
                keepdims=True,
            )
            small = jnp.exp(-jnp.abs(diff))
            inv = 1.0 / (1.0 + small)
            gate = jnp.where(diff >= 0, inv, small * inv)
            both = small * inv * inv
            gated = (g.astype(F32) * gate).astype(BF16)
            y_s[...] = jnp.zeros((BLK, width), F32)
            gr_s[...] = jnp.zeros((BLK, width), F32)

            def ff_body(k, c):
                w_i = win[k]
                w_d = wdn[k]
                pre = dot_nn(x, w_i)
                grad_h = dot_nt(gated, w_d)
                sq = pre * pre
                th = jnp.tanh(pre * (GELU_C + (GELU_C * GELU_A) * sq))
                half = 0.5 + 0.5 * th
                hid = (pre * half).astype(BF16)
                slope = half + (0.5 * pre) * (1.0 - th * th) * (
                    GELU_C + (3.0 * GELU_C * GELU_A) * sq
                )
                grad_pre = (grad_h * slope).astype(BF16)
                y_s[...] += dot_nn(hid, w_d)
                acc_d[k] += dot_tn(hid, gated)
                acc_i[k] += dot_tn(x, grad_pre)
                gr_s[...] += dot_nt(grad_pre, w_i)
                return c

            lax.fori_loop(0, n_ff, ff_body, 0)
            y = y_s[...]
            grad_gate = jnp.sum(g.astype(F32) * y, axis=1, keepdims=True) * both
            d_logit = jnp.where(mine_hot, grad_gate, 0.0) - jnp.where(other_hot, grad_gate, 0.0)
            d_high = d_logit.astype(BF16)
            d_low = (d_logit - d_high.astype(F32)).astype(BF16)
            router = router_ref[...]
            grt_ref[...] += dot_tn(d_high, x) + dot_tn(d_low, x)
            gr = gr_s[...] + (dot_nt(d_high, router) + dot_nt(d_low, router))
            xc[pl.ds(at_i, BLK), :] = (gate * y).astype(BF16)
            gc[pl.ds(at_i, BLK), :] = gr.astype(BF16)
            return carry

        lax.fori_loop(0, (count + BLK - 1) // BLK, tile_body, 0)
        for k in range(n_ff):
            win[k] = acc_i[k].astype(BF16)
            wdn[k] = acc_d[k].astype(BF16)
        pltpu.make_async_copy(win, gwi_hbm, sem.at[0]).start()
        pltpu.make_async_copy(wdn, gwd_hbm, sem.at[1]).start()

    @pl.when(step > n_blk)
    def _():
        at = window(scal_ref[step - n_blk - 1])
        pick = jnp.where(rank_ref[0] == (sub_iota + at), 1.0, 0.0).astype(BF16)
        y_out[...] = dot_tn(pick, xc[pl.ds(at, WIN), :]).astype(BF16)
        gr_out[...] = dot_tn(pick, gc[pl.ds(at, WIN), :]).astype(BF16)

    @pl.when(step == 2 * n_blk)
    def _():
        pltpu.make_async_copy(win, gwi_hbm, sem.at[0]).wait()
        pltpu.make_async_copy(wdn, gwd_hbm, sem.at[1]).wait()


def run_experts(x, g, rank, other, scal, router, win, wdn, max_rows):
    n_tok, width = x.shape
    n_blk = n_tok // BLK
    n_ff = win.shape[0]

    def first(s, sc):
        return (jnp.minimum(s, n_blk - 1), 0)

    def last(s, sc):
        return (jnp.maximum(s - n_blk - 1, 0), 0)

    def either(s, sc):
        return (jnp.where(s > n_blk, s - n_blk - 1, jnp.minimum(s, n_blk - 1)), 0, 0)

    rows = max_rows + WIN + PAD
    return pl.pallas_call(
        partial(experts_kernel, n_blk=n_blk, n_ff=n_ff),
        name="experts",
        grid_spec=pltpu.PrefetchScalarGridSpec(
            num_scalar_prefetch=1,
            grid=(2 * n_blk + 1,),
            in_specs=[
                pl.BlockSpec((BLK, width), first),
                pl.BlockSpec((BLK, width), first),
                pl.BlockSpec((1, 1, BLK), either),
                pl.BlockSpec((1, 1, BLK), either),
                pl.BlockSpec((width, 128), lambda s, sc: (0, 0)),
                pl.BlockSpec(memory_space=pl.ANY),
                pl.BlockSpec(memory_space=pl.ANY),
            ],
            out_specs=[
                pl.BlockSpec((BLK, width), last),
                pl.BlockSpec((BLK, width), last),
                pl.BlockSpec(memory_space=pl.ANY),
                pl.BlockSpec(memory_space=pl.ANY),
                pl.BlockSpec((128, width), lambda s, sc: (0, 0)),
            ],
            scratch_shapes=[
                pltpu.VMEM((rows, width), BF16),
                pltpu.VMEM((rows, width), BF16),
                pltpu.VMEM((rows, 1), F32),
                pltpu.VMEM((n_ff, width, width), BF16),
                pltpu.VMEM((n_ff, width, width), BF16),
                pltpu.VMEM((n_ff, width, width), F32),
                pltpu.VMEM((n_ff, width, width), F32),
                pltpu.VMEM((BLK, width), F32),
                pltpu.VMEM((BLK, width), F32),
                pltpu.SemaphoreType.DMA((2,)),
            ],
        ),
        out_shape=[
            jax.ShapeDtypeStruct((n_tok, width), BF16),
            jax.ShapeDtypeStruct((n_tok, width), BF16),
            jax.ShapeDtypeStruct((n_ff, width, width), BF16),
            jax.ShapeDtypeStruct((n_ff, width, width), BF16),
            jax.ShapeDtypeStruct((128, width), F32),
        ],
        compiler_params=pltpu.CompilerParams(vmem_limit_bytes=62 * 1024 * 1024),
    )(scal, x, g, rank, other, router, win, wdn)


def rms_back(values, inverse, gain_vec, grad_rows):
    scaled = gain_vec * grad_rows
    return inverse * scaled - values * inverse**3 * jnp.mean(values * scaled, axis=1, keepdims=True)


def local(
    tokens_in,
    gain_attn,
    w_qkv,
    w_out,
    rel_table,
    gain_moe,
    w_router,
    w_in,
    w_down,
    grad_out,
    routes,
    segments,
    rel_buckets,
):
    row_count = lax.axis_size("row")
    n_groups = lax.axis_size("dp") * lax.axis_size("col")
    tok_dev, width = tokens_in.shape
    tok_group = tok_dev * row_count
    n_experts = w_router.shape[1]
    capacity = 4 * tok_group // n_experts
    heads_here = w_qkv.shape[1]
    head_size = w_qkv.shape[2] // 3
    n_seqs = tok_group // SEQ
    assert row_count == 4 and n_seqs == 2 and n_experts == n_groups
    heads = 2 * heads_here
    row = lax.axis_index("row")
    member = row % 2
    first_half = member == 0

    def swap(value, mask):
        return lax.ppermute(value, "row", [(i, i ^ mask) for i in range(row_count)])

    def in_order(own, theirs):
        return jnp.where(
            first_half,
            jnp.concatenate([own, theirs], axis=0),
            jnp.concatenate([theirs, own], axis=0),
        )

    def half(value, which):
        return lax.dynamic_slice_in_dim(value, which * tok_dev, tok_dev, 0)

    tokens_f = tokens_in.astype(F32)
    inverse_one = lax.rsqrt(jnp.mean(tokens_f * tokens_f, axis=1, keepdims=True) + EPSILON)
    normed_one = (tokens_f * inverse_one * gain_attn).astype(BF16)
    qkv_mine = w_qkv.reshape(width, -1)
    qkv_other = swap(qkv_mine, 2)
    normed_other = swap(normed_one, 1)
    table_other = swap(rel_table, 2)
    grad_all = lax.all_gather(grad_out, ("dp", "col"), axis=0, tiled=True)
    routes_mine = lax.dynamic_slice_in_dim(routes, row * tok_dev, tok_dev, 0).T
    routes_all = lax.all_gather(routes_mine, ("dp", "col"), axis=0, tiled=False)

    normed_seq = in_order(normed_one, normed_other)
    qkv_both = jnp.concatenate([qkv_mine, qkv_other], axis=1)
    packed = jnp.dot(normed_seq, qkv_both, preferred_element_type=F32).astype(BF16)

    down, w_in_mine, w_down_mine, w_out_mine = lax.optimization_barrier(
        (normed_other, w_in[0], w_down[0], w_out)
    )
    out_parts = [w_out_mine] + [swap(w_out_mine, m) for m in (2, 1, 3)]
    w_out_all = jnp.concatenate(out_parts, axis=0)
    win_parts = [w_in_mine] + [swap(w_in_mine, m) for m in (2, 1, 3)]
    wdn_parts = [w_down_mine] + [swap(w_down_mine, m) for m in (2, 1, 3)]
    win_all = jnp.stack(win_parts)
    wdn_all = jnp.stack(wdn_parts)

    n_blocks = SEQ // BLK
    padded = jnp.concatenate(
        [jnp.full((BLK,), -1, jnp.int32), rel_buckets, rel_buckets[SEQ - 1 :]]
    )
    flipped = padded[::-1]
    pieces = []
    for t in range(n_blocks):
        begin = SEQ - (t + 1) * BLK
        piece = flipped[begin : begin + 2 * BLK]
        pieces += [piece[BLK:], piece[:BLK]]
    bucket_seq = jnp.concatenate(pieces)
    n_buckets = rel_table.shape[0]
    bucket_hot = (
        jnp.arange(n_buckets, dtype=jnp.int32)[:, None] == bucket_seq[None, :]
    ).astype(F32)
    table_both = jnp.concatenate([rel_table, table_other], axis=1)
    ext = jnp.dot(table_both.T, bucket_hot, precision=lax.Precision.HIGHEST)
    ext = jnp.where(bucket_seq[None, :] < 0, MASKED, ext).reshape(heads, n_blocks, 2 * BLK)
    segment_ids = lax.dynamic_slice_in_dim(segments, (row // 2) * SEQ, SEQ, 0)

    me = lax.axis_index("dp") * lax.axis_size("col") + lax.axis_index("col")
    hit = routes_all == me
    mine = (hit[:, 0] | hit[:, 1]).reshape(-1, BLK)
    other = jnp.sum(jnp.where(hit, 0, routes_all), axis=1).astype(F32).reshape(-1, 1, BLK)
    n_blk = mine.shape[0]
    before = (
        jnp.arange(BLK, dtype=jnp.int32)[:, None] < jnp.arange(BLK, dtype=jnp.int32)[None, :]
    ).astype(BF16)
    place = jnp.dot(mine.astype(BF16), before, preferred_element_type=F32).astype(jnp.int32)
    totals = jnp.sum(mine.astype(jnp.int32), axis=1)

    mixed, probs = attention_forward(packed, ext, segment_ids, heads, head_size)
    mixed_mine = half(mixed, member)
    mixed_theirs = swap(half(mixed, 1 - member), 1)
    mixed_all = jnp.concatenate([mixed_mine, mixed_theirs], axis=1)
    attention = jnp.dot(mixed_all, w_out_all, preferred_element_type=F32)
    hidden_one = tokens_f + attention
    inverse_two = lax.rsqrt(jnp.mean(hidden_one * hidden_one, axis=1, keepdims=True) + EPSILON)
    normed_two = (hidden_one * inverse_two * gain_moe).astype(BF16)
    normed_all = lax.all_gather(normed_two, ("dp", "col"), axis=0, tiled=True)

    router_pad = jnp.concatenate(
        [w_router, jnp.zeros((width, 128 - n_experts), BF16)], axis=1
    )
    max_group = min(tok_dev, capacity)
    chunk_groups = min(n_groups, 4096 // max_group)
    n_chunks = n_groups // chunk_groups
    blk_chunk = n_blk // n_chunks
    results = []
    for c in range(n_chunks):
        part = slice(c * blk_chunk, (c + 1) * blk_chunk)
        toks = slice(c * blk_chunk * BLK, (c + 1) * blk_chunk * BLK)
        tot = totals[part]
        index = jnp.arange(blk_chunk + 1, dtype=jnp.int32)
        starts = jnp.sum(jnp.where(index[None, :blk_chunk] < index[:, None], tot[None, :], 0), axis=1)
        rank = jnp.where(mine[part], place[part] + starts[:blk_chunk, None], -1)
        scal = jnp.concatenate([starts, me[None].astype(jnp.int32)])
        results.append(
            run_experts(
                normed_all[toks],
                grad_all[toks],
                rank.reshape(-1, 1, BLK),
                other[part],
                scal,
                router_pad,
                win_all,
                wdn_all,
                chunk_groups * max_group,
            )
        )
    if n_chunks == 1:
        y_all, gr_all, gwi, gwd, grt = results[0]
    else:
        y_all = jnp.concatenate([r[0] for r in results], axis=0)
        gr_all = jnp.concatenate([r[1] for r in results], axis=0)
        gwi = sum(r[2].astype(F32) for r in results).astype(BF16)
        gwd = sum(r[3].astype(F32) for r in results).astype(BF16)
        grt = sum(r[4] for r in results)
    grad_two = lax.psum_scatter(
        gr_all, ("dp", "col"), scatter_dimension=0, tiled=True
    ).astype(F32)
    mixture = lax.psum_scatter(y_all, ("dp", "col"), scatter_dimension=0, tiled=True).astype(F32)
    block_out = (hidden_one + mixture).astype(BF16)

    def gather_sum(parts):
        total = parts[0].astype(F32)
        for at, m in ((1, 2), (2, 1), (3, 3)):
            total = total + swap(parts[at], m).astype(F32)
        return total[None]

    grad_w_in = gather_sum(gwi)
    grad_w_down = gather_sum(gwd)

    cotangent = grad_out.astype(F32)
    grad_gain_moe = jnp.sum(grad_two * (hidden_one * inverse_two), axis=0)
    grad_hidden = cotangent + rms_back(hidden_one, inverse_two, gain_moe, grad_two)
    grad_attn = grad_hidden.astype(BF16)
    grad_w_out = dot_tn(mixed_all, grad_attn).astype(BF16).reshape(row_count, -1, width)
    grad_mixed = dot_nt(grad_attn, w_out_all).astype(BF16)
    half_cols = heads * head_size
    gm_theirs = swap(grad_mixed[:, half_cols:], 1)
    gm_seq = in_order(grad_mixed[:, :half_cols], gm_theirs)
    grad_packed, diag = attention_backward(packed, probs, gm_seq, heads, head_size)
    one_theirs = swap(dot_nt(half(grad_packed, 1 - member), qkv_both).astype(BF16), 1)
    grad_one = dot_nt(half(grad_packed, member), qkv_both) + one_theirs.astype(F32)
    grad_gain_attn = jnp.sum(grad_one * (tokens_f * inverse_one), axis=0)
    grad_input = (grad_hidden + rms_back(tokens_f, inverse_one, gain_attn, grad_one)).astype(BF16)

    qkv_cols = qkv_mine.shape[1]
    gq_theirs = swap(dot_tn(normed_seq, grad_packed[:, qkv_cols:]).astype(BF16), 2)
    gq = dot_tn(normed_seq, grad_packed[:, :qkv_cols]) + gq_theirs.astype(F32)
    grad_table = jnp.dot(
        bucket_hot, diag.reshape(heads, -1).T, precision=lax.Precision.HIGHEST
    )
    grad_table = grad_table[:, :heads_here] + swap(grad_table[:, heads_here:], 2)
    gwo = gather_sum(grad_w_out)[0]
    gq, gwo = lax.psum((gq.astype(BF16), gwo.astype(BF16)), ("dp", "col"))
    grad_table = lax.psum(grad_table, ("dp", "col"))
    gain_all, grad_gain_moe, grad_router = lax.psum(
        (grad_gain_attn, grad_gain_moe, grt[:n_experts]), ("dp", "row", "col")
    )
    gain_slice = lax.dynamic_slice_in_dim(
        gain_all, row * (width // row_count), width // row_count, 0
    )
    return (
        block_out,
        grad_input,
        gain_slice,
        gq.astype(F32).reshape(w_qkv.shape),
        gwo.astype(F32),
        grad_table,
        grad_gain_moe,
        grad_router.T,
        grad_w_in,
        grad_w_down,
    )


def solution(mesh):
    placed = (
        P(("dp", "col", "row"), None),
        P(),
        P(None, "row", None),
        P("row", None),
        P(None, "row"),
        P(),
        P(),
        P(("dp", "col"), None, "row"),
        P(("dp", "col"), "row", None),
        P(("dp", "col", "row"), None),
        P(("dp", "col"), None),
        P(("dp", "col")),
        P(),
    )
    return jax.shard_map(
        local,
        mesh=mesh,
        in_specs=placed,
        out_specs=(
            P(("dp", "col", "row"), None),
            P(("dp", "col", "row"), None),
            P("row"),
            P(None, "row", None),
            P("row", None),
            P(None, "row"),
            P(),
            P(),
            P(("dp", "col"), None, "row"),
            P(("dp", "col"), "row", None),
        ),
        check_vma=False,
    )
```

```python
from functools import partial

import jax
import jax.numpy as jnp
from jax import lax
from jax.experimental import pallas as pl
from jax.experimental.pallas import tpu as pltpu
from jax.sharding import PartitionSpec as P

SEQ = 1024
EPSILON = 1e-06
MASKED = -1e30
BLK = 256
PAD = 16
WIN = BLK + PAD
STEP = 128
PIECE = STEP + PAD
SUB = 4
F32 = jnp.float32
BF16 = jnp.bfloat16
GELU_C = 0.7978845608028654
GELU_A = 0.044715


def dot_nn(a, b):
    return lax.dot_general(a, b, (((1,), (0,)), ((), ())), preferred_element_type=F32)


def dot_nt(a, b):
    return lax.dot_general(a, b, (((1,), (1,)), ((), ())), preferred_element_type=F32)


def dot_tn(a, b):
    return lax.dot_general(a, b, (((0,), (0,)), ((), ())), preferred_element_type=F32)


def cost(micros):
    return pl.CostEstimate(flops=int(micros * 1e9), bytes_accessed=1 << 20, transcendentals=0)


def attn_fwd_kernel(packed_ref, ext_ref, segr_ref, segc_ref, mixed_ref, probs_ref, tile_ref, *, head_size):
    n_blocks = SEQ // BLK
    for hh in range(2):
        base = hh * 3 * head_size
        scale = jnp.asarray(head_size ** (-0.5), BF16)
        q_all = packed_ref[:, base : base + head_size] * scale
        k_all = packed_ref[:, base + head_size : base + 2 * head_size]
        v_all = packed_ref[:, base + 2 * head_size : base + 3 * head_size]
        for t in range(n_blocks):
            rows = jnp.broadcast_to(ext_ref[hh, t : t + 1, :], (BLK, 2 * BLK))
            tile_ref[t] = pltpu.roll(rows, 0, 1, stride=1, stride_axis=0)[:, :BLK]
        for qb in range(n_blocks):
            width = (qb + 1) * BLK
            rows = slice(qb * BLK, (qb + 1) * BLK)
            scores = dot_nt(q_all[rows], k_all[:width])
            bias = jnp.concatenate([tile_ref[qb - kb] for kb in range(qb + 1)], axis=1)
            same = segc_ref[rows, :] == segr_ref[:, :width]
            scores = jnp.where(same, scores + bias, MASKED)
            peak = jnp.max(scores, axis=1, keepdims=True)
            exp_rows = jnp.exp(scores - peak)
            total = jnp.sum(exp_rows, axis=1, keepdims=True)
            probs = (exp_rows * (1.0 / total)).astype(BF16)
            probs_ref[hh, rows, :width] = probs
            mixed_ref[rows, hh * head_size : (hh + 1) * head_size] = dot_nn(
                probs, v_all[:width]
            ).astype(BF16)


def attn_bwd_kernel(
    packed_ref, probs_ref, grad_ref, out_ref, diag_ref, dk_ref, dv_ref, tile_ref, *, head_size
):
    n_blocks = SEQ // BLK
    for hh in range(2):
        base = hh * 3 * head_size
        scale = jnp.asarray(head_size ** (-0.5), BF16)
        q_all = packed_ref[:, base : base + head_size] * scale
        k_all = packed_ref[:, base + head_size : base + 2 * head_size]
        v_all = packed_ref[:, base + 2 * head_size : base + 3 * head_size]
        g_all = grad_ref[:, hh * head_size : (hh + 1) * head_size]
        for qb in reversed(range(n_blocks)):
            width = (qb + 1) * BLK
            rows = slice(qb * BLK, (qb + 1) * BLK)
            probs_b = probs_ref[hh, rows, :width]
            probs = probs_b.astype(F32)
            grad_probs = dot_nt(g_all[rows], v_all[:width])
            delta = jnp.sum(probs * grad_probs, axis=1, keepdims=True)
            grad_scores = probs * (grad_probs - delta)
            scores_b = grad_scores.astype(BF16)
            dq = dot_nn(scores_b, k_all[:width]) * (head_size ** (-0.5))
            out_ref[rows, base : base + head_size] = dq.astype(BF16)
            dk = dot_tn(scores_b, q_all[rows])
            dv = dot_tn(probs_b, g_all[rows])
            if qb == n_blocks - 1:
                dk_ref[...] = dk
                dv_ref[...] = dv
            else:
                dk_ref[:width, :] += dk
                dv_ref[:width, :] += dv
            for kb in range(qb + 1):
                part = grad_scores[:, kb * BLK : (kb + 1) * BLK]
                if qb == n_blocks - 1:
                    tile_ref[qb - kb] = part
                else:
                    tile_ref[qb - kb] += part
        out_ref[:, base + head_size : base + 2 * head_size] = dk_ref[...].astype(BF16)
        out_ref[:, base + 2 * head_size : base + 3 * head_size] = dv_ref[...].astype(BF16)
        for t in range(n_blocks):
            left = tile_ref[t]
            fold = jnp.concatenate([left, jnp.zeros_like(left)], axis=1)
            n = BLK
            while n > 1:
                n //= 2
                fold = fold[:n] + pltpu.roll(fold[n:], 2 * BLK - n, 1)
            diag_ref[hh, t : t + 1, :] = fold


def attention_forward(packed, ext, seg, heads, head_size):
    n_blocks = SEQ // BLK
    return pl.pallas_call(
        partial(attn_fwd_kernel, head_size=head_size),
        name="attn_fwd",
        cost_estimate=cost(20),
        grid=(heads // 2,),
        in_specs=[
            pl.BlockSpec((SEQ, 6 * head_size), lambda p: (0, p)),
            pl.BlockSpec((2, n_blocks, 2 * BLK), lambda p: (p, 0, 0)),
            pl.BlockSpec((1, SEQ), lambda p: (0, 0)),
            pl.BlockSpec((SEQ, 1), lambda p: (0, 0)),
        ],
        out_specs=[
            pl.BlockSpec((SEQ, 2 * head_size), lambda p: (0, p)),
            pl.BlockSpec((2, SEQ, SEQ), lambda p: (p, 0, 0)),
        ],
        out_shape=[
            jax.ShapeDtypeStruct((SEQ, heads * head_size), BF16),
            jax.ShapeDtypeStruct((heads, SEQ, SEQ), BF16),
        ],
        scratch_shapes=[pltpu.VMEM((n_blocks, BLK, BLK), F32)],
    )(packed, ext, seg.reshape(1, SEQ), seg.reshape(SEQ, 1))


def attention_backward(packed, probs, grad_mixed, heads, head_size):
    n_blocks = SEQ // BLK
    return pl.pallas_call(
        partial(attn_bwd_kernel, head_size=head_size),
        name="attn_bwd",
        cost_estimate=cost(27),
        grid=(heads // 2,),
        in_specs=[
            pl.BlockSpec((SEQ, 6 * head_size), lambda p: (0, p)),
            pl.BlockSpec((2, SEQ, SEQ), lambda p: (p, 0, 0)),
            pl.BlockSpec((SEQ, 2 * head_size), lambda p: (0, p)),
        ],
        out_specs=[
            pl.BlockSpec((SEQ, 6 * head_size), lambda p: (0, p)),
            pl.BlockSpec((2, n_blocks, 2 * BLK), lambda p: (p, 0, 0)),
        ],
        out_shape=[
            jax.ShapeDtypeStruct((SEQ, heads * 3 * head_size), BF16),
            jax.ShapeDtypeStruct((heads, n_blocks, 2 * BLK), F32),
        ],
        scratch_shapes=[
            pltpu.VMEM((SEQ, head_size), F32),
            pltpu.VMEM((SEQ, head_size), F32),
            pltpu.VMEM((n_blocks, BLK, BLK), F32),
        ],
    )(packed, probs, grad_mixed)


def window(start):
    return pl.multiple_of((start // PAD) * PAD, PAD)


def hot_rows(rank_row, at, rows):
    return rank_row == (lax.broadcasted_iota(jnp.int32, (rows, BLK), 0) + at)


def n_pieces(scal_ref, block):
    return (scal_ref[block + 1] - scal_ref[block] + STEP - 1) // STEP


def compact_block(scal_ref, block, rank_row, source, dest):
    start = scal_ref[block]

    def piece(j, carry):
        first = start + j * STEP
        at = window(first)
        keep = lax.broadcasted_iota(jnp.int32, (PAD, 1), 0) < (first - at)
        pick = jnp.where(hot_rows(rank_row, at, PIECE), 1.0, 0.0).astype(BF16)
        rows = dot_nn(pick, source).astype(BF16)
        dest[pl.ds(at, PAD), :] = jnp.where(keep, dest[pl.ds(at, PAD), :], rows[:PAD])
        dest[pl.ds(at + PAD, STEP), :] = rows[PAD:]
        return carry

    piece(0, 0)
    lax.fori_loop(1, n_pieces(scal_ref, block), piece, 0)


def compact_end(count, dest):
    at = window(count)
    keep = lax.broadcasted_iota(jnp.int32, (WIN, 1), 0) < (count - at)
    old = dest[pl.ds(at, WIN), :]
    dest[pl.ds(at, WIN), :] = jnp.where(keep, old, jnp.zeros((), old.dtype))


def expand_block(scal_ref, block, rank_row, source, dest, place):
    start = scal_ref[block]

    def piece(j):
        first = start + j * STEP
        at = window(first)
        inside = (rank_row >= first) & (rank_row < first + STEP)
        pick = jnp.where(hot_rows(jnp.where(inside, rank_row, -1), at, PIECE), 1.0, 0.0)
        return dot_tn(pick.astype(BF16), source[pl.ds(at, PIECE), :]).astype(BF16)

    dest[place, :] = piece(0)

    def more(j, carry):
        dest[place, :] += piece(j)
        return carry

    lax.fori_loop(1, n_pieces(scal_ref, block), more, 0)


def compact_kernel(scal_ref, g_ref, rank_ref, other_ref, gc, oc, *, n_blk, sub):
    step = pl.program_id(0)
    for b in range(sub):
        block = step * sub + b
        rank_row = rank_ref[b]
        compact_block(scal_ref, block, rank_row, g_ref[b], gc)
        start = scal_ref[block]

        def ids_piece(j, carry):
            first = start + j * STEP
            at = window(first)
            keep = lax.broadcasted_iota(jnp.int32, (PIECE, 1), 0) < (first - at)
            hot = hot_rows(rank_row, at, PIECE)
            ids = jnp.sum(jnp.where(hot, other_ref[b], 0.0), axis=1, keepdims=True)
            oc[pl.ds(at, PIECE), :] = jnp.where(keep, oc[pl.ds(at, PIECE), :], ids)
            return carry

        ids_piece(0, 0)
        lax.fori_loop(1, n_pieces(scal_ref, block), ids_piece, 0)

    @pl.when(step == n_blk // sub - 1)
    def _():
        compact_end(scal_ref[n_blk], gc)
        compact_end(scal_ref[n_blk], oc)


def run_compact(g_all, rank, other, scal, rows, part, first):
    n_blk = rank.shape[0]
    sub = min(SUB, n_blk)
    width = g_all.shape[2]
    return pl.pallas_call(
        partial(compact_kernel, n_blk=n_blk, sub=sub),
        name="compact",
        cost_estimate=cost(7),
        grid_spec=pltpu.PrefetchScalarGridSpec(
            num_scalar_prefetch=1,
            grid=(n_blk // sub,),
            in_specs=[
                pl.BlockSpec((sub, BLK, width), lambda s, sc: (first // sub + s, part, 0)),
                pl.BlockSpec((sub, 1, BLK), lambda s, sc: (s, 0, 0)),
                pl.BlockSpec((sub, 1, BLK), lambda s, sc: (s, 0, 0)),
            ],
            out_specs=[
                pl.BlockSpec((rows, width), lambda s, sc: (0, 0)),
                pl.BlockSpec((rows, 1), lambda s, sc: (0, 0)),
            ],
        ),
        out_shape=[
            jax.ShapeDtypeStruct((rows, width), BF16),
            jax.ShapeDtypeStruct((rows, 1), F32),
        ],
    )(scal, g_all, rank, other)


def expand_kernel(scal_ref, rank_ref, *refs, sub, n_blk):
    out_ref = refs[-1]
    for c in range(len(refs) - 1):

        @pl.when(pl.program_id(0) == c)
        def _():
            for b in range(sub):
                block = c * (n_blk + 2) + pl.program_id(1) * sub + b
                expand_block(scal_ref, block, rank_ref[0, b], refs[c], out_ref.at[b], slice(None))


def run_expand(parts):
    n_parts = len(parts)
    n_blk = parts[0][1].shape[0]
    sub = min(SUB, n_blk)
    rows, width = parts[0][0].shape
    return pl.pallas_call(
        partial(expand_kernel, sub=sub, n_blk=n_blk),
        name="expand",
        cost_estimate=cost(6 * n_parts),
        grid_spec=pltpu.PrefetchScalarGridSpec(
            num_scalar_prefetch=1,
            grid=(n_parts, n_blk // sub),
            in_specs=[pl.BlockSpec((1, sub, 1, BLK), lambda c, s, sc: (c, s, 0, 0))]
            + [pl.BlockSpec((rows, width), lambda c, s, sc: (0, 0))] * n_parts,
            out_specs=pl.BlockSpec((sub, BLK, width), lambda c, s, sc: (s, c, 0)),
        ),
        out_shape=jax.ShapeDtypeStruct((n_blk, n_parts * BLK, width), BF16),
    )(
        jnp.concatenate([p[2] for p in parts]),
        jnp.stack([p[1] for p in parts]),
        *[p[0] for p in parts],
    )


def experts_kernel(
    scal_ref, x_ref, rank_ref, router_ref, oc, gc_hbm, *refs, n_blk, n_ff, sub, chained
):
    win_hbm, wdn_hbm = refs[:n_ff], refs[n_ff : 2 * n_ff]
    refs = refs[2 * n_ff :]
    if chained:
        gwi_old, gwd_old = refs[:n_ff], refs[n_ff : 2 * n_ff]
        refs = refs[2 * n_ff :]
    gr_out, yc_hbm, grt_ref = refs[:3]
    gwi_hbm, gwd_hbm = refs[3 : 3 + n_ff], refs[3 + n_ff : 3 + 2 * n_ff]
    xc, gc, win, wdn, acc_i, acc_d, y_s, gr_s, pre_s, gh_s, sem, old_i, old_d = refs[
        3 + 2 * n_ff :
    ]
    step = pl.program_id(0)
    n_steps = n_blk // sub
    width = xc.shape[1]
    count = scal_ref[n_blk]
    me = scal_ref[n_blk + 1]

    def loads():
        copies = [pltpu.make_async_copy(gc_hbm, gc, sem.at[2 * n_ff])]
        for k in range(n_ff):
            copies.append(pltpu.make_async_copy(win_hbm[k], win.at[k], sem.at[k]))
            copies.append(pltpu.make_async_copy(wdn_hbm[k], wdn.at[k], sem.at[n_ff + k]))
        return copies

    def olds():
        copies = []
        for k in range(n_ff if chained else 0):
            at = 2 * n_ff + 1 + 2 * k
            copies.append(pltpu.make_async_copy(gwi_old[k], old_i.at[k], sem.at[at]))
            copies.append(pltpu.make_async_copy(gwd_old[k], old_d.at[k], sem.at[at + 1]))
        return copies

    def saves():
        copies = [pltpu.make_async_copy(xc, yc_hbm, sem.at[2 * n_ff])]
        for k in range(n_ff):
            copies.append(pltpu.make_async_copy(win.at[k], gwi_hbm[k], sem.at[k]))
            copies.append(pltpu.make_async_copy(wdn.at[k], gwd_hbm[k], sem.at[n_ff + k]))
        return copies

    @pl.when(step == 0)
    def _():
        for copy in loads() + olds():
            copy.start()

    @pl.when(step < n_steps)
    def _():
        for b in range(sub):
            rows = slice(b * BLK, (b + 1) * BLK)
            compact_block(scal_ref, step * sub + b, rank_ref[b], x_ref[rows, :], xc)

    @pl.when(step == n_steps)
    def _():
        compact_end(count, xc)
        grt_ref[...] = jnp.zeros(grt_ref.shape, F32)
        for copy in loads():
            copy.wait()
        lane = lax.broadcasted_iota(jnp.int32, (BLK, 128), 1)

        def tile_body(i, carry):
            at_i = pl.multiple_of(i * BLK, BLK)
            x = xc[pl.ds(at_i, BLK), :]
            g = gc[pl.ds(at_i, BLK), :]
            mine_hot = lane == me
            other_hot = lane == oc[pl.ds(at_i, BLK), :].astype(jnp.int32)
            logits = dot_nn(x, router_ref[...])
            diff = jnp.sum(
                jnp.where(mine_hot, logits, 0.0) - jnp.where(other_hot, logits, 0.0),
                axis=1,
                keepdims=True,
            )
            small = jnp.exp(-jnp.abs(diff))
            inv = 1.0 / (1.0 + small)
            gate = jnp.where(diff >= 0, inv, small * inv)
            both = small * inv * inv
            gated = (g.astype(F32) * gate).astype(BF16)

            def first_products(k):
                pre_s[k % 2] = dot_nn(x, win[k])
                gh_s[k % 2] = dot_nt(gated, wdn[k])

            first_products(0)
            for k in range(n_ff):
                if k + 1 < n_ff:
                    first_products(k + 1)
                pre = pre_s[k % 2]
                sq = pre * pre
                th = jnp.tanh(pre * (GELU_C + (GELU_C * GELU_A) * sq))
                half = 0.5 + 0.5 * th
                hid = (pre * half).astype(BF16)
                slope = half + (0.5 * pre) * (1.0 - th * th) * (
                    GELU_C + (3.0 * GELU_C * GELU_A) * sq
                )
                grad_pre = (gh_s[k % 2] * slope).astype(BF16)
                y_new = dot_nn(hid, wdn[k])
                gr_new = dot_nt(grad_pre, win[k])
                y_s[...] = y_s[...] + y_new if k else y_new
                gr_s[...] = gr_s[...] + gr_new if k else gr_new
                acc_d[k] = dot_tn(hid, gated) + jnp.where(i > 0, acc_d[k], 0.0)
                acc_i[k] = dot_tn(x, grad_pre) + jnp.where(i > 0, acc_i[k], 0.0)

            y = y_s[...]
            grad_gate = jnp.sum(g.astype(F32) * y, axis=1, keepdims=True) * both
            d_logit = jnp.where(mine_hot, grad_gate, 0.0) - jnp.where(other_hot, grad_gate, 0.0)
            d_high = d_logit.astype(BF16)
            d_low = (d_logit - d_high.astype(F32)).astype(BF16)
            router = router_ref[...]
            grt_ref[...] += dot_tn(d_high, x) + dot_tn(d_low, x)
            gr = gr_s[...] + (dot_nt(d_high, router) + dot_nt(d_low, router))
            xc[pl.ds(at_i, BLK), :] = (gate * y).astype(BF16)
            gc[pl.ds(at_i, BLK), :] = gr.astype(BF16)
            return carry

        lax.fori_loop(0, jnp.maximum((count + BLK - 1) // BLK, 1), tile_body, 0)
        for copy in olds():
            copy.wait()
        for k in range(n_ff):
            if chained:
                win[k] = (acc_i[k] + old_i[k].astype(F32)).astype(BF16)
                wdn[k] = (acc_d[k] + old_d[k].astype(F32)).astype(BF16)
            else:
                win[k] = acc_i[k].astype(BF16)
                wdn[k] = acc_d[k].astype(BF16)
        for copy in saves():
            copy.start()

    @pl.when(step > n_steps)
    def _():
        for b in range(sub):
            place = slice(b * BLK, (b + 1) * BLK)
            block = (step - n_steps - 1) * sub + b
            expand_block(scal_ref, block, rank_ref[b], gc, gr_out, place)

    @pl.when(step == 2 * n_steps)
    def _():
        for copy in saves():
            copy.wait()


def run_experts(x, gc, oc, rank, scal, router, win, wdn, first, old):
    n_blk = rank.shape[0]
    sub = min(SUB, n_blk)
    n_steps = n_blk // sub
    width = x.shape[1]
    n_ff = len(win)
    rows = gc.shape[0]
    n_old = n_ff if old else 1

    def source(s, sc):
        return (first // sub + jnp.minimum(s, n_steps - 1), 0)

    def dest(s, sc):
        return (jnp.maximum(s - n_steps - 1, 0), 0)

    def either(s, sc):
        return (jnp.where(s > n_steps, s - n_steps - 1, jnp.minimum(s, n_steps - 1)), 0, 0)

    hbm = pl.BlockSpec(memory_space=pl.ANY)
    out = pl.pallas_call(
        partial(experts_kernel, n_blk=n_blk, n_ff=n_ff, sub=sub, chained=bool(old)),
        name="experts",
        cost_estimate=cost(40),
        grid_spec=pltpu.PrefetchScalarGridSpec(
            num_scalar_prefetch=1,
            grid=(2 * n_steps + 1,),
            in_specs=[
                pl.BlockSpec((sub * BLK, width), source),
                pl.BlockSpec((sub, 1, BLK), either),
                pl.BlockSpec((width, 128), lambda s, sc: (0, 0)),
                pl.BlockSpec((rows, 1), lambda s, sc: (0, 0)),
                hbm,
            ]
            + [hbm] * (2 * n_ff + len(old)),
            out_specs=[
                pl.BlockSpec((sub * BLK, width), dest),
                hbm,
                pl.BlockSpec((128, width), lambda s, sc: (0, 0)),
            ]
            + [hbm] * (2 * n_ff),
            scratch_shapes=[
                pltpu.VMEM((rows, width), BF16),
                pltpu.VMEM((rows, width), BF16),
                pltpu.VMEM((n_ff, width, width), BF16),
                pltpu.VMEM((n_ff, width, width), BF16),
                pltpu.VMEM((n_ff, width, width), F32),
                pltpu.VMEM((n_ff, width, width), F32),
                pltpu.VMEM((BLK, width), F32),
                pltpu.VMEM((BLK, width), F32),
                pltpu.VMEM((2, BLK, width), F32),
                pltpu.VMEM((2, BLK, width), F32),
                pltpu.SemaphoreType.DMA((4 * n_ff + 1,)),
                pltpu.VMEM((n_old, width, width) if old else (1, 8, 128), BF16),
                pltpu.VMEM((n_old, width, width) if old else (1, 8, 128), BF16),
            ],
        ),
        out_shape=[
            jax.ShapeDtypeStruct((n_blk * BLK, width), BF16),
            jax.ShapeDtypeStruct((rows, width), BF16),
            jax.ShapeDtypeStruct((128, width), F32),
        ]
        + [jax.ShapeDtypeStruct((width, width), BF16)] * (2 * n_ff),
        compiler_params=pltpu.CompilerParams(vmem_limit_bytes=62 * 1024 * 1024),
    )(scal, x, rank, router, oc, gc, *win, *wdn, *old)
    return out[0], out[1], out[2], list(out[3:])


def rms_back(values, inverse, gain_vec, grad_rows):
    scaled = gain_vec * grad_rows
    return inverse * scaled - values * inverse**3 * jnp.mean(values * scaled, axis=1, keepdims=True)


def after(value, *others):
    return lax.optimization_barrier((value,) + others)[0]


def pad_rows(value, rows):
    return jnp.concatenate(
        [value, jnp.zeros((rows - value.shape[0], value.shape[1]), value.dtype)], axis=0
    )


def round_up(n, m):
    return -(-n // m) * m


def reduce_z(value):
    n = lax.axis_size("dp")
    if n > 4:
        total = lax.psum(value, "dp")
        return total, total
    at = lax.axis_index("dp")
    parts = value.reshape(n, -1, value.shape[1])

    def pick(k):
        return lax.dynamic_index_in_dim(parts, (at + k) % n, 0, keepdims=False)

    def shift(v, k):
        return lax.ppermute(v, "dp", [(i, (i + k) % n) for i in range(n)])

    total = pick(0).astype(F32)
    for arrived in [shift(pick(k), k) for k in range(1, n)]:
        total = total + arrived.astype(F32)
    total = total.astype(BF16)
    pieces = [total] + [shift(total, k) for k in range(1, n)]
    rows = []
    for j in range(n):
        row = pieces[0]
        for k in range(1, n):
            row = jnp.where((at - k) % n == j, pieces[k], row)
        rows.append(row)
    return jnp.concatenate(rows, axis=0), total


def local(
    tokens_in,
    gain_attn,
    w_qkv,
    w_out,
    rel_table,
    gain_moe,
    w_router,
    w_in,
    w_down,
    grad_out,
    routes,
    segments,
    rel_buckets,
):
    row_count = lax.axis_size("row")
    n_groups = lax.axis_size("dp") * lax.axis_size("col")
    tok_dev, width = tokens_in.shape
    tok_group = tok_dev * row_count
    n_experts = w_router.shape[1]
    capacity = 4 * tok_group // n_experts
    heads_here = w_qkv.shape[1]
    head_size = w_qkv.shape[2] // 3
    n_seqs = tok_group // SEQ
    assert row_count == 4 and n_seqs == 2 and n_experts == n_groups
    heads = 2 * heads_here
    row = lax.axis_index("row")
    col = lax.axis_index("col")
    member = row % 2
    first_half = member == 0

    def swap(value, mask):
        return lax.ppermute(value, "row", [(i, i ^ mask) for i in range(row_count)])

    def swap_col(value):
        return lax.ppermute(value, "col", [(0, 1), (1, 0)])

    def in_order(own, theirs):
        return jnp.where(
            first_half,
            jnp.concatenate([own, theirs], axis=0),
            jnp.concatenate([theirs, own], axis=0),
        )

    def half(value, which):
        return lax.dynamic_slice_in_dim(value, which * tok_dev, tok_dev, 0)

    tokens_f = tokens_in.astype(F32)
    inverse_one = lax.rsqrt(jnp.mean(tokens_f * tokens_f, axis=1, keepdims=True) + EPSILON)
    normed_one = (tokens_f * inverse_one * gain_attn).astype(BF16)
    qkv_mine = w_qkv.reshape(width, -1)
    qkv_cols = qkv_mine.shape[1]
    qkv_other = swap(qkv_mine, 2)
    normed_other = swap(normed_one, 1)
    table_other = swap(rel_table, 2)

    routes_mine = lax.dynamic_slice_in_dim(routes, row * tok_dev, tok_dev, 0).T
    route_len = round_up(2 * tok_dev, PAD * width)
    routes_row = jnp.concatenate(
        [routes_mine.reshape(-1), jnp.zeros((route_len - 2 * tok_dev,), jnp.int32)]
    )
    grad_ext = jnp.concatenate([grad_out, routes_row.astype(BF16).reshape(-1, width)], axis=0)
    grad_all = lax.all_gather(grad_ext, ("dp", "col"), axis=0, tiled=False)

    normed_seq = in_order(normed_one, normed_other)
    qkv_both = jnp.concatenate([qkv_mine, qkv_other], axis=1)
    packed = jnp.dot(normed_seq, qkv_both, preferred_element_type=F32).astype(BF16)

    w_in_mine, w_down_mine, w_out_mine = (
        after(w, normed_other, qkv_other) for w in (w_in[0], w_down[0], w_out)
    )
    wo_x = swap(w_out_mine, 1)
    wo_y = swap(w_out_mine, 2)
    wo_d = swap(wo_x, 2)
    w_out_all = jnp.concatenate([w_out_mine, wo_y, wo_x, wo_d], axis=0)
    wi_x = swap(w_in_mine, 1)
    wd_y = swap(w_down_mine, 2)
    wi_y = swap(w_in_mine, 2)
    wd_x = swap(w_down_mine, 1)
    wi_d = swap(wi_x, 2)
    wd_d = swap(wd_y, 1)
    win_parts = [w_in_mine, wi_y, wi_x, wi_d]
    wdn_parts = [w_down_mine, wd_y, wd_x, wd_d]

    n_blocks = SEQ // BLK
    padded = jnp.concatenate(
        [jnp.full((BLK,), -1, jnp.int32), rel_buckets, rel_buckets[SEQ - 1 :]]
    )
    flipped = padded[::-1]
    pieces = []
    for t in range(n_blocks):
        begin = SEQ - (t + 1) * BLK
        piece = flipped[begin : begin + 2 * BLK]
        pieces += [piece[BLK:], piece[:BLK]]
    bucket_seq = jnp.concatenate(pieces)
    n_buckets = rel_table.shape[0]
    bucket_hot = (
        jnp.arange(n_buckets, dtype=jnp.int32)[:, None] == bucket_seq[None, :]
    ).astype(F32)
    table_both = jnp.concatenate([rel_table, table_other], axis=1)
    ext = jnp.dot(table_both.T, bucket_hot, precision=lax.Precision.HIGHEST)
    ext = jnp.where(bucket_seq[None, :] < 0, MASKED, ext).reshape(heads, n_blocks, 2 * BLK)
    segment_ids = lax.dynamic_slice_in_dim(segments, (row // 2) * SEQ, SEQ, 0)

    mixed, probs = attention_forward(packed, ext, segment_ids, heads, head_size)
    mixed = after(mixed, wi_x, wd_y)
    mixed_mine = half(mixed, member)
    mixed_theirs = swap(half(mixed, 1 - member), 1)
    mixed_all = jnp.concatenate([mixed_mine, mixed_theirs], axis=1)
    attention = jnp.dot(mixed_all, w_out_all, preferred_element_type=F32)
    hidden_one = tokens_f + attention
    inverse_two = lax.rsqrt(jnp.mean(hidden_one * hidden_one, axis=1, keepdims=True) + EPSILON)
    normed_two = (hidden_one * inverse_two * gain_moe).astype(BF16)
    n_parts = tok_dev // BLK
    normed_all = []
    for c in range(n_parts):
        piece = normed_two[c * BLK : (c + 1) * BLK]
        normed_all.append(piece)

    me = lax.axis_index("dp") * lax.axis_size("col") + col
    routes_all = (
        grad_all[:, tok_dev:]
        .reshape(n_groups, -1)[:, : 2 * tok_dev]
        .astype(jnp.int32)
        .reshape(n_groups, 2, n_parts, BLK)
    )
    hit = routes_all == me
    mine = hit[:, 0] | hit[:, 1]
    other = jnp.sum(jnp.where(hit, 0, routes_all), axis=1).astype(F32)
    before = (
        jnp.arange(BLK, dtype=jnp.int32)[:, None] < jnp.arange(BLK, dtype=jnp.int32)[None, :]
    ).astype(BF16)
    place = jnp.dot(
        mine.reshape(-1, BLK).astype(BF16), before, preferred_element_type=F32
    ).astype(jnp.int32).reshape(mine.shape)
    totals = jnp.sum(mine.astype(jnp.int32), axis=2)

    router_pad = jnp.concatenate(
        [w_router, jnp.zeros((width, 128 - n_experts), BF16)], axis=1
    )
    max_group = min(BLK, capacity)
    chunk = min(n_groups, 2048 // max_group)
    rows = chunk * max_group + WIN + PAD
    index = jnp.arange(chunk + 1, dtype=jnp.int32)
    plans = []
    for c in range(n_parts):
        for g0 in range(0, n_groups, chunk):
            tot = totals[g0 : g0 + chunk, c]
            starts = jnp.sum(
                jnp.where(index[None, :chunk] < index[:, None], tot[None, :], 0), axis=1
            )
            rank = jnp.where(
                mine[g0 : g0 + chunk, c],
                place[g0 : g0 + chunk, c] + starts[:chunk, None],
                -1,
            ).reshape(-1, 1, BLK)
            scal = jnp.concatenate([starts, me[None].astype(jnp.int32)])
            others = other[g0 : g0 + chunk, c].reshape(-1, 1, BLK)
            gc, oc = run_compact(grad_all, rank, others, scal, rows, c, g0)
            plans.append((c, g0, rank, scal, gc, oc))
    for c in range(n_parts):
        if c:
            piece = after(normed_all[c], *[p[4] for p in plans if p[0] == c - 1])
        else:
            piece = after(normed_all[c], grad_all, wi_x, wi_y, wd_x, wd_y)
        normed_all[c] = lax.all_gather(piece, ("dp", "col"), axis=0, tiled=True)
    grad_parts = [[] for unused in range(n_parts)]
    y_parts = [[] for unused in range(n_parts)]
    weight_grads = []
    grt = 0.0
    last_gc = plans[-1][4]
    for c, g0, rank, scal, gc, oc in plans:
        gr, yc, grt_part, weight_grads = run_experts(
            normed_all[c], gc, after(oc, last_gc), rank, scal, router_pad,
            win_parts, wdn_parts, g0, weight_grads,
        )
        grad_parts[c].append(gr)
        y_parts[c].append((yc, rank, scal))
        grt = grt + grt_part

    def scatter(value):
        return lax.psum_scatter(value, ("dp", "col"), scatter_dimension=0, tiled=True)

    def join(values):
        return values[0] if len(values) == 1 else jnp.concatenate(values, axis=0)

    grad_two = jnp.concatenate([scatter(join(g)) for g in grad_parts], axis=0)
    last = grad_parts[-1][-1]
    y_all = join(
        [
            run_expand([(after(y[at][0], last),) + y[at][1:] for y in y_parts])
            for at in range(n_groups // chunk)
        ]
    ).reshape(-1, width)

    gwi, gwd = weight_grads[:row_count], weight_grads[row_count:]
    gi_x, gi_d = swap(gwi[2], 1), swap(gwi[3], 1)
    gd_y, gd_d = swap(gwd[1], 2), swap(gwd[3], 2)
    gi_two = (gwi[1].astype(F32) + gi_d.astype(F32)).astype(BF16)
    gd_two = (gwd[2].astype(F32) + gd_d.astype(F32)).astype(BF16)
    grad_two = after(grad_two, gi_x, gi_two, gd_y, gd_two, y_all).astype(F32)

    cotangent = grad_out.astype(F32)
    grad_gain_moe = jnp.sum(grad_two * (hidden_one * inverse_two), axis=0)
    grad_hidden = cotangent + rms_back(hidden_one, inverse_two, gain_moe, grad_two)
    grad_attn = grad_hidden.astype(BF16)
    grad_mixed = dot_nt(grad_attn, w_out_all).astype(BF16)
    half_cols = heads * head_size
    gm_theirs = swap(grad_mixed[:, half_cols:], 1)
    gm_seq = in_order(grad_mixed[:, :half_cols], gm_theirs)
    mixture = scatter(after(y_all, gm_seq))
    gi_y = swap(after(gi_two, gm_seq), 2)
    gd_x = swap(after(gd_two, gm_seq), 1)
    grad_packed, diag = attention_backward(packed, probs, gm_seq, heads, head_size)

    out_rows = w_out.shape[0]
    small = jnp.concatenate([grt[:n_experts], grad_gain_moe[None]], axis=0)
    early_rows = round_up(out_rows + small.shape[0], 32)
    gwo = dot_tn(after(mixed_all, gm_seq), grad_attn)
    early_parts = [
        pad_rows(
            jnp.concatenate([gwo[k * out_rows : (k + 1) * out_rows], small], axis=0), early_rows
        ).astype(BF16)
        for k in range(row_count)
    ]
    early_sent = [swap(early_parts[k], m) for k, m in ((1, 2), (2, 1), (3, 3))]
    grad_packed, diag = lax.optimization_barrier(
        (grad_packed, diag, gi_y, gd_x, *early_sent)
    )[:2]
    early = early_parts[0].astype(F32) + sum(e.astype(F32) for e in early_sent)
    grad_w_in = (gwi[0].astype(F32) + gi_x.astype(F32) + gi_y.astype(F32))[None]
    grad_w_down = (gwd[0].astype(F32) + gd_y.astype(F32) + gd_x.astype(F32))[None]

    def keep_half(value):
        parts = value.reshape(2, -1, width)
        sent = swap_col(lax.dynamic_index_in_dim(parts, 1 - col, 0, keepdims=False).astype(BF16))
        kept = lax.dynamic_index_in_dim(parts, col, 0, keepdims=False)
        return kept.astype(F32) + sent.astype(F32)

    early_half = keep_half(early)

    one_theirs = swap(dot_nt(half(grad_packed, 1 - member), qkv_both).astype(BF16), 1)
    gq = dot_tn(grad_packed, normed_seq)
    gain_part = jnp.sum(gq * qkv_both.T.astype(F32), axis=0) / gain_attn
    table_grad = jnp.dot(
        bucket_hot, diag.reshape(heads, -1).T, precision=lax.Precision.HIGHEST
    )
    late_rows = round_up(qkv_cols + 2, 32)

    def late_block(which, gain):
        cols = table_grad[:, which * heads_here : (which + 1) * heads_here].reshape(1, -1)
        table_row = jnp.concatenate(
            [cols, jnp.zeros((1, width - cols.shape[1]), F32)], axis=1
        )
        block = gq[which * qkv_cols : (which + 1) * qkv_cols]
        return pad_rows(jnp.concatenate([block, gain[None], table_row], axis=0), late_rows)

    late_own = late_block(0, gain_part)
    late_other = late_block(1, gain_part)
    both_half = keep_half(
        jnp.stack([late_own.reshape(2, -1, width), late_other.reshape(2, -1, width)], axis=1)
    ).reshape(2, -1, width)
    late_half = both_half[0] + swap(both_half[1].astype(BF16), 2).astype(F32)
    late_n, early_n = late_half.shape[0], early_half.shape[0]
    total_rows = round_up(late_n + early_n, 16 * 4)
    summed, arrived_z = reduce_z(
        pad_rows(jnp.concatenate([late_half, early_half], axis=0).astype(BF16), total_rows)
    )
    one_theirs = after(one_theirs, arrived_z)
    theirs = swap_col(summed)
    low = jnp.where(col == 0, summed, theirs)
    high = jnp.where(col == 0, theirs, summed)
    late = jnp.concatenate([low[:late_n], high[:late_n]], axis=0).astype(F32)
    early = jnp.concatenate(
        [low[late_n : late_n + early_n], high[late_n : late_n + early_n]], axis=0
    ).astype(F32)
    gain_row = late[qkv_cols]
    slice_n = width // row_count
    gain_slice = lax.dynamic_slice_in_dim(gain_row, row * slice_n, slice_n, 0) + swap(
        lax.dynamic_slice_in_dim(gain_row, (row ^ 1) * slice_n, slice_n, 0), 1
    )
    grad_table = late[qkv_cols + 1, : n_buckets * heads_here].reshape(n_buckets, heads_here)

    grad_one = dot_nt(half(grad_packed, member), qkv_both) + one_theirs.astype(F32)
    grad_input = (grad_hidden + rms_back(tokens_f, inverse_one, gain_attn, grad_one)).astype(BF16)
    mixture = after(mixture, both_half)
    block_out = (hidden_one + mixture.astype(F32)).astype(BF16)
    return (
        block_out,
        grad_input,
        gain_slice,
        late[:qkv_cols].T.reshape(w_qkv.shape),
        early[:out_rows],
        grad_table,
        early[out_rows + n_experts],
        early[out_rows : out_rows + n_experts].T,
        grad_w_in,
        grad_w_down,
    )


def solution(mesh):
    placed = (
        P(("dp", "col", "row"), None),
        P(),
        P(None, "row", None),
        P("row", None),
        P(None, "row"),
        P(),
        P(),
        P(("dp", "col"), None, "row"),
        P(("dp", "col"), "row", None),
        P(("dp", "col", "row"), None),
        P(("dp", "col"), None),
        P(("dp", "col")),
        P(),
    )
    return jax.shard_map(
        local,
        mesh=mesh,
        in_specs=placed,
        out_specs=(
            P(("dp", "col", "row"), None),
            P(("dp", "col", "row"), None),
            P("row"),
            P(None, "row", None),
            P("row", None),
            P(None, "row"),
            P(),
            P(),
            P(("dp", "col"), None, "row"),
            P(("dp", "col"), "row", None),
        ),
        check_vma=False,
    )
```

```python
from functools import partial

import jax
import jax.numpy as jnp
from jax import lax
from jax.experimental import pallas as pl
from jax.experimental.pallas import tpu as pltpu
from jax.sharding import PartitionSpec as P

SEQ = 1024
EPSILON = 1e-06
MASKED = -1e30
BLK = 256
PAD = 16
WIN = BLK + PAD
STEP = 128
PIECE = STEP + PAD
SUB = 4
F32 = jnp.float32
BF16 = jnp.bfloat16
GELU_C = 0.7978845608028654
GELU_A = 0.044715


def dot_nn(a, b):
    return lax.dot_general(a, b, (((1,), (0,)), ((), ())), preferred_element_type=F32)


def dot_nt(a, b):
    return lax.dot_general(a, b, (((1,), (1,)), ((), ())), preferred_element_type=F32)


def dot_tn(a, b):
    return lax.dot_general(a, b, (((0,), (0,)), ((), ())), preferred_element_type=F32)


def cost(micros):
    return pl.CostEstimate(flops=int(micros * 1e9), bytes_accessed=1 << 20, transcendentals=0)


def attn_fwd_kernel(packed_ref, ext_ref, segr_ref, segc_ref, mixed_ref, probs_ref, tile_ref, *, head_size):
    n_blocks = SEQ // BLK
    for hh in range(2):
        base = hh * 3 * head_size
        scale = jnp.asarray(head_size ** (-0.5), BF16)
        q_all = packed_ref[:, base : base + head_size] * scale
        k_all = packed_ref[:, base + head_size : base + 2 * head_size]
        v_all = packed_ref[:, base + 2 * head_size : base + 3 * head_size]
        for t in range(n_blocks):
            rows = jnp.broadcast_to(ext_ref[hh, t : t + 1, :], (BLK, 2 * BLK))
            tile_ref[t] = pltpu.roll(rows, 0, 1, stride=1, stride_axis=0)[:, :BLK]
        for qb in range(n_blocks):
            width = (qb + 1) * BLK
            rows = slice(qb * BLK, (qb + 1) * BLK)
            scores = dot_nt(q_all[rows], k_all[:width])
            bias = jnp.concatenate([tile_ref[qb - kb] for kb in range(qb + 1)], axis=1)
            same = segc_ref[rows, :] == segr_ref[:, :width]
            scores = jnp.where(same, scores + bias, MASKED)
            peak = jnp.max(scores, axis=1, keepdims=True)
            exp_rows = jnp.exp(scores - peak)
            total = jnp.sum(exp_rows, axis=1, keepdims=True)
            probs = (exp_rows * (1.0 / total)).astype(BF16)
            probs_ref[hh, rows, :width] = probs
            mixed_ref[rows, hh * head_size : (hh + 1) * head_size] = dot_nn(
                probs, v_all[:width]
            ).astype(BF16)


def attn_bwd_kernel(
    packed_ref, probs_ref, grad_ref, out_ref, diag_ref, dk_ref, dv_ref, tile_ref, *, head_size
):
    n_blocks = SEQ // BLK
    for hh in range(2):
        base = hh * 3 * head_size
        scale = jnp.asarray(head_size ** (-0.5), BF16)
        q_all = packed_ref[:, base : base + head_size] * scale
        k_all = packed_ref[:, base + head_size : base + 2 * head_size]
        v_all = packed_ref[:, base + 2 * head_size : base + 3 * head_size]
        g_all = grad_ref[:, hh * head_size : (hh + 1) * head_size]
        for qb in reversed(range(n_blocks)):
            width = (qb + 1) * BLK
            rows = slice(qb * BLK, (qb + 1) * BLK)
            probs_b = probs_ref[hh, rows, :width]
            probs = probs_b.astype(F32)
            grad_probs = dot_nt(g_all[rows], v_all[:width])
            delta = jnp.sum(probs * grad_probs, axis=1, keepdims=True)
            grad_scores = probs * (grad_probs - delta)
            scores_b = grad_scores.astype(BF16)
            dq = dot_nn(scores_b, k_all[:width]) * (head_size ** (-0.5))
            out_ref[rows, base : base + head_size] = dq.astype(BF16)
            dk = dot_tn(scores_b, q_all[rows])
            dv = dot_tn(probs_b, g_all[rows])
            if qb == n_blocks - 1:
                dk_ref[...] = dk
                dv_ref[...] = dv
            else:
                dk_ref[:width, :] += dk
                dv_ref[:width, :] += dv
            for kb in range(qb + 1):
                part = grad_scores[:, kb * BLK : (kb + 1) * BLK]
                if qb == n_blocks - 1:
                    tile_ref[qb - kb] = part
                else:
                    tile_ref[qb - kb] += part
        out_ref[:, base + head_size : base + 2 * head_size] = dk_ref[...].astype(BF16)
        out_ref[:, base + 2 * head_size : base + 3 * head_size] = dv_ref[...].astype(BF16)
        for t in range(n_blocks):
            left = tile_ref[t]
            fold = jnp.concatenate([left, jnp.zeros_like(left)], axis=1)
            n = BLK
            while n > 1:
                n //= 2
                fold = fold[:n] + pltpu.roll(fold[n:], 2 * BLK - n, 1)
            diag_ref[hh, t : t + 1, :] = fold


def attention_forward(packed, ext, seg, heads, head_size):
    n_blocks = SEQ // BLK
    return pl.pallas_call(
        partial(attn_fwd_kernel, head_size=head_size),
        name="attn_fwd",
        cost_estimate=cost(20),
        grid=(heads // 2,),
        in_specs=[
            pl.BlockSpec((SEQ, 6 * head_size), lambda p: (0, p)),
            pl.BlockSpec((2, n_blocks, 2 * BLK), lambda p: (p, 0, 0)),
            pl.BlockSpec((1, SEQ), lambda p: (0, 0)),
            pl.BlockSpec((SEQ, 1), lambda p: (0, 0)),
        ],
        out_specs=[
            pl.BlockSpec((SEQ, 2 * head_size), lambda p: (0, p)),
            pl.BlockSpec((2, SEQ, SEQ), lambda p: (p, 0, 0)),
        ],
        out_shape=[
            jax.ShapeDtypeStruct((SEQ, heads * head_size), BF16),
            jax.ShapeDtypeStruct((heads, SEQ, SEQ), BF16),
        ],
        scratch_shapes=[pltpu.VMEM((n_blocks, BLK, BLK), F32)],
    )(packed, ext, seg.reshape(1, SEQ), seg.reshape(SEQ, 1))


def attention_backward(packed, probs, grad_mixed, heads, head_size):
    n_blocks = SEQ // BLK
    return pl.pallas_call(
        partial(attn_bwd_kernel, head_size=head_size),
        name="attn_bwd",
        cost_estimate=cost(27),
        grid=(heads // 2,),
        in_specs=[
            pl.BlockSpec((SEQ, 6 * head_size), lambda p: (0, p)),
            pl.BlockSpec((2, SEQ, SEQ), lambda p: (p, 0, 0)),
            pl.BlockSpec((SEQ, 2 * head_size), lambda p: (0, p)),
        ],
        out_specs=[
            pl.BlockSpec((SEQ, 6 * head_size), lambda p: (0, p)),
            pl.BlockSpec((2, n_blocks, 2 * BLK), lambda p: (p, 0, 0)),
        ],
        out_shape=[
            jax.ShapeDtypeStruct((SEQ, heads * 3 * head_size), BF16),
            jax.ShapeDtypeStruct((heads, n_blocks, 2 * BLK), F32),
        ],
        scratch_shapes=[
            pltpu.VMEM((SEQ, head_size), F32),
            pltpu.VMEM((SEQ, head_size), F32),
            pltpu.VMEM((n_blocks, BLK, BLK), F32),
        ],
    )(packed, probs, grad_mixed)


def window(start):
    return pl.multiple_of((start // PAD) * PAD, PAD)


def hot_rows(rank_row, at, rows):
    return rank_row == (lax.broadcasted_iota(jnp.int32, (rows, BLK), 0) + at)


def n_pieces(scal_ref, block):
    return (scal_ref[block + 1] - scal_ref[block] + STEP - 1) // STEP


def compact_block(scal_ref, block, rank_row, source, dest):
    start = scal_ref[block]

    def piece(j, carry):
        first = start + j * STEP
        at = window(first)
        keep = lax.broadcasted_iota(jnp.int32, (PAD, 1), 0) < (first - at)
        pick = jnp.where(hot_rows(rank_row, at, PIECE), 1.0, 0.0).astype(BF16)
        rows = dot_nn(pick, source).astype(BF16)
        dest[pl.ds(at, PAD), :] = jnp.where(keep, dest[pl.ds(at, PAD), :], rows[:PAD])
        dest[pl.ds(at + PAD, STEP), :] = rows[PAD:]
        return carry

    piece(0, 0)
    lax.fori_loop(1, n_pieces(scal_ref, block), piece, 0)


def compact_end(count, dest):
    at = window(count)
    keep = lax.broadcasted_iota(jnp.int32, (WIN, 1), 0) < (count - at)
    old = dest[pl.ds(at, WIN), :]
    dest[pl.ds(at, WIN), :] = jnp.where(keep, old, jnp.zeros((), old.dtype))


def expand_block(scal_ref, block, rank_row, source, dest, place):
    start = scal_ref[block]

    def piece(j):
        first = start + j * STEP
        at = window(first)
        inside = (rank_row >= first) & (rank_row < first + STEP)
        pick = jnp.where(hot_rows(jnp.where(inside, rank_row, -1), at, PIECE), 1.0, 0.0)
        return dot_tn(pick.astype(BF16), source[pl.ds(at, PIECE), :]).astype(BF16)

    dest[place, :] = piece(0)

    def more(j, carry):
        dest[place, :] += piece(j)
        return carry

    lax.fori_loop(1, n_pieces(scal_ref, block), more, 0)


def compact_kernel(scal_ref, g_ref, rank_ref, other_ref, gc, oc, *, n_blk, sub):
    step = pl.program_id(0)
    for b in range(sub):
        block = step * sub + b
        rank_row = rank_ref[b]
        compact_block(scal_ref, block, rank_row, g_ref[b], gc)
        start = scal_ref[block]

        def ids_piece(j, carry):
            first = start + j * STEP
            at = window(first)
            keep = lax.broadcasted_iota(jnp.int32, (PIECE, 1), 0) < (first - at)
            hot = hot_rows(rank_row, at, PIECE)
            ids = jnp.sum(jnp.where(hot, other_ref[b], 0.0), axis=1, keepdims=True)
            oc[pl.ds(at, PIECE), :] = jnp.where(keep, oc[pl.ds(at, PIECE), :], ids)
            return carry

        ids_piece(0, 0)
        lax.fori_loop(1, n_pieces(scal_ref, block), ids_piece, 0)

    @pl.when(step == n_blk // sub - 1)
    def _():
        compact_end(scal_ref[n_blk], gc)
        compact_end(scal_ref[n_blk], oc)


def run_compact(g_all, rank, other, scal, rows, part, first):
    n_blk = rank.shape[0]
    sub = min(SUB, n_blk)
    width = g_all.shape[2]
    return pl.pallas_call(
        partial(compact_kernel, n_blk=n_blk, sub=sub),
        name="compact",
        cost_estimate=cost(20 if part else 0.5),
        grid_spec=pltpu.PrefetchScalarGridSpec(
            num_scalar_prefetch=1,
            grid=(n_blk // sub,),
            in_specs=[
                pl.BlockSpec((sub, BLK, width), lambda s, sc: (first // sub + s, part, 0)),
                pl.BlockSpec((sub, 1, BLK), lambda s, sc: (s, 0, 0)),
                pl.BlockSpec((sub, 1, BLK), lambda s, sc: (s, 0, 0)),
            ],
            out_specs=[
                pl.BlockSpec((rows, width), lambda s, sc: (0, 0)),
                pl.BlockSpec((rows, 1), lambda s, sc: (0, 0)),
            ],
        ),
        out_shape=[
            jax.ShapeDtypeStruct((rows, width), BF16),
            jax.ShapeDtypeStruct((rows, 1), F32),
        ],
    )(scal, g_all, rank, other)


def expand_kernel(scal_ref, rank_ref, *refs, sub, n_blk):
    out_ref = refs[-1]
    for c in range(len(refs) - 1):

        @pl.when(pl.program_id(0) == c)
        def _():
            for b in range(sub):
                block = c * (n_blk + 2) + pl.program_id(1) * sub + b
                expand_block(scal_ref, block, rank_ref[0, b], refs[c], out_ref.at[b], slice(None))


def run_expand(parts):
    n_parts = len(parts)
    n_blk = parts[0][1].shape[0]
    sub = min(SUB, n_blk)
    rows, width = parts[0][0].shape
    return pl.pallas_call(
        partial(expand_kernel, sub=sub, n_blk=n_blk),
        name="expand",
        cost_estimate=cost(6 * n_parts),
        grid_spec=pltpu.PrefetchScalarGridSpec(
            num_scalar_prefetch=1,
            grid=(n_parts, n_blk // sub),
            in_specs=[pl.BlockSpec((1, sub, 1, BLK), lambda c, s, sc: (c, s, 0, 0))]
            + [pl.BlockSpec((rows, width), lambda c, s, sc: (0, 0))] * n_parts,
            out_specs=pl.BlockSpec((sub, BLK, width), lambda c, s, sc: (s, c, 0)),
        ),
        out_shape=jax.ShapeDtypeStruct((n_blk, n_parts * BLK, width), BF16),
    )(
        jnp.concatenate([p[2] for p in parts]),
        jnp.stack([p[1] for p in parts]),
        *[p[0] for p in parts],
    )


def experts_kernel(
    scal_ref, x_ref, rank_ref, router_ref, oc, gc_hbm, *refs, n_blk, n_ff, sub, chained
):
    win_hbm, wdn_hbm = refs[:n_ff], refs[n_ff : 2 * n_ff]
    refs = refs[2 * n_ff :]
    if chained:
        gwi_old, gwd_old = refs[:n_ff], refs[n_ff : 2 * n_ff]
        refs = refs[2 * n_ff :]
    gr_out, yc_hbm, grt_ref = refs[:3]
    gwi_hbm, gwd_hbm = refs[3 : 3 + n_ff], refs[3 + n_ff : 3 + 2 * n_ff]
    xc, gc, win, wdn, acc_i, acc_d, y_s, gr_s, pre_s, gh_s, sem, old_i, old_d = refs[
        3 + 2 * n_ff :
    ]
    step = pl.program_id(0)
    n_steps = n_blk // sub
    width = xc.shape[1]
    count = scal_ref[n_blk]
    me = scal_ref[n_blk + 1]

    def loads():
        copies = [pltpu.make_async_copy(gc_hbm, gc, sem.at[2 * n_ff])]
        for k in range(n_ff):
            copies.append(pltpu.make_async_copy(win_hbm[k], win.at[k], sem.at[k]))
            copies.append(pltpu.make_async_copy(wdn_hbm[k], wdn.at[k], sem.at[n_ff + k]))
        return copies

    def olds():
        copies = []
        for k in range(n_ff if chained else 0):
            at = 2 * n_ff + 1 + 2 * k
            copies.append(pltpu.make_async_copy(gwi_old[k], old_i.at[k], sem.at[at]))
            copies.append(pltpu.make_async_copy(gwd_old[k], old_d.at[k], sem.at[at + 1]))
        return copies

    def saves():
        copies = [pltpu.make_async_copy(xc, yc_hbm, sem.at[2 * n_ff])]
        for k in range(n_ff):
            copies.append(pltpu.make_async_copy(win.at[k], gwi_hbm[k], sem.at[k]))
            copies.append(pltpu.make_async_copy(wdn.at[k], gwd_hbm[k], sem.at[n_ff + k]))
        return copies

    @pl.when(step == 0)
    def _():
        for copy in loads():
            copy.start()
        for k in range(n_ff):
            acc_i[k] = jnp.zeros((width, width), F32)
            acc_d[k] = jnp.zeros((width, width), F32)

    @pl.when(step < n_steps)
    def _():
        for b in range(sub):
            rows = slice(b * BLK, (b + 1) * BLK)
            compact_block(scal_ref, step * sub + b, rank_ref[b], x_ref[rows, :], xc)

    @pl.when(step == n_steps)
    def _():
        compact_end(count, xc)
        grt_ref[...] = jnp.zeros(grt_ref.shape, F32)
        for copy in loads():
            copy.wait()
        for copy in olds():
            copy.start()
        lane = lax.broadcasted_iota(jnp.int32, (BLK, 128), 1)

        def tile_body(i, carry):
            at_i = pl.multiple_of(i * BLK, BLK)
            x = xc[pl.ds(at_i, BLK), :]
            g = gc[pl.ds(at_i, BLK), :]
            mine_hot = lane == me
            other_hot = lane == oc[pl.ds(at_i, BLK), :].astype(jnp.int32)
            logits = dot_nn(x, router_ref[...])
            diff = jnp.sum(
                jnp.where(mine_hot, logits, 0.0) - jnp.where(other_hot, logits, 0.0),
                axis=1,
                keepdims=True,
            )
            small = jnp.exp(-jnp.abs(diff))
            inv = 1.0 / (1.0 + small)
            gate = jnp.where(diff >= 0, inv, small * inv)
            both = small * inv * inv
            gated = (g.astype(F32) * gate).astype(BF16)

            def first_products(k):
                pre_s[k % 2] = dot_nn(x, win[k])
                gh_s[k % 2] = dot_nt(gated, wdn[k])

            first_products(0)
            for k in range(n_ff):
                if k + 1 < n_ff:
                    first_products(k + 1)
                pre = pre_s[k % 2]
                sq = pre * pre
                th = jnp.tanh(pre * (GELU_C + (GELU_C * GELU_A) * sq))
                half = 0.5 + 0.5 * th
                hid = (pre * half).astype(BF16)
                slope = half + (0.5 * pre) * (1.0 - th * th) * (
                    GELU_C + (3.0 * GELU_C * GELU_A) * sq
                )
                grad_pre = (gh_s[k % 2] * slope).astype(BF16)
                y_new = dot_nn(hid, wdn[k])
                gr_new = dot_nt(grad_pre, win[k])
                y_s[...] = y_s[...] + y_new if k else y_new
                gr_s[...] = gr_s[...] + gr_new if k else gr_new
                acc_d[k] += dot_tn(hid, gated)
                acc_i[k] += dot_tn(x, grad_pre)

            y = y_s[...]
            grad_gate = jnp.sum(g.astype(F32) * y, axis=1, keepdims=True) * both
            d_logit = jnp.where(mine_hot, grad_gate, 0.0) - jnp.where(other_hot, grad_gate, 0.0)
            d_high = d_logit.astype(BF16)
            d_low = (d_logit - d_high.astype(F32)).astype(BF16)
            router = router_ref[...]
            grt_ref[...] += dot_tn(d_high, x) + dot_tn(d_low, x)
            gr = gr_s[...] + (dot_nt(d_high, router) + dot_nt(d_low, router))
            xc[pl.ds(at_i, BLK), :] = (gate * y).astype(BF16)
            gc[pl.ds(at_i, BLK), :] = gr.astype(BF16)
            return carry

        lax.fori_loop(0, (count + BLK - 1) // BLK, tile_body, 0)
        for copy in olds():
            copy.wait()
        for k in range(n_ff):
            if chained:
                win[k] = (acc_i[k] + old_i[k].astype(F32)).astype(BF16)
                wdn[k] = (acc_d[k] + old_d[k].astype(F32)).astype(BF16)
            else:
                win[k] = acc_i[k].astype(BF16)
                wdn[k] = acc_d[k].astype(BF16)
        for copy in saves():
            copy.start()

    @pl.when(step > n_steps)
    def _():
        for b in range(sub):
            place = slice(b * BLK, (b + 1) * BLK)
            block = (step - n_steps - 1) * sub + b
            expand_block(scal_ref, block, rank_ref[b], gc, gr_out, place)

    @pl.when(step == 2 * n_steps)
    def _():
        for copy in saves():
            copy.wait()


def run_experts(x, gc, oc, rank, scal, router, win, wdn, first, old):
    n_blk = rank.shape[0]
    sub = min(SUB, n_blk)
    n_steps = n_blk // sub
    width = x.shape[1]
    n_ff = len(win)
    rows = gc.shape[0]
    n_old = n_ff if old else 1

    def source(s, sc):
        return (first // sub + jnp.minimum(s, n_steps - 1), 0)

    def dest(s, sc):
        return (jnp.maximum(s - n_steps - 1, 0), 0)

    def either(s, sc):
        return (jnp.where(s > n_steps, s - n_steps - 1, jnp.minimum(s, n_steps - 1)), 0, 0)

    hbm = pl.BlockSpec(memory_space=pl.ANY)
    out = pl.pallas_call(
        partial(experts_kernel, n_blk=n_blk, n_ff=n_ff, sub=sub, chained=bool(old)),
        name="experts",
        cost_estimate=cost(40),
        grid_spec=pltpu.PrefetchScalarGridSpec(
            num_scalar_prefetch=1,
            grid=(2 * n_steps + 1,),
            in_specs=[
                pl.BlockSpec((sub * BLK, width), source),
                pl.BlockSpec((sub, 1, BLK), either),
                pl.BlockSpec((width, 128), lambda s, sc: (0, 0)),
                pl.BlockSpec((rows, 1), lambda s, sc: (0, 0)),
                hbm,
            ]
            + [hbm] * (2 * n_ff + len(old)),
            out_specs=[
                pl.BlockSpec((sub * BLK, width), dest),
                hbm,
                pl.BlockSpec((128, width), lambda s, sc: (0, 0)),
            ]
            + [hbm] * (2 * n_ff),
            scratch_shapes=[
                pltpu.VMEM((rows, width), BF16),
                pltpu.VMEM((rows, width), BF16),
                pltpu.VMEM((n_ff, width, width), BF16),
                pltpu.VMEM((n_ff, width, width), BF16),
                pltpu.VMEM((n_ff, width, width), F32),
                pltpu.VMEM((n_ff, width, width), F32),
                pltpu.VMEM((BLK, width), F32),
                pltpu.VMEM((BLK, width), F32),
                pltpu.VMEM((2, BLK, width), F32),
                pltpu.VMEM((2, BLK, width), F32),
                pltpu.SemaphoreType.DMA((4 * n_ff + 1,)),
                pltpu.VMEM((n_old, width, width) if old else (1, 8, 128), BF16),
                pltpu.VMEM((n_old, width, width) if old else (1, 8, 128), BF16),
            ],
        ),
        out_shape=[
            jax.ShapeDtypeStruct((n_blk * BLK, width), BF16),
            jax.ShapeDtypeStruct((rows, width), BF16),
            jax.ShapeDtypeStruct((128, width), F32),
        ]
        + [jax.ShapeDtypeStruct((width, width), BF16)] * (2 * n_ff),
        compiler_params=pltpu.CompilerParams(vmem_limit_bytes=62 * 1024 * 1024),
    )(scal, x, rank, router, oc, gc, *win, *wdn, *old)
    return out[0], out[1], out[2], list(out[3:])


def rms_back(values, inverse, gain_vec, grad_rows):
    scaled = gain_vec * grad_rows
    return inverse * scaled - values * inverse**3 * jnp.mean(values * scaled, axis=1, keepdims=True)


def after(value, *others):
    return lax.optimization_barrier((value,) + others)[0]


def pad_rows(value, rows):
    return jnp.concatenate(
        [value, jnp.zeros((rows - value.shape[0], value.shape[1]), value.dtype)], axis=0
    )


def round_up(n, m):
    return -(-n // m) * m


def reduce_z(value):
    n = lax.axis_size("dp")
    if n > 4:
        total = lax.psum(value, "dp")
        return total, total
    at = lax.axis_index("dp")
    parts = value.reshape(n, -1, value.shape[1])

    def pick(k):
        return lax.dynamic_index_in_dim(parts, (at + k) % n, 0, keepdims=False)

    def shift(v, k):
        return lax.ppermute(v, "dp", [(i, (i + k) % n) for i in range(n)])

    total = pick(0).astype(F32)
    for arrived in [shift(pick(k), k) for k in range(1, n)]:
        total = total + arrived.astype(F32)
    total = total.astype(BF16)
    pieces = [total] + [shift(total, k) for k in range(1, n)]
    rows = []
    for j in range(n):
        row = pieces[0]
        for k in range(1, n):
            row = jnp.where((at - k) % n == j, pieces[k], row)
        rows.append(row)
    return jnp.concatenate(rows, axis=0), total


def local(
    tokens_in,
    gain_attn,
    w_qkv,
    w_out,
    rel_table,
    gain_moe,
    w_router,
    w_in,
    w_down,
    grad_out,
    routes,
    segments,
    rel_buckets,
):
    row_count = lax.axis_size("row")
    n_groups = lax.axis_size("dp") * lax.axis_size("col")
    tok_dev, width = tokens_in.shape
    tok_group = tok_dev * row_count
    n_experts = w_router.shape[1]
    capacity = 4 * tok_group // n_experts
    heads_here = w_qkv.shape[1]
    head_size = w_qkv.shape[2] // 3
    n_seqs = tok_group // SEQ
    assert row_count == 4 and n_seqs == 2 and n_experts == n_groups
    heads = 2 * heads_here
    row = lax.axis_index("row")
    col = lax.axis_index("col")
    member = row % 2
    first_half = member == 0

    def swap(value, mask):
        return lax.ppermute(value, "row", [(i, i ^ mask) for i in range(row_count)])

    def swap_col(value):
        return lax.ppermute(value, "col", [(0, 1), (1, 0)])

    def in_order(own, theirs):
        return jnp.where(
            first_half,
            jnp.concatenate([own, theirs], axis=0),
            jnp.concatenate([theirs, own], axis=0),
        )

    def half(value, which):
        return lax.dynamic_slice_in_dim(value, which * tok_dev, tok_dev, 0)

    tokens_f = tokens_in.astype(F32)
    inverse_one = lax.rsqrt(jnp.mean(tokens_f * tokens_f, axis=1, keepdims=True) + EPSILON)
    normed_one = (tokens_f * inverse_one * gain_attn).astype(BF16)
    qkv_mine = w_qkv.reshape(width, -1)
    qkv_cols = qkv_mine.shape[1]
    qkv_other = swap(qkv_mine, 2)
    normed_other = swap(normed_one, 1)
    table_other = swap(rel_table, 2)

    routes_mine = lax.dynamic_slice_in_dim(routes, row * tok_dev, tok_dev, 0).T
    route_len = round_up(2 * tok_dev, PAD * width)
    routes_row = jnp.concatenate(
        [routes_mine.reshape(-1), jnp.zeros((route_len - 2 * tok_dev,), jnp.int32)]
    )
    grad_ext = jnp.concatenate([grad_out, routes_row.astype(BF16).reshape(-1, width)], axis=0)
    grad_all = lax.all_gather(grad_ext, ("dp", "col"), axis=0, tiled=False)

    normed_seq = in_order(normed_one, normed_other)
    qkv_both = jnp.concatenate([qkv_mine, qkv_other], axis=1)
    packed = jnp.dot(normed_seq, qkv_both, preferred_element_type=F32).astype(BF16)

    w_in_mine, w_down_mine, w_out_mine = (
        after(w, normed_other, qkv_other) for w in (w_in[0], w_down[0], w_out)
    )
    wo_x = swap(w_out_mine, 1)
    wo_y = swap(w_out_mine, 2)
    wo_d = swap(wo_x, 2)
    w_out_all = jnp.concatenate([w_out_mine, wo_y, wo_x, wo_d], axis=0)
    wi_x = swap(w_in_mine, 1)
    wd_y = swap(w_down_mine, 2)
    wi_y = swap(w_in_mine, 2)
    wd_x = swap(w_down_mine, 1)
    wi_d = swap(wi_x, 2)
    wd_d = swap(wd_y, 1)
    win_parts = [w_in_mine, wi_y, wi_x, wi_d]
    wdn_parts = [w_down_mine, wd_y, wd_x, wd_d]

    n_blocks = SEQ // BLK
    padded = jnp.concatenate(
        [jnp.full((BLK,), -1, jnp.int32), rel_buckets, rel_buckets[SEQ - 1 :]]
    )
    flipped = padded[::-1]
    pieces = []
    for t in range(n_blocks):
        begin = SEQ - (t + 1) * BLK
        piece = flipped[begin : begin + 2 * BLK]
        pieces += [piece[BLK:], piece[:BLK]]
    bucket_seq = jnp.concatenate(pieces)
    n_buckets = rel_table.shape[0]
    bucket_hot = (
        jnp.arange(n_buckets, dtype=jnp.int32)[:, None] == bucket_seq[None, :]
    ).astype(F32)
    table_both = jnp.concatenate([rel_table, table_other], axis=1)
    ext = jnp.dot(table_both.T, bucket_hot, precision=lax.Precision.HIGHEST)
    ext = jnp.where(bucket_seq[None, :] < 0, MASKED, ext).reshape(heads, n_blocks, 2 * BLK)
    segment_ids = lax.dynamic_slice_in_dim(segments, (row // 2) * SEQ, SEQ, 0)

    mixed, probs = attention_forward(packed, ext, segment_ids, heads, head_size)
    mixed = after(mixed, wi_x, wd_y)
    mixed_mine = half(mixed, member)
    mixed_theirs = swap(half(mixed, 1 - member), 1)
    mixed_all = jnp.concatenate([mixed_mine, mixed_theirs], axis=1)
    attention = jnp.dot(mixed_all, w_out_all, preferred_element_type=F32)
    hidden_one = tokens_f + attention
    inverse_two = lax.rsqrt(jnp.mean(hidden_one * hidden_one, axis=1, keepdims=True) + EPSILON)
    normed_two = (hidden_one * inverse_two * gain_moe).astype(BF16)
    n_parts = tok_dev // BLK
    normed_all = []
    for c in range(n_parts):
        piece = normed_two[c * BLK : (c + 1) * BLK]
        normed_all.append(piece)

    me = lax.axis_index("dp") * lax.axis_size("col") + col
    routes_all = (
        grad_all[:, tok_dev:]
        .reshape(n_groups, -1)[:, : 2 * tok_dev]
        .astype(jnp.int32)
        .reshape(n_groups, 2, n_parts, BLK)
    )
    hit = routes_all == me
    mine = hit[:, 0] | hit[:, 1]
    other = jnp.sum(jnp.where(hit, 0, routes_all), axis=1).astype(F32)
    before = (
        jnp.arange(BLK, dtype=jnp.int32)[:, None] < jnp.arange(BLK, dtype=jnp.int32)[None, :]
    ).astype(BF16)
    place = jnp.dot(
        mine.reshape(-1, BLK).astype(BF16), before, preferred_element_type=F32
    ).astype(jnp.int32).reshape(mine.shape)
    totals = jnp.sum(mine.astype(jnp.int32), axis=2)

    router_pad = jnp.concatenate(
        [w_router, jnp.zeros((width, 128 - n_experts), BF16)], axis=1
    )
    max_group = min(BLK, capacity)
    chunk = min(n_groups, 2048 // max_group)
    rows = chunk * max_group + WIN + PAD
    index = jnp.arange(chunk + 1, dtype=jnp.int32)
    plans = []
    for c in range(n_parts):
        for g0 in range(0, n_groups, chunk):
            tot = totals[g0 : g0 + chunk, c]
            starts = jnp.sum(
                jnp.where(index[None, :chunk] < index[:, None], tot[None, :], 0), axis=1
            )
            rank = jnp.where(
                mine[g0 : g0 + chunk, c],
                place[g0 : g0 + chunk, c] + starts[:chunk, None],
                -1,
            ).reshape(-1, 1, BLK)
            scal = jnp.concatenate([starts, me[None].astype(jnp.int32)])
            others = other[g0 : g0 + chunk, c].reshape(-1, 1, BLK)
            grad_src = after(grad_all, wi_y, wd_x) if c else grad_all
            gc, oc = run_compact(grad_src, rank, others, scal, rows, c, g0)
            plans.append((c, g0, rank, scal, gc, oc))
    for c in range(n_parts):
        if c:
            piece = after(normed_all[c], wi_y, wd_x, *[p[4] for p in plans if p[0] == c - 1])
        else:
            piece = after(normed_all[c], grad_all)
        normed_all[c] = lax.all_gather(piece, ("dp", "col"), axis=0, tiled=True)
    grad_parts = [[] for unused in range(n_parts)]
    y_parts = [[] for unused in range(n_parts)]
    weight_grads = []
    grt = 0.0
    last_gc = plans[-1][4]
    for c, g0, rank, scal, gc, oc in plans:
        gr, yc, grt_part, weight_grads = run_experts(
            normed_all[c], gc, after(oc, last_gc), rank, scal, router_pad,
            win_parts, wdn_parts, g0, weight_grads,
        )
        grad_parts[c].append(gr)
        y_parts[c].append((yc, rank, scal))
        grt = grt + grt_part

    def scatter(value):
        return lax.psum_scatter(value, ("dp", "col"), scatter_dimension=0, tiled=True)

    def join(values):
        return values[0] if len(values) == 1 else jnp.concatenate(values, axis=0)

    grad_two = jnp.concatenate([scatter(join(g)) for g in grad_parts], axis=0)
    last = grad_parts[-1][-1]
    y_all = join(
        [
            run_expand([(after(y[at][0], last),) + y[at][1:] for y in y_parts])
            for at in range(n_groups // chunk)
        ]
    ).reshape(-1, width)

    gwi, gwd = weight_grads[:row_count], weight_grads[row_count:]
    gi_x, gi_d = swap(gwi[2], 1), swap(gwi[3], 1)
    gd_y, gd_d = swap(gwd[1], 2), swap(gwd[3], 2)
    gi_two = (gwi[1].astype(F32) + gi_d.astype(F32)).astype(BF16)
    gd_two = (gwd[2].astype(F32) + gd_d.astype(F32)).astype(BF16)
    grad_two = after(grad_two, gi_x, gi_two, gd_y, gd_two, y_all).astype(F32)

    cotangent = grad_out.astype(F32)
    grad_gain_moe = jnp.sum(grad_two * (hidden_one * inverse_two), axis=0)
    grad_hidden = cotangent + rms_back(hidden_one, inverse_two, gain_moe, grad_two)
    grad_attn = grad_hidden.astype(BF16)
    grad_mixed = dot_nt(grad_attn, w_out_all).astype(BF16)
    half_cols = heads * head_size
    gm_theirs = swap(grad_mixed[:, half_cols:], 1)
    out_rows = w_out.shape[0]
    small = jnp.concatenate([grt[:n_experts], grad_gain_moe[None]], axis=0)
    early_rows = round_up(out_rows + small.shape[0], 32)
    gwo = dot_tn(mixed_all, grad_attn)
    early_parts = [
        pad_rows(
            jnp.concatenate([gwo[k * out_rows : (k + 1) * out_rows], small], axis=0), early_rows
        ).astype(BF16)
        for k in range(row_count)
    ]
    gm_theirs = after(gm_theirs, *early_parts)
    gm_seq = in_order(grad_mixed[:, :half_cols], gm_theirs)
    mixture = scatter(after(y_all, gm_seq))
    gi_y = swap(after(gi_two, gm_seq), 2)
    gd_x = swap(after(gd_two, gm_seq), 1)
    grad_packed, diag = attention_backward(packed, probs, gm_seq, heads, head_size)

    early_sent = [swap(early_parts[k], m) for k, m in ((1, 2), (2, 1), (3, 3))]
    grad_packed, diag = lax.optimization_barrier(
        (grad_packed, diag, gi_y, gd_x, *early_sent)
    )[:2]
    early = early_parts[0].astype(F32) + sum(e.astype(F32) for e in early_sent)
    grad_w_in = (gwi[0].astype(F32) + gi_x.astype(F32) + gi_y.astype(F32))[None]
    grad_w_down = (gwd[0].astype(F32) + gd_y.astype(F32) + gd_x.astype(F32))[None]

    def keep_half(value):
        parts = value.reshape(2, -1, width)
        sent = swap_col(lax.dynamic_index_in_dim(parts, 1 - col, 0, keepdims=False).astype(BF16))
        kept = lax.dynamic_index_in_dim(parts, col, 0, keepdims=False)
        return kept.astype(F32) + sent.astype(F32)

    early_half = keep_half(early)

    one_theirs = swap(dot_nt(half(grad_packed, 1 - member), qkv_both).astype(BF16), 1)
    gq = dot_tn(grad_packed, normed_seq)
    gain_part = jnp.sum(gq * qkv_both.T.astype(F32), axis=0) / gain_attn
    table_grad = jnp.dot(
        bucket_hot, diag.reshape(heads, -1).T, precision=lax.Precision.HIGHEST
    )
    late_rows = round_up(qkv_cols + 2, 32)

    def late_block(which, gain):
        cols = table_grad[:, which * heads_here : (which + 1) * heads_here].reshape(1, -1)
        table_row = jnp.concatenate(
            [cols, jnp.zeros((1, width - cols.shape[1]), F32)], axis=1
        )
        block = gq[which * qkv_cols : (which + 1) * qkv_cols]
        return pad_rows(jnp.concatenate([block, gain[None], table_row], axis=0), late_rows)

    late_own = late_block(0, gain_part)
    late_other = late_block(1, gain_part)
    both_half = keep_half(
        jnp.stack([late_own.reshape(2, -1, width), late_other.reshape(2, -1, width)], axis=1)
    ).reshape(2, -1, width)
    late_half = both_half[0] + swap(both_half[1].astype(BF16), 2).astype(F32)
    late_n, early_n = late_half.shape[0], early_half.shape[0]
    total_rows = round_up(late_n + early_n, 16 * 4)
    summed, arrived_z = reduce_z(
        pad_rows(jnp.concatenate([late_half, early_half], axis=0).astype(BF16), total_rows)
    )
    one_theirs = after(one_theirs, arrived_z)
    theirs = swap_col(summed)
    low = jnp.where(col == 0, summed, theirs)
    high = jnp.where(col == 0, theirs, summed)
    late = jnp.concatenate([low[:late_n], high[:late_n]], axis=0).astype(F32)
    early = jnp.concatenate(
        [low[late_n : late_n + early_n], high[late_n : late_n + early_n]], axis=0
    ).astype(F32)
    gain_row = late[qkv_cols]
    slice_n = width // row_count
    gain_slice = lax.dynamic_slice_in_dim(gain_row, row * slice_n, slice_n, 0) + swap(
        lax.dynamic_slice_in_dim(gain_row, (row ^ 1) * slice_n, slice_n, 0), 1
    )
    grad_table = late[qkv_cols + 1, : n_buckets * heads_here].reshape(n_buckets, heads_here)

    grad_one = dot_nt(half(grad_packed, member), qkv_both) + one_theirs.astype(F32)
    grad_input = (grad_hidden + rms_back(tokens_f, inverse_one, gain_attn, grad_one)).astype(BF16)
    mixture = after(mixture, both_half)
    block_out = (hidden_one + mixture.astype(F32)).astype(BF16)
    return (
        block_out,
        grad_input,
        gain_slice,
        late[:qkv_cols].T.reshape(w_qkv.shape),
        early[:out_rows],
        grad_table,
        early[out_rows + n_experts],
        early[out_rows : out_rows + n_experts].T,
        grad_w_in,
        grad_w_down,
    )


def solution(mesh):
    placed = (
        P(("dp", "col", "row"), None),
        P(),
        P(None, "row", None),
        P("row", None),
        P(None, "row"),
        P(),
        P(),
        P(("dp", "col"), None, "row"),
        P(("dp", "col"), "row", None),
        P(("dp", "col", "row"), None),
        P(("dp", "col"), None),
        P(("dp", "col")),
        P(),
    )
    return jax.shard_map(
        local,
        mesh=mesh,
        in_specs=placed,
        out_specs=(
            P(("dp", "col", "row"), None),
            P(("dp", "col", "row"), None),
            P("row"),
            P(None, "row", None),
            P("row", None),
            P(None, "row"),
            P(),
            P(),
            P(("dp", "col"), None, "row"),
            P(("dp", "col"), "row", None),
        ),
        check_vma=False,
    )
```

```python
from functools import partial

import jax
import jax.numpy as jnp
from jax import lax
from jax.experimental import pallas as pl
from jax.experimental.pallas import tpu as pltpu
from jax.sharding import PartitionSpec as P

SEQ = 1024
EPSILON = 1e-06
MASKED = -1e30
BLK = 256
PAD = 16
WIN = BLK + PAD
STEP = 128
PIECE = STEP + PAD
SUB = 4
F32 = jnp.float32
BF16 = jnp.bfloat16
GELU_C = 0.7978845608028654
GELU_A = 0.044715


def dot_nn(a, b):
    return lax.dot_general(a, b, (((1,), (0,)), ((), ())), preferred_element_type=F32)


def dot_nt(a, b):
    return lax.dot_general(a, b, (((1,), (1,)), ((), ())), preferred_element_type=F32)


def dot_tn(a, b):
    return lax.dot_general(a, b, (((0,), (0,)), ((), ())), preferred_element_type=F32)


def cost(micros):
    return pl.CostEstimate(flops=int(micros * 1e9), bytes_accessed=1 << 20, transcendentals=0)


def attn_fwd_kernel(packed_ref, ext_ref, segr_ref, segc_ref, mixed_ref, probs_ref, tile_ref, *, head_size):
    n_blocks = SEQ // BLK
    for hh in range(2):
        base = hh * 3 * head_size
        scale = jnp.asarray(head_size ** (-0.5), BF16)
        q_all = packed_ref[:, base : base + head_size] * scale
        k_all = packed_ref[:, base + head_size : base + 2 * head_size]
        v_all = packed_ref[:, base + 2 * head_size : base + 3 * head_size]
        for t in range(n_blocks):
            rows = jnp.broadcast_to(ext_ref[hh, t : t + 1, :], (BLK, 2 * BLK))
            tile_ref[t] = pltpu.roll(rows, 0, 1, stride=1, stride_axis=0)[:, :BLK]
        for qb in range(n_blocks):
            width = (qb + 1) * BLK
            rows = slice(qb * BLK, (qb + 1) * BLK)
            scores = dot_nt(q_all[rows], k_all[:width])
            bias = jnp.concatenate([tile_ref[qb - kb] for kb in range(qb + 1)], axis=1)
            same = segc_ref[rows, :] == segr_ref[:, :width]
            scores = jnp.where(same, scores + bias, MASKED)
            peak = jnp.max(scores, axis=1, keepdims=True)
            exp_rows = jnp.exp(scores - peak)
            total = jnp.sum(exp_rows, axis=1, keepdims=True)
            probs = (exp_rows * (1.0 / total)).astype(BF16)
            probs_ref[hh, rows, :width] = probs
            mixed_ref[rows, hh * head_size : (hh + 1) * head_size] = dot_nn(
                probs, v_all[:width]
            ).astype(BF16)


def attn_bwd_kernel(
    packed_ref, probs_ref, grad_ref, out_ref, diag_ref, dk_ref, dv_ref, tile_ref, *, head_size
):
    n_blocks = SEQ // BLK
    for hh in range(2):
        base = hh * 3 * head_size
        scale = jnp.asarray(head_size ** (-0.5), BF16)
        q_all = packed_ref[:, base : base + head_size] * scale
        k_all = packed_ref[:, base + head_size : base + 2 * head_size]
        v_all = packed_ref[:, base + 2 * head_size : base + 3 * head_size]
        g_all = grad_ref[:, hh * head_size : (hh + 1) * head_size]
        for qb in reversed(range(n_blocks)):
            width = (qb + 1) * BLK
            rows = slice(qb * BLK, (qb + 1) * BLK)
            probs_b = probs_ref[hh, rows, :width]
            probs = probs_b.astype(F32)
            grad_probs = dot_nt(g_all[rows], v_all[:width])
            delta = jnp.sum(probs * grad_probs, axis=1, keepdims=True)
            grad_scores = probs * (grad_probs - delta)
            scores_b = grad_scores.astype(BF16)
            dq = dot_nn(scores_b, k_all[:width]) * (head_size ** (-0.5))
            out_ref[rows, base : base + head_size] = dq.astype(BF16)
            dk = dot_tn(scores_b, q_all[rows])
            dv = dot_tn(probs_b, g_all[rows])
            if qb == n_blocks - 1:
                dk_ref[...] = dk
                dv_ref[...] = dv
            else:
                dk_ref[:width, :] += dk
                dv_ref[:width, :] += dv
            for kb in range(qb + 1):
                part = grad_scores[:, kb * BLK : (kb + 1) * BLK]
                if qb == n_blocks - 1:
                    tile_ref[qb - kb] = part
                else:
                    tile_ref[qb - kb] += part
        out_ref[:, base + head_size : base + 2 * head_size] = dk_ref[...].astype(BF16)
        out_ref[:, base + 2 * head_size : base + 3 * head_size] = dv_ref[...].astype(BF16)
        for t in range(n_blocks):
            left = tile_ref[t]
            fold = jnp.concatenate([left, jnp.zeros_like(left)], axis=1)
            n = BLK
            while n > 1:
                n //= 2
                fold = fold[:n] + pltpu.roll(fold[n:], 2 * BLK - n, 1)
            diag_ref[hh, t : t + 1, :] = fold


def attention_forward(packed, ext, seg, heads, head_size):
    n_blocks = SEQ // BLK
    return pl.pallas_call(
        partial(attn_fwd_kernel, head_size=head_size),
        name="attn_fwd",
        cost_estimate=cost(20),
        grid=(heads // 2,),
        in_specs=[
            pl.BlockSpec((SEQ, 6 * head_size), lambda p: (0, p)),
            pl.BlockSpec((2, n_blocks, 2 * BLK), lambda p: (p, 0, 0)),
            pl.BlockSpec((1, SEQ), lambda p: (0, 0)),
            pl.BlockSpec((SEQ, 1), lambda p: (0, 0)),
        ],
        out_specs=[
            pl.BlockSpec((SEQ, 2 * head_size), lambda p: (0, p)),
            pl.BlockSpec((2, SEQ, SEQ), lambda p: (p, 0, 0)),
        ],
        out_shape=[
            jax.ShapeDtypeStruct((SEQ, heads * head_size), BF16),
            jax.ShapeDtypeStruct((heads, SEQ, SEQ), BF16),
        ],
        scratch_shapes=[pltpu.VMEM((n_blocks, BLK, BLK), F32)],
    )(packed, ext, seg.reshape(1, SEQ), seg.reshape(SEQ, 1))


def attention_backward(packed, probs, grad_mixed, heads, head_size):
    n_blocks = SEQ // BLK
    return pl.pallas_call(
        partial(attn_bwd_kernel, head_size=head_size),
        name="attn_bwd",
        cost_estimate=cost(27),
        grid=(heads // 2,),
        in_specs=[
            pl.BlockSpec((SEQ, 6 * head_size), lambda p: (0, p)),
            pl.BlockSpec((2, SEQ, SEQ), lambda p: (p, 0, 0)),
            pl.BlockSpec((SEQ, 2 * head_size), lambda p: (0, p)),
        ],
        out_specs=[
            pl.BlockSpec((SEQ, 6 * head_size), lambda p: (0, p)),
            pl.BlockSpec((2, n_blocks, 2 * BLK), lambda p: (p, 0, 0)),
        ],
        out_shape=[
            jax.ShapeDtypeStruct((SEQ, heads * 3 * head_size), BF16),
            jax.ShapeDtypeStruct((heads, n_blocks, 2 * BLK), F32),
        ],
        scratch_shapes=[
            pltpu.VMEM((SEQ, head_size), F32),
            pltpu.VMEM((SEQ, head_size), F32),
            pltpu.VMEM((n_blocks, BLK, BLK), F32),
        ],
    )(packed, probs, grad_mixed)


def window(start):
    return pl.multiple_of((start // PAD) * PAD, PAD)


def hot_rows(rank_row, at, rows):
    return rank_row == (lax.broadcasted_iota(jnp.int32, (rows, BLK), 0) + at)


def n_pieces(scal_ref, block):
    return (scal_ref[block + 1] - scal_ref[block] + STEP - 1) // STEP


def compact_block(scal_ref, block, rank_row, source, dest):
    start = scal_ref[block]

    def piece(j, carry):
        first = start + j * STEP
        at = window(first)
        keep = lax.broadcasted_iota(jnp.int32, (PAD, 1), 0) < (first - at)
        pick = jnp.where(hot_rows(rank_row, at, PIECE), 1.0, 0.0).astype(BF16)
        rows = dot_nn(pick, source).astype(BF16)
        dest[pl.ds(at, PAD), :] = jnp.where(keep, dest[pl.ds(at, PAD), :], rows[:PAD])
        dest[pl.ds(at + PAD, STEP), :] = rows[PAD:]
        return carry

    piece(0, 0)
    lax.fori_loop(1, n_pieces(scal_ref, block), piece, 0)


def compact_end(count, dest):
    at = window(count)
    keep = lax.broadcasted_iota(jnp.int32, (WIN, 1), 0) < (count - at)
    old = dest[pl.ds(at, WIN), :]
    dest[pl.ds(at, WIN), :] = jnp.where(keep, old, jnp.zeros((), old.dtype))


def expand_block(scal_ref, block, rank_row, source, dest, place):
    start = scal_ref[block]

    def piece(j):
        first = start + j * STEP
        at = window(first)
        inside = (rank_row >= first) & (rank_row < first + STEP)
        pick = jnp.where(hot_rows(jnp.where(inside, rank_row, -1), at, PIECE), 1.0, 0.0)
        return dot_tn(pick.astype(BF16), source[pl.ds(at, PIECE), :]).astype(BF16)

    dest[place, :] = piece(0)

    def more(j, carry):
        dest[place, :] += piece(j)
        return carry

    lax.fori_loop(1, n_pieces(scal_ref, block), more, 0)


def compact_kernel(scal_ref, g_ref, rank_ref, other_ref, gc, oc, *, n_blk, sub):
    step = pl.program_id(0)
    for b in range(sub):
        block = step * sub + b
        rank_row = rank_ref[b]
        compact_block(scal_ref, block, rank_row, g_ref[b], gc)
        start = scal_ref[block]

        def ids_piece(j, carry):
            first = start + j * STEP
            at = window(first)
            keep = lax.broadcasted_iota(jnp.int32, (PIECE, 1), 0) < (first - at)
            hot = hot_rows(rank_row, at, PIECE)
            ids = jnp.sum(jnp.where(hot, other_ref[b], 0.0), axis=1, keepdims=True)
            oc[pl.ds(at, PIECE), :] = jnp.where(keep, oc[pl.ds(at, PIECE), :], ids)
            return carry

        ids_piece(0, 0)
        lax.fori_loop(1, n_pieces(scal_ref, block), ids_piece, 0)

    @pl.when(step == n_blk // sub - 1)
    def _():
        compact_end(scal_ref[n_blk], gc)
        compact_end(scal_ref[n_blk], oc)


def run_compact(g_all, rank, other, scal, rows, part, first):
    n_blk = rank.shape[0]
    sub = min(SUB, n_blk)
    width = g_all.shape[2]
    return pl.pallas_call(
        partial(compact_kernel, n_blk=n_blk, sub=sub),
        name="compact",
        cost_estimate=cost(20 if part else 0.5),
        grid_spec=pltpu.PrefetchScalarGridSpec(
            num_scalar_prefetch=1,
            grid=(n_blk // sub,),
            in_specs=[
                pl.BlockSpec((sub, BLK, width), lambda s, sc: (first // sub + s, part, 0)),
                pl.BlockSpec((sub, 1, BLK), lambda s, sc: (s, 0, 0)),
                pl.BlockSpec((sub, 1, BLK), lambda s, sc: (s, 0, 0)),
            ],
            out_specs=[
                pl.BlockSpec((rows, width), lambda s, sc: (0, 0)),
                pl.BlockSpec((rows, 1), lambda s, sc: (0, 0)),
            ],
        ),
        out_shape=[
            jax.ShapeDtypeStruct((rows, width), BF16),
            jax.ShapeDtypeStruct((rows, 1), F32),
        ],
    )(scal, g_all, rank, other)


def expand_kernel(scal_ref, rank_ref, *refs, sub, n_blk):
    out_ref = refs[-1]
    for c in range(len(refs) - 1):

        @pl.when(pl.program_id(0) == c)
        def _():
            for b in range(sub):
                block = c * (n_blk + 2) + pl.program_id(1) * sub + b
                expand_block(scal_ref, block, rank_ref[0, b], refs[c], out_ref.at[b], slice(None))


def run_expand(parts):
    n_parts = len(parts)
    n_blk = parts[0][1].shape[0]
    sub = min(SUB, n_blk)
    rows, width = parts[0][0].shape
    return pl.pallas_call(
        partial(expand_kernel, sub=sub, n_blk=n_blk),
        name="expand",
        cost_estimate=cost(6 * n_parts),
        grid_spec=pltpu.PrefetchScalarGridSpec(
            num_scalar_prefetch=1,
            grid=(n_parts, n_blk // sub),
            in_specs=[pl.BlockSpec((1, sub, 1, BLK), lambda c, s, sc: (c, s, 0, 0))]
            + [pl.BlockSpec((rows, width), lambda c, s, sc: (0, 0))] * n_parts,
            out_specs=pl.BlockSpec((sub, BLK, width), lambda c, s, sc: (s, c, 0)),
        ),
        out_shape=jax.ShapeDtypeStruct((n_blk, n_parts * BLK, width), BF16),
    )(
        jnp.concatenate([p[2] for p in parts]),
        jnp.stack([p[1] for p in parts]),
        *[p[0] for p in parts],
    )


def experts_kernel(
    scal_ref, x_ref, rank_ref, router_ref, oc, gc_hbm, *refs, n_blk, n_ff, sub, chained
):
    win_hbm, wdn_hbm = refs[:n_ff], refs[n_ff : 2 * n_ff]
    refs = refs[2 * n_ff :]
    if chained:
        gwi_old, gwd_old = refs[:n_ff], refs[n_ff : 2 * n_ff]
        refs = refs[2 * n_ff :]
    gr_out, yc_hbm, grt_ref = refs[:3]
    gwi_hbm, gwd_hbm = refs[3 : 3 + n_ff], refs[3 + n_ff : 3 + 2 * n_ff]
    xc, gc, win, wdn, acc_i, acc_d, y_s, gr_s, pre_s, gh_s, sem, old_i, old_d = refs[
        3 + 2 * n_ff :
    ]
    step = pl.program_id(0)
    n_steps = n_blk // sub
    width = xc.shape[1]
    count = scal_ref[n_blk]
    me = scal_ref[n_blk + 1]

    def loads():
        copies = [pltpu.make_async_copy(gc_hbm, gc, sem.at[2 * n_ff])]
        for k in range(n_ff):
            copies.append(pltpu.make_async_copy(win_hbm[k], win.at[k], sem.at[k]))
            copies.append(pltpu.make_async_copy(wdn_hbm[k], wdn.at[k], sem.at[n_ff + k]))
        return copies

    def olds():
        copies = []
        for k in range(n_ff if chained else 0):
            at = 2 * n_ff + 1 + 2 * k
            copies.append(pltpu.make_async_copy(gwi_old[k], old_i.at[k], sem.at[at]))
            copies.append(pltpu.make_async_copy(gwd_old[k], old_d.at[k], sem.at[at + 1]))
        return copies

    def saves():
        copies = [pltpu.make_async_copy(xc, yc_hbm, sem.at[2 * n_ff])]
        for k in range(n_ff):
            copies.append(pltpu.make_async_copy(win.at[k], gwi_hbm[k], sem.at[k]))
            copies.append(pltpu.make_async_copy(wdn.at[k], gwd_hbm[k], sem.at[n_ff + k]))
        return copies

    @pl.when(step == 0)
    def _():
        for copy in loads():
            copy.start()
        for k in range(n_ff):
            acc_i[k] = jnp.zeros((width, width), F32)
            acc_d[k] = jnp.zeros((width, width), F32)

    @pl.when(step < n_steps)
    def _():
        for b in range(sub):
            rows = slice(b * BLK, (b + 1) * BLK)
            compact_block(scal_ref, step * sub + b, rank_ref[b], x_ref[rows, :], xc)

    @pl.when(step == n_steps)
    def _():
        compact_end(count, xc)
        grt_ref[...] = jnp.zeros(grt_ref.shape, F32)
        for copy in loads():
            copy.wait()
        for copy in olds():
            copy.start()
        lane = lax.broadcasted_iota(jnp.int32, (BLK, 128), 1)

        def tile_body(i, carry):
            at_i = pl.multiple_of(i * BLK, BLK)
            x = xc[pl.ds(at_i, BLK), :]
            g = gc[pl.ds(at_i, BLK), :]
            mine_hot = lane == me
            other_hot = lane == oc[pl.ds(at_i, BLK), :].astype(jnp.int32)
            logits = dot_nn(x, router_ref[...])
            diff = jnp.sum(
                jnp.where(mine_hot, logits, 0.0) - jnp.where(other_hot, logits, 0.0),
                axis=1,
                keepdims=True,
            )
            small = jnp.exp(-jnp.abs(diff))
            inv = 1.0 / (1.0 + small)
            gate = jnp.where(diff >= 0, inv, small * inv)
            both = small * inv * inv
            gated = (g.astype(F32) * gate).astype(BF16)

            def first_products(k):
                pre_s[k % 2] = dot_nn(x, win[k])
                gh_s[k % 2] = dot_nt(gated, wdn[k])

            first_products(0)
            for k in range(n_ff):
                if k + 1 < n_ff:
                    first_products(k + 1)
                pre = pre_s[k % 2]
                sq = pre * pre
                th = jnp.tanh(pre * (GELU_C + (GELU_C * GELU_A) * sq))
                half = 0.5 + 0.5 * th
                hid = (pre * half).astype(BF16)
                slope = half + (0.5 * pre) * (1.0 - th * th) * (
                    GELU_C + (3.0 * GELU_C * GELU_A) * sq
                )
                grad_pre = (gh_s[k % 2] * slope).astype(BF16)
                y_new = dot_nn(hid, wdn[k])
                gr_new = dot_nt(grad_pre, win[k])
                y_s[...] = y_s[...] + y_new if k else y_new
                gr_s[...] = gr_s[...] + gr_new if k else gr_new
                acc_d[k] += dot_tn(hid, gated)
                acc_i[k] += dot_tn(x, grad_pre)

            y = y_s[...]
            grad_gate = jnp.sum(g.astype(F32) * y, axis=1, keepdims=True) * both
            d_logit = jnp.where(mine_hot, grad_gate, 0.0) - jnp.where(other_hot, grad_gate, 0.0)
            d_high = d_logit.astype(BF16)
            d_low = (d_logit - d_high.astype(F32)).astype(BF16)
            router = router_ref[...]
            grt_ref[...] += dot_tn(d_high, x) + dot_tn(d_low, x)
            gr = gr_s[...] + (dot_nt(d_high, router) + dot_nt(d_low, router))
            xc[pl.ds(at_i, BLK), :] = (gate * y).astype(BF16)
            gc[pl.ds(at_i, BLK), :] = gr.astype(BF16)
            return carry

        lax.fori_loop(0, (count + BLK - 1) // BLK, tile_body, 0)
        for copy in olds():
            copy.wait()
        for k in range(n_ff):
            if chained:
                win[k] = (acc_i[k] + old_i[k].astype(F32)).astype(BF16)
                wdn[k] = (acc_d[k] + old_d[k].astype(F32)).astype(BF16)
            else:
                win[k] = acc_i[k].astype(BF16)
                wdn[k] = acc_d[k].astype(BF16)
        for copy in saves():
            copy.start()

    @pl.when(step > n_steps)
    def _():
        for b in range(sub):
            place = slice(b * BLK, (b + 1) * BLK)
            block = (step - n_steps - 1) * sub + b
            expand_block(scal_ref, block, rank_ref[b], gc, gr_out, place)

    @pl.when(step == 2 * n_steps)
    def _():
        for copy in saves():
            copy.wait()


def run_experts(x, gc, oc, rank, scal, router, win, wdn, first, old):
    n_blk = rank.shape[0]
    sub = min(SUB, n_blk)
    n_steps = n_blk // sub
    width = x.shape[1]
    n_ff = len(win)
    rows = gc.shape[0]
    n_old = n_ff if old else 1

    def source(s, sc):
        return (first // sub + jnp.minimum(s, n_steps - 1), 0)

    def dest(s, sc):
        return (jnp.maximum(s - n_steps - 1, 0), 0)

    def either(s, sc):
        return (jnp.where(s > n_steps, s - n_steps - 1, jnp.minimum(s, n_steps - 1)), 0, 0)

    hbm = pl.BlockSpec(memory_space=pl.ANY)
    out = pl.pallas_call(
        partial(experts_kernel, n_blk=n_blk, n_ff=n_ff, sub=sub, chained=bool(old)),
        name="experts",
        cost_estimate=cost(40),
        grid_spec=pltpu.PrefetchScalarGridSpec(
            num_scalar_prefetch=1,
            grid=(2 * n_steps + 1,),
            in_specs=[
                pl.BlockSpec((sub * BLK, width), source),
                pl.BlockSpec((sub, 1, BLK), either),
                pl.BlockSpec((width, 128), lambda s, sc: (0, 0)),
                pl.BlockSpec((rows, 1), lambda s, sc: (0, 0)),
                hbm,
            ]
            + [hbm] * (2 * n_ff + len(old)),
            out_specs=[
                pl.BlockSpec((sub * BLK, width), dest),
                hbm,
                pl.BlockSpec((128, width), lambda s, sc: (0, 0)),
            ]
            + [hbm] * (2 * n_ff),
            scratch_shapes=[
                pltpu.VMEM((rows, width), BF16),
                pltpu.VMEM((rows, width), BF16),
                pltpu.VMEM((n_ff, width, width), BF16),
                pltpu.VMEM((n_ff, width, width), BF16),
                pltpu.VMEM((n_ff, width, width), F32),
                pltpu.VMEM((n_ff, width, width), F32),
                pltpu.VMEM((BLK, width), F32),
                pltpu.VMEM((BLK, width), F32),
                pltpu.VMEM((2, BLK, width), F32),
                pltpu.VMEM((2, BLK, width), F32),
                pltpu.SemaphoreType.DMA((4 * n_ff + 1,)),
                pltpu.VMEM((n_old, width, width) if old else (1, 8, 128), BF16),
                pltpu.VMEM((n_old, width, width) if old else (1, 8, 128), BF16),
            ],
        ),
        out_shape=[
            jax.ShapeDtypeStruct((n_blk * BLK, width), BF16),
            jax.ShapeDtypeStruct((rows, width), BF16),
            jax.ShapeDtypeStruct((128, width), F32),
        ]
        + [jax.ShapeDtypeStruct((width, width), BF16)] * (2 * n_ff),
        compiler_params=pltpu.CompilerParams(vmem_limit_bytes=62 * 1024 * 1024),
    )(scal, x, rank, router, oc, gc, *win, *wdn, *old)
    return out[0], out[1], out[2], list(out[3:])


def rms_back(values, inverse, gain_vec, grad_rows):
    scaled = gain_vec * grad_rows
    return inverse * scaled - values * inverse**3 * jnp.mean(values * scaled, axis=1, keepdims=True)


def after(value, *others):
    return lax.optimization_barrier((value,) + others)[0]


def pad_rows(value, rows):
    return jnp.concatenate(
        [value, jnp.zeros((rows - value.shape[0], value.shape[1]), value.dtype)], axis=0
    )


def round_up(n, m):
    return -(-n // m) * m


def reduce_z(value, *ready):
    n = lax.axis_size("dp")
    if n > 4:
        total = lax.psum(value, "dp")
        return total, total
    at = lax.axis_index("dp")
    parts = value.reshape(n, -1, value.shape[1])

    def pick(k):
        return lax.dynamic_index_in_dim(parts, (at + k) % n, 0, keepdims=False)

    def shift(v, k):
        return lax.ppermute(v, "dp", [(i, (i + k) % n) for i in range(n)])

    total = pick(0).astype(F32)
    for arrived in [shift(pick(k), k) for k in range(1, n)]:
        total = total + arrived.astype(F32)
    total = after(total.astype(BF16), *ready)
    pieces = [total] + [shift(total, k) for k in range(1, n)]
    rows = []
    for j in range(n):
        row = pieces[0]
        for k in range(1, n):
            row = jnp.where((at - k) % n == j, pieces[k], row)
        rows.append(row)
    return jnp.concatenate(rows, axis=0), total


def local(
    tokens_in,
    gain_attn,
    w_qkv,
    w_out,
    rel_table,
    gain_moe,
    w_router,
    w_in,
    w_down,
    grad_out,
    routes,
    segments,
    rel_buckets,
):
    row_count = lax.axis_size("row")
    n_groups = lax.axis_size("dp") * lax.axis_size("col")
    tok_dev, width = tokens_in.shape
    tok_group = tok_dev * row_count
    n_experts = w_router.shape[1]
    capacity = 4 * tok_group // n_experts
    heads_here = w_qkv.shape[1]
    head_size = w_qkv.shape[2] // 3
    n_seqs = tok_group // SEQ
    assert row_count == 4 and n_seqs == 2 and n_experts == n_groups
    heads = 2 * heads_here
    row = lax.axis_index("row")
    col = lax.axis_index("col")
    member = row % 2
    first_half = member == 0

    def swap(value, mask):
        return lax.ppermute(value, "row", [(i, i ^ mask) for i in range(row_count)])

    def swap_col(value):
        return lax.ppermute(value, "col", [(0, 1), (1, 0)])

    def in_order(own, theirs):
        return jnp.where(
            first_half,
            jnp.concatenate([own, theirs], axis=0),
            jnp.concatenate([theirs, own], axis=0),
        )

    def half(value, which):
        return lax.dynamic_slice_in_dim(value, which * tok_dev, tok_dev, 0)

    tokens_f = tokens_in.astype(F32)
    inverse_one = lax.rsqrt(jnp.mean(tokens_f * tokens_f, axis=1, keepdims=True) + EPSILON)
    normed_one = (tokens_f * inverse_one * gain_attn).astype(BF16)
    qkv_mine = w_qkv.reshape(width, -1)
    qkv_cols = qkv_mine.shape[1]
    qkv_other = swap(qkv_mine, 2)
    normed_other = swap(normed_one, 1)
    table_other = swap(rel_table, 2)

    routes_mine = lax.dynamic_slice_in_dim(routes, row * tok_dev, tok_dev, 0).T
    route_len = round_up(2 * tok_dev, PAD * width)
    routes_row = jnp.concatenate(
        [routes_mine.reshape(-1), jnp.zeros((route_len - 2 * tok_dev,), jnp.int32)]
    )
    grad_ext = jnp.concatenate([grad_out, routes_row.astype(BF16).reshape(-1, width)], axis=0)
    grad_all = lax.all_gather(grad_ext, ("dp", "col"), axis=0, tiled=False)

    normed_seq = in_order(normed_one, normed_other)
    qkv_both = jnp.concatenate([qkv_mine, qkv_other], axis=1)
    packed = jnp.dot(normed_seq, qkv_both, preferred_element_type=F32).astype(BF16)

    w_in_mine, w_down_mine, w_out_mine = (
        after(w, normed_other, qkv_other) for w in (w_in[0], w_down[0], w_out)
    )
    wo_x = swap(w_out_mine, 1)
    wo_y = swap(w_out_mine, 2)
    wo_d = swap(wo_x, 2)
    w_out_all = jnp.concatenate([w_out_mine, wo_y, wo_x, wo_d], axis=0)
    wi_x = swap(w_in_mine, 1)
    wd_y = swap(w_down_mine, 2)
    wi_y = swap(w_in_mine, 2)
    wd_x = swap(w_down_mine, 1)
    wi_d = swap(wi_x, 2)
    wd_d = swap(wd_y, 1)
    win_parts = [w_in_mine, wi_y, wi_x, wi_d]
    wdn_parts = [w_down_mine, wd_y, wd_x, wd_d]

    n_blocks = SEQ // BLK
    padded = jnp.concatenate(
        [jnp.full((BLK,), -1, jnp.int32), rel_buckets, rel_buckets[SEQ - 1 :]]
    )
    flipped = padded[::-1]
    pieces = []
    for t in range(n_blocks):
        begin = SEQ - (t + 1) * BLK
        piece = flipped[begin : begin + 2 * BLK]
        pieces += [piece[BLK:], piece[:BLK]]
    bucket_seq = jnp.concatenate(pieces)
    n_buckets = rel_table.shape[0]
    bucket_hot = (
        jnp.arange(n_buckets, dtype=jnp.int32)[:, None] == bucket_seq[None, :]
    ).astype(F32)
    table_both = jnp.concatenate([rel_table, table_other], axis=1)
    ext = jnp.dot(table_both.T, bucket_hot, precision=lax.Precision.HIGHEST)
    ext = jnp.where(bucket_seq[None, :] < 0, MASKED, ext).reshape(heads, n_blocks, 2 * BLK)
    segment_ids = lax.dynamic_slice_in_dim(segments, (row // 2) * SEQ, SEQ, 0)

    mixed, probs = attention_forward(packed, ext, segment_ids, heads, head_size)
    mixed = after(mixed, wi_x, wd_y)
    mixed_mine = half(mixed, member)
    mixed_theirs = swap(half(mixed, 1 - member), 1)
    mixed_all = jnp.concatenate([mixed_mine, mixed_theirs], axis=1)
    attention = jnp.dot(mixed_all, w_out_all, preferred_element_type=F32)
    hidden_one = tokens_f + attention
    inverse_two = lax.rsqrt(jnp.mean(hidden_one * hidden_one, axis=1, keepdims=True) + EPSILON)
    normed_two = (hidden_one * inverse_two * gain_moe).astype(BF16)
    n_parts = tok_dev // BLK
    normed_all = []
    for c in range(n_parts):
        piece = normed_two[c * BLK : (c + 1) * BLK]
        normed_all.append(piece)

    me = lax.axis_index("dp") * lax.axis_size("col") + col
    routes_all = (
        grad_all[:, tok_dev:]
        .reshape(n_groups, -1)[:, : 2 * tok_dev]
        .astype(jnp.int32)
        .reshape(n_groups, 2, n_parts, BLK)
    )
    hit = routes_all == me
    mine = hit[:, 0] | hit[:, 1]
    other = jnp.sum(jnp.where(hit, 0, routes_all), axis=1).astype(F32)
    before = (
        jnp.arange(BLK, dtype=jnp.int32)[:, None] < jnp.arange(BLK, dtype=jnp.int32)[None, :]
    ).astype(BF16)
    place = jnp.dot(
        mine.reshape(-1, BLK).astype(BF16), before, preferred_element_type=F32
    ).astype(jnp.int32).reshape(mine.shape)
    totals = jnp.sum(mine.astype(jnp.int32), axis=2)

    router_pad = jnp.concatenate(
        [w_router, jnp.zeros((width, 128 - n_experts), BF16)], axis=1
    )
    max_group = min(BLK, capacity)
    chunk = min(n_groups, 2048 // max_group)
    rows = chunk * max_group + WIN + PAD
    index = jnp.arange(chunk + 1, dtype=jnp.int32)
    plans = []
    for c in range(n_parts):
        for g0 in range(0, n_groups, chunk):
            tot = totals[g0 : g0 + chunk, c]
            starts = jnp.sum(
                jnp.where(index[None, :chunk] < index[:, None], tot[None, :], 0), axis=1
            )
            rank = jnp.where(
                mine[g0 : g0 + chunk, c],
                place[g0 : g0 + chunk, c] + starts[:chunk, None],
                -1,
            ).reshape(-1, 1, BLK)
            scal = jnp.concatenate([starts, me[None].astype(jnp.int32)])
            others = other[g0 : g0 + chunk, c].reshape(-1, 1, BLK)
            grad_src = after(grad_all, wi_y, wd_x) if c else grad_all
            gc, oc = run_compact(grad_src, rank, others, scal, rows, c, g0)
            plans.append((c, g0, rank, scal, gc, oc))
    for c in range(n_parts):
        if c:
            piece = after(normed_all[c], wi_y, wd_x, *[p[4] for p in plans if p[0] == c - 1])
        else:
            piece = after(normed_all[c], grad_all)
        normed_all[c] = lax.all_gather(piece, ("dp", "col"), axis=0, tiled=True)
    grad_parts = [[] for unused in range(n_parts)]
    y_parts = [[] for unused in range(n_parts)]
    weight_grads = []
    grt = 0.0
    last_gc = plans[-1][4]
    for c, g0, rank, scal, gc, oc in plans:
        gr, yc, grt_part, weight_grads = run_experts(
            normed_all[c], gc, after(oc, last_gc), rank, scal, router_pad,
            win_parts, wdn_parts, g0, weight_grads,
        )
        grad_parts[c].append(gr)
        y_parts[c].append((yc, rank, scal))
        grt = grt + grt_part

    def scatter(value):
        return lax.psum_scatter(value, ("dp", "col"), scatter_dimension=0, tiled=True)

    def join(values):
        return values[0] if len(values) == 1 else jnp.concatenate(values, axis=0)

    grad_two = jnp.concatenate([scatter(join(g)) for g in grad_parts], axis=0)
    last = grad_parts[-1][-1]
    y_all = join(
        [
            run_expand([(after(y[at][0], last),) + y[at][1:] for y in y_parts])
            for at in range(n_groups // chunk)
        ]
    ).reshape(-1, width)

    gwi, gwd = weight_grads[:row_count], weight_grads[row_count:]
    gi_x, gi_d = swap(gwi[2], 1), swap(gwi[3], 1)
    gd_y, gd_d = swap(gwd[1], 2), swap(gwd[3], 2)
    gi_two = (gwi[1].astype(F32) + gi_d.astype(F32)).astype(BF16)
    gd_two = (gwd[2].astype(F32) + gd_d.astype(F32)).astype(BF16)
    grad_two = after(grad_two, gi_x, gi_two, gd_y, gd_two, y_all).astype(F32)

    cotangent = grad_out.astype(F32)
    grad_gain_moe = jnp.sum(grad_two * (hidden_one * inverse_two), axis=0)
    grad_hidden = cotangent + rms_back(hidden_one, inverse_two, gain_moe, grad_two)
    grad_attn = grad_hidden.astype(BF16)
    grad_mixed = dot_nt(grad_attn, w_out_all).astype(BF16)
    half_cols = heads * head_size
    gm_theirs = swap(grad_mixed[:, half_cols:], 1)
    out_rows = w_out.shape[0]
    small = jnp.concatenate([grt[:n_experts], grad_gain_moe[None]], axis=0)
    early_rows = round_up(out_rows + small.shape[0], 32)
    gwo = dot_tn(mixed_all, grad_attn)
    early_parts = [
        pad_rows(
            jnp.concatenate([gwo[k * out_rows : (k + 1) * out_rows], small], axis=0), early_rows
        ).astype(BF16)
        for k in range(row_count)
    ]
    gm_theirs = after(gm_theirs, *early_parts)
    gm_seq = in_order(grad_mixed[:, :half_cols], gm_theirs)
    mixture = scatter(after(y_all, gm_seq))
    grad_packed, diag = attention_backward(packed, probs, gm_seq, heads, head_size)

    early_sent = [swap(early_parts[k], m) for k, m in ((1, 2), (2, 1), (3, 3))]
    grad_packed, diag = lax.optimization_barrier(
        (grad_packed, diag, *early_sent)
    )[:2]
    early = early_parts[0].astype(F32) + sum(e.astype(F32) for e in early_sent)

    def keep_half(value):
        parts = value.reshape(2, -1, width)
        sent = swap_col(lax.dynamic_index_in_dim(parts, 1 - col, 0, keepdims=False).astype(BF16))
        kept = lax.dynamic_index_in_dim(parts, col, 0, keepdims=False)
        return kept.astype(F32) + sent.astype(F32)

    early_half = keep_half(early)

    one_theirs = swap(dot_nt(half(grad_packed, 1 - member), qkv_both).astype(BF16), 1)
    gq = dot_tn(grad_packed, normed_seq)
    gain_part = jnp.sum(gq * qkv_both.T.astype(F32), axis=0) / gain_attn
    table_grad = jnp.dot(
        bucket_hot, diag.reshape(heads, -1).T, precision=lax.Precision.HIGHEST
    )
    late_rows = round_up(qkv_cols + 2, 32)

    def late_block(which, gain):
        cols = table_grad[:, which * heads_here : (which + 1) * heads_here].reshape(1, -1)
        table_row = jnp.concatenate(
            [cols, jnp.zeros((1, width - cols.shape[1]), F32)], axis=1
        )
        block = gq[which * qkv_cols : (which + 1) * qkv_cols]
        return pad_rows(jnp.concatenate([block, gain[None], table_row], axis=0), late_rows)

    late_own = late_block(0, gain_part)
    late_other = late_block(1, gain_part)
    both_half = keep_half(
        jnp.stack([late_own.reshape(2, -1, width), late_other.reshape(2, -1, width)], axis=1)
    ).reshape(2, -1, width)
    late_half = both_half[0] + swap(both_half[1].astype(BF16), 2).astype(F32)
    late_n, early_n = late_half.shape[0], early_half.shape[0]

    gi_y = swap(after(gi_two, late_half), 2)
    gd_x = swap(after(gd_two, late_half), 1)
    mixture = after(mixture, both_half)
    block_out = (hidden_one + mixture.astype(F32)).astype(BF16)
    total_rows = round_up(late_n + early_n, 16 * 4)
    summed, arrived_z = reduce_z(
        pad_rows(jnp.concatenate([late_half, early_half], axis=0).astype(BF16), total_rows),
        gi_y,
        gd_x,
        block_out,
    )
    one_theirs = after(one_theirs, arrived_z)
    grad_one = dot_nt(half(grad_packed, member), qkv_both) + one_theirs.astype(F32)
    grad_input = (grad_hidden + rms_back(tokens_f, inverse_one, gain_attn, grad_one)).astype(BF16)
    grad_w_in = (gwi[0].astype(F32) + gi_x.astype(F32) + gi_y.astype(F32))[None]
    grad_w_down = (gwd[0].astype(F32) + gd_y.astype(F32) + gd_x.astype(F32))[None]
    summed = after(summed, grad_w_in, grad_w_down, grad_input)
    theirs = swap_col(summed)
    low = jnp.where(col == 0, summed, theirs)
    high = jnp.where(col == 0, theirs, summed)
    late = jnp.concatenate([low[:late_n], high[:late_n]], axis=0).astype(F32)
    early = jnp.concatenate(
        [low[late_n : late_n + early_n], high[late_n : late_n + early_n]], axis=0
    ).astype(F32)
    gain_row = late[qkv_cols]
    slice_n = width // row_count
    gain_slice = lax.dynamic_slice_in_dim(gain_row, row * slice_n, slice_n, 0) + swap(
        lax.dynamic_slice_in_dim(gain_row, (row ^ 1) * slice_n, slice_n, 0), 1
    )
    grad_table = late[qkv_cols + 1, : n_buckets * heads_here].reshape(n_buckets, heads_here)
    return (
        block_out,
        grad_input,
        gain_slice,
        late[:qkv_cols].T.reshape(w_qkv.shape),
        early[:out_rows],
        grad_table,
        early[out_rows + n_experts],
        early[out_rows : out_rows + n_experts].T,
        grad_w_in,
        grad_w_down,
    )


def solution(mesh):
    placed = (
        P(("dp", "col", "row"), None),
        P(),
        P(None, "row", None),
        P("row", None),
        P(None, "row"),
        P(),
        P(),
        P(("dp", "col"), None, "row"),
        P(("dp", "col"), "row", None),
        P(("dp", "col", "row"), None),
        P(("dp", "col"), None),
        P(("dp", "col")),
        P(),
    )
    return jax.shard_map(
        local,
        mesh=mesh,
        in_specs=placed,
        out_specs=(
            P(("dp", "col", "row"), None),
            P(("dp", "col", "row"), None),
            P("row"),
            P(None, "row", None),
            P("row", None),
            P(None, "row"),
            P(),
            P(),
            P(("dp", "col"), None, "row"),
            P(("dp", "col"), "row", None),
        ),
        check_vma=False,
    )
```

```python
from functools import partial

import jax
import jax.numpy as jnp
from jax import lax
from jax.experimental import pallas as pl
from jax.experimental.pallas import tpu as pltpu
from jax.sharding import PartitionSpec as P

SEQ = 1024
EPSILON = 1e-06
MASKED = -1e30
BLK = 256
PAD = 16
WIN = BLK + PAD
STEP = 160
PIECE = STEP + PAD
SUB = 4
F32 = jnp.float32
BF16 = jnp.bfloat16
GELU_C = 0.7978845608028654
GELU_A = 0.044715


def dot_nn(a, b):
    return lax.dot_general(a, b, (((1,), (0,)), ((), ())), preferred_element_type=F32)


def dot_nt(a, b):
    return lax.dot_general(a, b, (((1,), (1,)), ((), ())), preferred_element_type=F32)


def dot_tn(a, b):
    return lax.dot_general(a, b, (((0,), (0,)), ((), ())), preferred_element_type=F32)


def cost(micros):
    return pl.CostEstimate(flops=int(micros * 1e9), bytes_accessed=1 << 20, transcendentals=0)


def attn_fwd_kernel(packed_ref, ext_ref, segr_ref, segc_ref, mixed_ref, probs_ref, tile_ref, *, head_size):
    n_blocks = SEQ // BLK
    for hh in range(2):
        base = hh * 3 * head_size
        scale = jnp.asarray(head_size ** (-0.5), BF16)
        q_all = packed_ref[:, base : base + head_size] * scale
        k_all = packed_ref[:, base + head_size : base + 2 * head_size]
        v_all = packed_ref[:, base + 2 * head_size : base + 3 * head_size]
        for t in range(n_blocks):
            rows = jnp.broadcast_to(ext_ref[hh, t : t + 1, :], (BLK, 2 * BLK))
            tile_ref[t] = pltpu.roll(rows, 0, 1, stride=1, stride_axis=0)[:, :BLK]
        for qb in range(n_blocks):
            width = (qb + 1) * BLK
            rows = slice(qb * BLK, (qb + 1) * BLK)
            scores = dot_nt(q_all[rows], k_all[:width])
            bias = jnp.concatenate([tile_ref[qb - kb] for kb in range(qb + 1)], axis=1)
            same = segc_ref[rows, :] == segr_ref[:, :width]
            scores = jnp.where(same, scores + bias, MASKED)
            peak = jnp.max(scores, axis=1, keepdims=True)
            exp_rows = jnp.exp(scores - peak)
            total = jnp.sum(exp_rows, axis=1, keepdims=True)
            probs = (exp_rows * (1.0 / total)).astype(BF16)
            probs_ref[hh, rows, :width] = probs
            mixed_ref[rows, hh * head_size : (hh + 1) * head_size] = dot_nn(
                probs, v_all[:width]
            ).astype(BF16)


def attn_bwd_kernel(
    packed_ref, probs_ref, grad_ref, out_ref, diag_ref, dk_ref, dv_ref, tile_ref, *, head_size
):
    n_blocks = SEQ // BLK
    for hh in range(2):
        base = hh * 3 * head_size
        scale = jnp.asarray(head_size ** (-0.5), BF16)
        q_all = packed_ref[:, base : base + head_size] * scale
        k_all = packed_ref[:, base + head_size : base + 2 * head_size]
        v_all = packed_ref[:, base + 2 * head_size : base + 3 * head_size]
        g_all = grad_ref[:, hh * head_size : (hh + 1) * head_size]
        for qb in reversed(range(n_blocks)):
            width = (qb + 1) * BLK
            rows = slice(qb * BLK, (qb + 1) * BLK)
            probs_b = probs_ref[hh, rows, :width]
            probs = probs_b.astype(F32)
            grad_probs = dot_nt(g_all[rows], v_all[:width])
            delta = jnp.sum(probs * grad_probs, axis=1, keepdims=True)
            grad_scores = probs * (grad_probs - delta)
            scores_b = grad_scores.astype(BF16)
            dq = dot_nn(scores_b, k_all[:width]) * (head_size ** (-0.5))
            out_ref[rows, base : base + head_size] = dq.astype(BF16)
            dk = dot_tn(scores_b, q_all[rows])
            dv = dot_tn(probs_b, g_all[rows])
            if qb == n_blocks - 1:
                dk_ref[...] = dk
                dv_ref[...] = dv
            else:
                dk_ref[:width, :] += dk
                dv_ref[:width, :] += dv
            for kb in range(qb + 1):
                part = grad_scores[:, kb * BLK : (kb + 1) * BLK]
                if qb == n_blocks - 1:
                    tile_ref[qb - kb] = part
                else:
                    tile_ref[qb - kb] += part
        out_ref[:, base + head_size : base + 2 * head_size] = dk_ref[...].astype(BF16)
        out_ref[:, base + 2 * head_size : base + 3 * head_size] = dv_ref[...].astype(BF16)
        for t in range(n_blocks):
            left = tile_ref[t]
            fold = jnp.concatenate([left, jnp.zeros_like(left)], axis=1)
            n = BLK
            while n > 1:
                n //= 2
                fold = fold[:n] + pltpu.roll(fold[n:], 2 * BLK - n, 1)
            diag_ref[hh, t : t + 1, :] = fold


def attention_forward(packed, ext, seg, heads, head_size):
    n_blocks = SEQ // BLK
    return pl.pallas_call(
        partial(attn_fwd_kernel, head_size=head_size),
        name="attn_fwd",
        cost_estimate=cost(20),
        grid=(heads // 2,),
        in_specs=[
            pl.BlockSpec((SEQ, 6 * head_size), lambda p: (0, p)),
            pl.BlockSpec((2, n_blocks, 2 * BLK), lambda p: (p, 0, 0)),
            pl.BlockSpec((1, SEQ), lambda p: (0, 0)),
            pl.BlockSpec((SEQ, 1), lambda p: (0, 0)),
        ],
        out_specs=[
            pl.BlockSpec((SEQ, 2 * head_size), lambda p: (0, p)),
            pl.BlockSpec((2, SEQ, SEQ), lambda p: (p, 0, 0)),
        ],
        out_shape=[
            jax.ShapeDtypeStruct((SEQ, heads * head_size), BF16),
            jax.ShapeDtypeStruct((heads, SEQ, SEQ), BF16),
        ],
        scratch_shapes=[pltpu.VMEM((n_blocks, BLK, BLK), F32)],
    )(packed, ext, seg.reshape(1, SEQ), seg.reshape(SEQ, 1))


def attention_backward(packed, probs, grad_mixed, heads, head_size):
    n_blocks = SEQ // BLK
    return pl.pallas_call(
        partial(attn_bwd_kernel, head_size=head_size),
        name="attn_bwd",
        cost_estimate=cost(27),
        grid=(heads // 2,),
        in_specs=[
            pl.BlockSpec((SEQ, 6 * head_size), lambda p: (0, p)),
            pl.BlockSpec((2, SEQ, SEQ), lambda p: (p, 0, 0)),
            pl.BlockSpec((SEQ, 2 * head_size), lambda p: (0, p)),
        ],
        out_specs=[
            pl.BlockSpec((SEQ, 6 * head_size), lambda p: (0, p)),
            pl.BlockSpec((2, n_blocks, 2 * BLK), lambda p: (p, 0, 0)),
        ],
        out_shape=[
            jax.ShapeDtypeStruct((SEQ, heads * 3 * head_size), BF16),
            jax.ShapeDtypeStruct((heads, n_blocks, 2 * BLK), F32),
        ],
        scratch_shapes=[
            pltpu.VMEM((SEQ, head_size), F32),
            pltpu.VMEM((SEQ, head_size), F32),
            pltpu.VMEM((n_blocks, BLK, BLK), F32),
        ],
    )(packed, probs, grad_mixed)


def window(start):
    return pl.multiple_of((start // PAD) * PAD, PAD)


def hot_rows(rank_row, at, rows):
    return rank_row == (lax.broadcasted_iota(jnp.int32, (rows, BLK), 0) + at)


def n_pieces(scal_ref, block):
    return (scal_ref[block + 1] - scal_ref[block] + STEP - 1) // STEP


def compact_block(scal_ref, block, rank_row, source, dest):
    start = scal_ref[block]

    def piece(j, carry):
        first = start + j * STEP
        at = window(first)
        keep = lax.broadcasted_iota(jnp.int32, (PAD, 1), 0) < (first - at)
        pick = jnp.where(hot_rows(rank_row, at, PIECE), 1.0, 0.0).astype(BF16)
        rows = dot_nn(pick, source).astype(BF16)
        dest[pl.ds(at, PAD), :] = jnp.where(keep, dest[pl.ds(at, PAD), :], rows[:PAD])
        dest[pl.ds(at + PAD, STEP), :] = rows[PAD:]
        return carry

    piece(0, 0)
    lax.fori_loop(1, n_pieces(scal_ref, block), piece, 0)


def compact_end(count, dest):
    at = window(count)
    keep = lax.broadcasted_iota(jnp.int32, (WIN, 1), 0) < (count - at)
    old = dest[pl.ds(at, WIN), :]
    dest[pl.ds(at, WIN), :] = jnp.where(keep, old, jnp.zeros((), old.dtype))


def expand_block(scal_ref, block, rank_row, source, dest, place):
    start = scal_ref[block]

    def piece(j):
        first = start + j * STEP
        at = window(first)
        inside = (rank_row >= first) & (rank_row < first + STEP)
        pick = jnp.where(hot_rows(jnp.where(inside, rank_row, -1), at, PIECE), 1.0, 0.0)
        return dot_tn(pick.astype(BF16), source[pl.ds(at, PIECE), :]).astype(BF16)

    dest[place, :] = piece(0)

    def more(j, carry):
        dest[place, :] += piece(j)
        return carry

    lax.fori_loop(1, n_pieces(scal_ref, block), more, 0)


def compact_kernel(scal_ref, g_ref, rank_ref, other_ref, gc, oc, *, n_blk, sub):
    step = pl.program_id(0)
    for b in range(sub):
        block = step * sub + b
        rank_row = rank_ref[b]
        compact_block(scal_ref, block, rank_row, g_ref[b], gc)
        start = scal_ref[block]

        def ids_piece(j, carry):
            first = start + j * STEP
            at = window(first)
            keep = lax.broadcasted_iota(jnp.int32, (PIECE, 1), 0) < (first - at)
            hot = hot_rows(rank_row, at, PIECE)
            ids = jnp.sum(jnp.where(hot, other_ref[b], 0.0), axis=1, keepdims=True)
            oc[pl.ds(at, PIECE), :] = jnp.where(keep, oc[pl.ds(at, PIECE), :], ids)
            return carry

        ids_piece(0, 0)
        lax.fori_loop(1, n_pieces(scal_ref, block), ids_piece, 0)

    @pl.when(step == n_blk // sub - 1)
    def _():
        compact_end(scal_ref[n_blk], gc)
        compact_end(scal_ref[n_blk], oc)


def run_compact(g_all, rank, other, scal, rows, part, first):
    n_blk = rank.shape[0]
    sub = min(SUB, n_blk)
    width = g_all.shape[2]
    return pl.pallas_call(
        partial(compact_kernel, n_blk=n_blk, sub=sub),
        name="compact",
        cost_estimate=cost(20 if part else 0.5),
        grid_spec=pltpu.PrefetchScalarGridSpec(
            num_scalar_prefetch=1,
            grid=(n_blk // sub,),
            in_specs=[
                pl.BlockSpec((sub, BLK, width), lambda s, sc: (first // sub + s, part, 0)),
                pl.BlockSpec((sub, 1, BLK), lambda s, sc: (s, 0, 0)),
                pl.BlockSpec((sub, 1, BLK), lambda s, sc: (s, 0, 0)),
            ],
            out_specs=[
                pl.BlockSpec((rows, width), lambda s, sc: (0, 0)),
                pl.BlockSpec((rows, 1), lambda s, sc: (0, 0)),
            ],
        ),
        out_shape=[
            jax.ShapeDtypeStruct((rows, width), BF16),
            jax.ShapeDtypeStruct((rows, 1), F32),
        ],
    )(scal, g_all, rank, other)


def expand_kernel(scal_ref, rank_ref, *refs, sub, n_blk):
    out_ref = refs[-1]
    for c in range(len(refs) - 1):

        @pl.when(pl.program_id(0) == c)
        def _():
            for b in range(sub):
                block = c * (n_blk + 2) + pl.program_id(1) * sub + b
                expand_block(scal_ref, block, rank_ref[0, b], refs[c], out_ref.at[b], slice(None))


def run_expand(parts):
    n_parts = len(parts)
    n_blk = parts[0][1].shape[0]
    sub = min(SUB, n_blk)
    rows, width = parts[0][0].shape
    return pl.pallas_call(
        partial(expand_kernel, sub=sub, n_blk=n_blk),
        name="expand",
        cost_estimate=cost(6 * n_parts),
        grid_spec=pltpu.PrefetchScalarGridSpec(
            num_scalar_prefetch=1,
            grid=(n_parts, n_blk // sub),
            in_specs=[pl.BlockSpec((1, sub, 1, BLK), lambda c, s, sc: (c, s, 0, 0))]
            + [pl.BlockSpec((rows, width), lambda c, s, sc: (0, 0))] * n_parts,
            out_specs=pl.BlockSpec((sub, BLK, width), lambda c, s, sc: (s, c, 0)),
        ),
        out_shape=jax.ShapeDtypeStruct((n_blk, n_parts * BLK, width), BF16),
    )(
        jnp.concatenate([p[2] for p in parts]),
        jnp.stack([p[1] for p in parts]),
        *[p[0] for p in parts],
    )


def experts_kernel(
    scal_ref, x_ref, rank_ref, router_ref, oc, gc_hbm, *refs, n_blk, n_ff, sub, chained
):
    win_hbm, wdn_hbm = refs[:n_ff], refs[n_ff : 2 * n_ff]
    refs = refs[2 * n_ff :]
    if chained:
        gwi_old, gwd_old = refs[:n_ff], refs[n_ff : 2 * n_ff]
        refs = refs[2 * n_ff :]
    gr_out, yc_hbm, grt_ref = refs[:3]
    gwi_hbm, gwd_hbm = refs[3 : 3 + n_ff], refs[3 + n_ff : 3 + 2 * n_ff]
    xc, gc, win, wdn, acc_i, acc_d, y_s, gr_s, pre_s, gh_s, sem, old_i, old_d = refs[
        3 + 2 * n_ff :
    ]
    step = pl.program_id(0)
    n_steps = n_blk // sub
    width = xc.shape[1]
    count = scal_ref[n_blk]
    me = scal_ref[n_blk + 1]

    def loads():
        copies = [pltpu.make_async_copy(gc_hbm, gc, sem.at[2 * n_ff])]
        for k in range(n_ff):
            copies.append(pltpu.make_async_copy(win_hbm[k], win.at[k], sem.at[k]))
            copies.append(pltpu.make_async_copy(wdn_hbm[k], wdn.at[k], sem.at[n_ff + k]))
        return copies

    def olds():
        copies = []
        for k in range(n_ff if chained else 0):
            at = 2 * n_ff + 1 + 2 * k
            copies.append(pltpu.make_async_copy(gwi_old[k], old_i.at[k], sem.at[at]))
            copies.append(pltpu.make_async_copy(gwd_old[k], old_d.at[k], sem.at[at + 1]))
        return copies

    def saves():
        copies = [pltpu.make_async_copy(xc, yc_hbm, sem.at[2 * n_ff])]
        for k in range(n_ff):
            copies.append(pltpu.make_async_copy(win.at[k], gwi_hbm[k], sem.at[k]))
            copies.append(pltpu.make_async_copy(wdn.at[k], gwd_hbm[k], sem.at[n_ff + k]))
        return copies

    @pl.when(step == 0)
    def _():
        for copy in loads():
            copy.start()
        for k in range(n_ff):
            acc_i[k] = jnp.zeros((width, width), F32)
            acc_d[k] = jnp.zeros((width, width), F32)

    @pl.when(step < n_steps)
    def _():
        for b in range(sub):
            rows = slice(b * BLK, (b + 1) * BLK)
            compact_block(scal_ref, step * sub + b, rank_ref[b], x_ref[rows, :], xc)

    @pl.when(step == n_steps)
    def _():
        compact_end(count, xc)
        grt_ref[...] = jnp.zeros(grt_ref.shape, F32)
        for copy in loads():
            copy.wait()
        for copy in olds():
            copy.start()
        lane = lax.broadcasted_iota(jnp.int32, (BLK, 128), 1)

        def tile_body(i, carry):
            at_i = pl.multiple_of(i * BLK, BLK)
            x = xc[pl.ds(at_i, BLK), :]
            g = gc[pl.ds(at_i, BLK), :]
            mine_hot = lane == me
            other_hot = lane == oc[pl.ds(at_i, BLK), :].astype(jnp.int32)
            logits = dot_nn(x, router_ref[...])
            diff = jnp.sum(
                jnp.where(mine_hot, logits, 0.0) - jnp.where(other_hot, logits, 0.0),
                axis=1,
                keepdims=True,
            )
            small = jnp.exp(-jnp.abs(diff))
            inv = 1.0 / (1.0 + small)
            gate = jnp.where(diff >= 0, inv, small * inv)
            both = small * inv * inv
            gated = (g.astype(F32) * gate).astype(BF16)

            def first_products(k):
                pre_s[k % 2] = dot_nn(x, win[k])
                gh_s[k % 2] = dot_nt(gated, wdn[k])

            first_products(0)
            for k in range(n_ff):
                if k + 1 < n_ff:
                    first_products(k + 1)
                pre = pre_s[k % 2]
                sq = pre * pre
                th = jnp.tanh(pre * (GELU_C + (GELU_C * GELU_A) * sq))
                half = 0.5 + 0.5 * th
                hid = (pre * half).astype(BF16)
                slope = half + (0.5 * pre) * (1.0 - th * th) * (
                    GELU_C + (3.0 * GELU_C * GELU_A) * sq
                )
                grad_pre = (gh_s[k % 2] * slope).astype(BF16)
                y_new = dot_nn(hid, wdn[k])
                gr_new = dot_nt(grad_pre, win[k])
                y_s[...] = y_s[...] + y_new if k else y_new
                gr_s[...] = gr_s[...] + gr_new if k else gr_new
                acc_d[k] += dot_tn(hid, gated)
                acc_i[k] += dot_tn(x, grad_pre)

            y = y_s[...]
            grad_gate = jnp.sum(g.astype(F32) * y, axis=1, keepdims=True) * both
            d_logit = jnp.where(mine_hot, grad_gate, 0.0) - jnp.where(other_hot, grad_gate, 0.0)
            d_high = d_logit.astype(BF16)
            d_low = (d_logit - d_high.astype(F32)).astype(BF16)
            router = router_ref[...]
            grt_ref[...] += dot_tn(d_high, x) + dot_tn(d_low, x)
            gr = gr_s[...] + (dot_nt(d_high, router) + dot_nt(d_low, router))
            xc[pl.ds(at_i, BLK), :] = (gate * y).astype(BF16)
            gc[pl.ds(at_i, BLK), :] = gr.astype(BF16)
            return carry

        lax.fori_loop(0, (count + BLK - 1) // BLK, tile_body, 0)
        for copy in olds():
            copy.wait()
        for k in range(n_ff):
            if chained:
                win[k] = (acc_i[k] + old_i[k].astype(F32)).astype(BF16)
                wdn[k] = (acc_d[k] + old_d[k].astype(F32)).astype(BF16)
            else:
                win[k] = acc_i[k].astype(BF16)
                wdn[k] = acc_d[k].astype(BF16)
        for copy in saves():
            copy.start()

    @pl.when(step > n_steps)
    def _():
        for b in range(sub):
            place = slice(b * BLK, (b + 1) * BLK)
            block = (step - n_steps - 1) * sub + b
            expand_block(scal_ref, block, rank_ref[b], gc, gr_out, place)

    @pl.when(step == 2 * n_steps)
    def _():
        for copy in saves():
            copy.wait()


def run_experts(x, gc, oc, rank, scal, router, win, wdn, first, old):
    n_blk = rank.shape[0]
    sub = min(SUB, n_blk)
    n_steps = n_blk // sub
    width = x.shape[1]
    n_ff = len(win)
    rows = gc.shape[0]
    n_old = n_ff if old else 1

    def source(s, sc):
        return (first // sub + jnp.minimum(s, n_steps - 1), 0)

    def dest(s, sc):
        return (jnp.maximum(s - n_steps - 1, 0), 0)

    def either(s, sc):
        return (jnp.where(s > n_steps, s - n_steps - 1, jnp.minimum(s, n_steps - 1)), 0, 0)

    hbm = pl.BlockSpec(memory_space=pl.ANY)
    out = pl.pallas_call(
        partial(experts_kernel, n_blk=n_blk, n_ff=n_ff, sub=sub, chained=bool(old)),
        name="experts",
        cost_estimate=cost(40),
        grid_spec=pltpu.PrefetchScalarGridSpec(
            num_scalar_prefetch=1,
            grid=(2 * n_steps + 1,),
            in_specs=[
                pl.BlockSpec((sub * BLK, width), source),
                pl.BlockSpec((sub, 1, BLK), either),
                pl.BlockSpec((width, 128), lambda s, sc: (0, 0)),
                pl.BlockSpec((rows, 1), lambda s, sc: (0, 0)),
                hbm,
            ]
            + [hbm] * (2 * n_ff + len(old)),
            out_specs=[
                pl.BlockSpec((sub * BLK, width), dest),
                hbm,
                pl.BlockSpec((128, width), lambda s, sc: (0, 0)),
            ]
            + [hbm] * (2 * n_ff),
            scratch_shapes=[
                pltpu.VMEM((rows, width), BF16),
                pltpu.VMEM((rows, width), BF16),
                pltpu.VMEM((n_ff, width, width), BF16),
                pltpu.VMEM((n_ff, width, width), BF16),
                pltpu.VMEM((n_ff, width, width), F32),
                pltpu.VMEM((n_ff, width, width), F32),
                pltpu.VMEM((BLK, width), F32),
                pltpu.VMEM((BLK, width), F32),
                pltpu.VMEM((2, BLK, width), F32),
                pltpu.VMEM((2, BLK, width), F32),
                pltpu.SemaphoreType.DMA((4 * n_ff + 1,)),
                pltpu.VMEM((n_old, width, width) if old else (1, 8, 128), BF16),
                pltpu.VMEM((n_old, width, width) if old else (1, 8, 128), BF16),
            ],
        ),
        out_shape=[
            jax.ShapeDtypeStruct((n_blk * BLK, width), BF16),
            jax.ShapeDtypeStruct((rows, width), BF16),
            jax.ShapeDtypeStruct((128, width), F32),
        ]
        + [jax.ShapeDtypeStruct((width, width), BF16)] * (2 * n_ff),
        compiler_params=pltpu.CompilerParams(vmem_limit_bytes=62 * 1024 * 1024),
    )(scal, x, rank, router, oc, gc, *win, *wdn, *old)
    return out[0], out[1], out[2], list(out[3:])


def rms_back(values, inverse, gain_vec, grad_rows):
    scaled = gain_vec * grad_rows
    return inverse * scaled - values * inverse**3 * jnp.mean(values * scaled, axis=1, keepdims=True)


def after(value, *others):
    return lax.optimization_barrier((value,) + others)[0]


def pad_rows(value, rows):
    return jnp.concatenate(
        [value, jnp.zeros((rows - value.shape[0], value.shape[1]), value.dtype)], axis=0
    )


def round_up(n, m):
    return -(-n // m) * m


def reduce_z(value, *ready):
    n = lax.axis_size("dp")
    if n > 4:
        total = lax.psum(value, "dp")
        return total, total
    at = lax.axis_index("dp")
    parts = value.reshape(n, -1, value.shape[1])

    def pick(k):
        return lax.dynamic_index_in_dim(parts, (at + k) % n, 0, keepdims=False)

    def shift(v, k):
        return lax.ppermute(v, "dp", [(i, (i + k) % n) for i in range(n)])

    total = pick(0).astype(F32)
    for arrived in [shift(pick(k), k) for k in range(1, n)]:
        total = total + arrived.astype(F32)
    total = after(total.astype(BF16), *ready)
    pieces = [total] + [shift(total, k) for k in range(1, n)]
    rows = []
    for j in range(n):
        row = pieces[0]
        for k in range(1, n):
            row = jnp.where((at - k) % n == j, pieces[k], row)
        rows.append(row)
    return jnp.concatenate(rows, axis=0), total


def local(
    tokens_in,
    gain_attn,
    w_qkv,
    w_out,
    rel_table,
    gain_moe,
    w_router,
    w_in,
    w_down,
    grad_out,
    routes,
    segments,
    rel_buckets,
):
    row_count = lax.axis_size("row")
    n_groups = lax.axis_size("dp") * lax.axis_size("col")
    tok_dev, width = tokens_in.shape
    tok_group = tok_dev * row_count
    n_experts = w_router.shape[1]
    capacity = 4 * tok_group // n_experts
    heads_here = w_qkv.shape[1]
    head_size = w_qkv.shape[2] // 3
    n_seqs = tok_group // SEQ
    assert row_count == 4 and n_seqs == 2 and n_experts == n_groups
    heads = 2 * heads_here
    row = lax.axis_index("row")
    col = lax.axis_index("col")
    member = row % 2
    first_half = member == 0

    def swap(value, mask):
        return lax.ppermute(value, "row", [(i, i ^ mask) for i in range(row_count)])

    def swap_col(value):
        return lax.ppermute(value, "col", [(0, 1), (1, 0)])

    def in_order(own, theirs):
        return jnp.where(
            first_half,
            jnp.concatenate([own, theirs], axis=0),
            jnp.concatenate([theirs, own], axis=0),
        )

    def half(value, which):
        return lax.dynamic_slice_in_dim(value, which * tok_dev, tok_dev, 0)

    tokens_f = tokens_in.astype(F32)
    inverse_one = lax.rsqrt(jnp.mean(tokens_f * tokens_f, axis=1, keepdims=True) + EPSILON)
    normed_one = (tokens_f * inverse_one * gain_attn).astype(BF16)
    qkv_mine = w_qkv.reshape(width, -1)
    qkv_cols = qkv_mine.shape[1]
    qkv_other = swap(qkv_mine, 2)
    normed_other = swap(normed_one, 1)
    table_other = swap(rel_table, 2)

    routes_mine = lax.dynamic_slice_in_dim(routes, row * tok_dev, tok_dev, 0).T
    route_len = round_up(2 * tok_dev, PAD * width)
    routes_row = jnp.concatenate(
        [routes_mine.reshape(-1), jnp.zeros((route_len - 2 * tok_dev,), jnp.int32)]
    )
    grad_ext = jnp.concatenate([grad_out, routes_row.astype(BF16).reshape(-1, width)], axis=0)
    grad_all = lax.all_gather(grad_ext, ("dp", "col"), axis=0, tiled=False)

    normed_seq = in_order(normed_one, normed_other)
    qkv_both = jnp.concatenate([qkv_mine, qkv_other], axis=1)
    packed = jnp.dot(normed_seq, qkv_both, preferred_element_type=F32).astype(BF16)

    w_in_mine, w_down_mine, w_out_mine = (
        after(w, normed_other, qkv_other) for w in (w_in[0], w_down[0], w_out)
    )
    wo_x = swap(w_out_mine, 1)
    wo_y = swap(w_out_mine, 2)
    wo_d = swap(wo_x, 2)
    w_out_all = jnp.concatenate([w_out_mine, wo_y, wo_x, wo_d], axis=0)
    wi_x = swap(w_in_mine, 1)
    wd_y = swap(w_down_mine, 2)
    wi_y = swap(w_in_mine, 2)
    wd_x = swap(w_down_mine, 1)
    wi_d = swap(wi_x, 2)
    wd_d = swap(wd_y, 1)
    win_parts = [w_in_mine, wi_y, wi_x, wi_d]
    wdn_parts = [w_down_mine, wd_y, wd_x, wd_d]

    n_blocks = SEQ // BLK
    padded = jnp.concatenate(
        [jnp.full((BLK,), -1, jnp.int32), rel_buckets, rel_buckets[SEQ - 1 :]]
    )
    flipped = padded[::-1]
    pieces = []
    for t in range(n_blocks):
        begin = SEQ - (t + 1) * BLK
        piece = flipped[begin : begin + 2 * BLK]
        pieces += [piece[BLK:], piece[:BLK]]
    bucket_seq = jnp.concatenate(pieces)
    n_buckets = rel_table.shape[0]
    bucket_hot = (
        jnp.arange(n_buckets, dtype=jnp.int32)[:, None] == bucket_seq[None, :]
    ).astype(F32)
    table_both = jnp.concatenate([rel_table, table_other], axis=1)
    ext = jnp.dot(table_both.T, bucket_hot, precision=lax.Precision.HIGHEST)
    ext = jnp.where(bucket_seq[None, :] < 0, MASKED, ext).reshape(heads, n_blocks, 2 * BLK)
    segment_ids = lax.dynamic_slice_in_dim(segments, (row // 2) * SEQ, SEQ, 0)

    mixed, probs = attention_forward(packed, ext, segment_ids, heads, head_size)
    mixed = after(mixed, wi_x, wd_y)
    mixed_mine = half(mixed, member)
    mixed_theirs = swap(half(mixed, 1 - member), 1)
    mixed_all = jnp.concatenate([mixed_mine, mixed_theirs], axis=1)
    attention = jnp.dot(mixed_all, w_out_all, preferred_element_type=F32)
    hidden_one = tokens_f + attention
    inverse_two = lax.rsqrt(jnp.mean(hidden_one * hidden_one, axis=1, keepdims=True) + EPSILON)
    normed_two = (hidden_one * inverse_two * gain_moe).astype(BF16)
    n_parts = tok_dev // BLK
    normed_all = []
    for c in range(n_parts):
        piece = normed_two[c * BLK : (c + 1) * BLK]
        normed_all.append(piece)

    me = lax.axis_index("dp") * lax.axis_size("col") + col
    routes_all = (
        grad_all[:, tok_dev:]
        .reshape(n_groups, -1)[:, : 2 * tok_dev]
        .astype(jnp.int32)
        .reshape(n_groups, 2, n_parts, BLK)
    )
    hit = routes_all == me
    mine = hit[:, 0] | hit[:, 1]
    other = jnp.sum(jnp.where(hit, 0, routes_all), axis=1).astype(F32)
    before = (
        jnp.arange(BLK, dtype=jnp.int32)[:, None] < jnp.arange(BLK, dtype=jnp.int32)[None, :]
    ).astype(BF16)
    place = jnp.dot(
        mine.reshape(-1, BLK).astype(BF16), before, preferred_element_type=F32
    ).astype(jnp.int32).reshape(mine.shape)
    totals = jnp.sum(mine.astype(jnp.int32), axis=2)

    router_pad = jnp.concatenate(
        [w_router, jnp.zeros((width, 128 - n_experts), BF16)], axis=1
    )
    max_group = min(BLK, capacity)
    chunk = min(n_groups, 2048 // max_group)
    rows = chunk * max_group + WIN + PAD
    index = jnp.arange(chunk + 1, dtype=jnp.int32)
    plans = []
    for c in range(n_parts):
        for g0 in range(0, n_groups, chunk):
            tot = totals[g0 : g0 + chunk, c]
            starts = jnp.sum(
                jnp.where(index[None, :chunk] < index[:, None], tot[None, :], 0), axis=1
            )
            rank = jnp.where(
                mine[g0 : g0 + chunk, c],
                place[g0 : g0 + chunk, c] + starts[:chunk, None],
                -1,
            ).reshape(-1, 1, BLK)
            scal = jnp.concatenate([starts, me[None].astype(jnp.int32)])
            others = other[g0 : g0 + chunk, c].reshape(-1, 1, BLK)
            grad_src = after(grad_all, wi_y, wd_x) if c else grad_all
            gc, oc = run_compact(grad_src, rank, others, scal, rows, c, g0)
            plans.append((c, g0, rank, scal, gc, oc))
    for c in range(n_parts):
        if c:
            piece = after(normed_all[c], wi_y, wd_x, *[p[4] for p in plans if p[0] == c - 1])
        else:
            piece = after(normed_all[c], grad_all)
        normed_all[c] = lax.all_gather(piece, ("dp", "col"), axis=0, tiled=True)
    grad_parts = [[] for unused in range(n_parts)]
    y_parts = [[] for unused in range(n_parts)]
    weight_grads = []
    grt = 0.0
    last_gc = plans[-1][4]
    for c, g0, rank, scal, gc, oc in plans:
        gr, yc, grt_part, weight_grads = run_experts(
            normed_all[c], gc, after(oc, last_gc), rank, scal, router_pad,
            win_parts, wdn_parts, g0, weight_grads,
        )
        grad_parts[c].append(gr)
        y_parts[c].append((yc, rank, scal))
        grt = grt + grt_part

    def scatter(value):
        return lax.psum_scatter(value, ("dp", "col"), scatter_dimension=0, tiled=True)

    def join(values):
        return values[0] if len(values) == 1 else jnp.concatenate(values, axis=0)

    grad_two = jnp.concatenate([scatter(join(g)) for g in grad_parts], axis=0)
    last = grad_parts[-1][-1]
    y_all = join(
        [
            run_expand([(after(y[at][0], last),) + y[at][1:] for y in y_parts])
            for at in range(n_groups // chunk)
        ]
    ).reshape(-1, width)

    gwi, gwd = weight_grads[:row_count], weight_grads[row_count:]
    gi_x, gi_d = swap(gwi[2], 1), swap(gwi[3], 1)
    gd_y, gd_d = swap(gwd[1], 2), swap(gwd[3], 2)
    gi_two = (gwi[1].astype(F32) + gi_d.astype(F32)).astype(BF16)
    gd_two = (gwd[2].astype(F32) + gd_d.astype(F32)).astype(BF16)
    grad_two = after(grad_two, gi_x, gi_two, gd_y, gd_two, y_all).astype(F32)

    cotangent = grad_out.astype(F32)
    grad_gain_moe = jnp.sum(grad_two * (hidden_one * inverse_two), axis=0)
    grad_hidden = cotangent + rms_back(hidden_one, inverse_two, gain_moe, grad_two)
    grad_attn = grad_hidden.astype(BF16)
    grad_mixed = dot_nt(grad_attn, w_out_all).astype(BF16)
    half_cols = heads * head_size
    gm_theirs = swap(grad_mixed[:, half_cols:], 1)
    out_rows = w_out.shape[0]
    small = jnp.concatenate([grt[:n_experts], grad_gain_moe[None]], axis=0)
    early_rows = round_up(out_rows + small.shape[0], 32)
    gwo = dot_tn(mixed_all, grad_attn)
    early_parts = [
        pad_rows(
            jnp.concatenate([gwo[k * out_rows : (k + 1) * out_rows], small], axis=0), early_rows
        ).astype(BF16)
        for k in range(row_count)
    ]
    gm_theirs = after(gm_theirs, *early_parts)
    gm_seq = in_order(grad_mixed[:, :half_cols], gm_theirs)
    mixture = scatter(after(y_all, gm_seq))
    grad_packed, diag = attention_backward(packed, probs, gm_seq, heads, head_size)

    early_sent = [swap(early_parts[k], m) for k, m in ((1, 2), (2, 1), (3, 3))]
    grad_packed, diag = lax.optimization_barrier(
        (grad_packed, diag, *early_sent)
    )[:2]
    early = early_parts[0].astype(F32) + sum(e.astype(F32) for e in early_sent)

    def keep_half(value):
        parts = value.reshape(2, -1, width)
        sent = swap_col(lax.dynamic_index_in_dim(parts, 1 - col, 0, keepdims=False).astype(BF16))
        kept = lax.dynamic_index_in_dim(parts, col, 0, keepdims=False)
        return kept.astype(F32) + sent.astype(F32)

    early_half = keep_half(early)

    one_theirs = swap(dot_nt(half(grad_packed, 1 - member), qkv_both).astype(BF16), 1)
    gq = dot_tn(grad_packed, normed_seq)
    gain_part = jnp.sum(gq * qkv_both.T.astype(F32), axis=0) / gain_attn
    table_grad = jnp.dot(
        bucket_hot, diag.reshape(heads, -1).T, precision=lax.Precision.HIGHEST
    )
    late_rows = round_up(qkv_cols + 2, 32)

    def late_block(which, gain):
        cols = table_grad[:, which * heads_here : (which + 1) * heads_here].reshape(1, -1)
        table_row = jnp.concatenate(
            [cols, jnp.zeros((1, width - cols.shape[1]), F32)], axis=1
        )
        block = gq[which * qkv_cols : (which + 1) * qkv_cols]
        return pad_rows(jnp.concatenate([block, gain[None], table_row], axis=0), late_rows)

    late_own = late_block(0, gain_part)
    late_other = late_block(1, gain_part)
    both_half = keep_half(
        jnp.stack([late_own.reshape(2, -1, width), late_other.reshape(2, -1, width)], axis=1)
    ).reshape(2, -1, width)
    late_half = both_half[0] + swap(both_half[1].astype(BF16), 2).astype(F32)
    late_n, early_n = late_half.shape[0], early_half.shape[0]

    gi_y = swap(after(gi_two, late_half), 2)
    gd_x = swap(after(gd_two, late_half), 1)
    mixture = after(mixture, both_half)
    block_out = (hidden_one + mixture.astype(F32)).astype(BF16)
    total_rows = round_up(late_n + early_n, 16 * 4)
    summed, arrived_z = reduce_z(
        pad_rows(jnp.concatenate([late_half, early_half], axis=0).astype(BF16), total_rows),
        gi_y,
        gd_x,
        block_out,
    )
    one_theirs = after(one_theirs, arrived_z)
    grad_one = dot_nt(half(grad_packed, member), qkv_both) + one_theirs.astype(F32)
    grad_input = (grad_hidden + rms_back(tokens_f, inverse_one, gain_attn, grad_one)).astype(BF16)
    grad_w_in = (gwi[0].astype(F32) + gi_x.astype(F32) + gi_y.astype(F32))[None]
    grad_w_down = (gwd[0].astype(F32) + gd_y.astype(F32) + gd_x.astype(F32))[None]
    summed = after(summed, grad_w_in, grad_w_down, grad_input)
    theirs = swap_col(summed)
    low = jnp.where(col == 0, summed, theirs)
    high = jnp.where(col == 0, theirs, summed)
    late = jnp.concatenate([low[:late_n], high[:late_n]], axis=0).astype(F32)
    early = jnp.concatenate(
        [low[late_n : late_n + early_n], high[late_n : late_n + early_n]], axis=0
    ).astype(F32)
    gain_row = late[qkv_cols]
    slice_n = width // row_count
    gain_slice = lax.dynamic_slice_in_dim(gain_row, row * slice_n, slice_n, 0) + swap(
        lax.dynamic_slice_in_dim(gain_row, (row ^ 1) * slice_n, slice_n, 0), 1
    )
    grad_table = late[qkv_cols + 1, : n_buckets * heads_here].reshape(n_buckets, heads_here)
    return (
        block_out,
        grad_input,
        gain_slice,
        late[:qkv_cols].T.reshape(w_qkv.shape),
        early[:out_rows],
        grad_table,
        early[out_rows + n_experts],
        early[out_rows : out_rows + n_experts].T,
        grad_w_in,
        grad_w_down,
    )


def solution(mesh):
    placed = (
        P(("dp", "col", "row"), None),
        P(),
        P(None, "row", None),
        P("row", None),
        P(None, "row"),
        P(),
        P(),
        P(("dp", "col"), None, "row"),
        P(("dp", "col"), "row", None),
        P(("dp", "col", "row"), None),
        P(("dp", "col"), None),
        P(("dp", "col")),
        P(),
    )
    return jax.shard_map(
        local,
        mesh=mesh,
        in_specs=placed,
        out_specs=(
            P(("dp", "col", "row"), None),
            P(("dp", "col", "row"), None),
            P("row"),
            P(None, "row", None),
            P("row", None),
            P(None, "row"),
            P(),
            P(),
            P(("dp", "col"), None, "row"),
            P(("dp", "col"), "row", None),
        ),
        check_vma=False,
    )
```
